32 devices in a mesh: dp: 16 (over z, x, core), tensor: 2 (over y).
Axes of the slice: x: 2, y: 2, z: 4, core: 2. Of those that a mesh axis runs over, the one named last changes fastest.
Arguments:
- tokens: bfloat16 [4096, 2048], P(('dp', 'tensor')), may hold values from -6 to 6
- segments: int32 [4096], P('dp'), may hold values from -1 to 0, as said below
- cotangent: bfloat16 [4096, 2048], P(('dp', 'tensor')), may hold values from -6 to 6
- first_gain: bfloat16 [2048], P('dp'), may hold values from 0.5 to 1.5
- mixer_in: bfloat16 [2048, 2, 3072], P('dp', None, 'tensor'), may hold values from -0.125 to 0.125
- state_weight: bfloat16 [2048, 512], P('dp'), may hold values from -0.125 to 0.125
- step_weight: bfloat16 [2048, 24], P('dp', 'tensor'), may hold values from -0.125 to 0.125
- filter_taps: bfloat16 [5, 24, 128], P(None, 'tensor', 'dp'), may hold values from -3 to 3
- state_taps: bfloat16 [5, 512], P(None, 'dp'), may hold values from -3 to 3
- decay_log: float32 [24], P('tensor'), may hold values from -2 to 1.5
- step_bias: float32 [24], P('tensor'), may hold values from -6 to -2
- skip_gain: float32 [24], P('tensor'), may hold values from 0.5 to 1.5
- gate_gain: bfloat16 [24, 128], P('tensor', 'dp'), may hold values from 0.5 to 1.5
- mixer_out: bfloat16 [3072, 2048], P('tensor', 'dp'), may hold values from -0.109375 to 0.109375
- query_weight: bfloat16 [2048, 1024], P('dp', 'tensor'), may hold values from -1 to 1
- key_value_matrix: bfloat16 [2048, 2, 256], P('dp', None, 'tensor'), may hold values from -1 to 1
- attend_out: bfloat16 [1024, 2048], P('tensor', 'dp'), may hold values from -1.5 to 1.5
- second_gain: bfloat16 [2048], P('dp'), may hold values from 0.5 to 1.5
- gate_up: bfloat16 [2048, 2, 4096], P('dp', None, 'tensor'), may hold values from -0.125 to 0.125
- down_weight: bfloat16 [4096, 2048], P('tensor', 'dp'), may hold values from -0.09375 to 0.09375
Outputs:
- output: bfloat16 [4096, 2048], P(('dp', 'tensor'))
- tokens_grad: float32 [4096, 2048], P(('dp', 'tensor'))
- first_gain_grad: float32 [2048], P('dp')
- mixer_in_grad: float32 [2048, 2, 3072], P('dp', None, 'tensor')
- state_weight_grad: float32 [2048, 512], P('dp')
- step_weight_grad: float32 [2048, 24], P('dp', 'tensor')
- filter_taps_grad: float32 [5, 24, 128], P(None, 'tensor', 'dp')
- state_taps_grad: float32 [5, 512], P(None, 'dp')
- decay_log_grad: float32 [24], P('tensor')
- step_bias_grad: float32 [24], P('tensor')
- skip_gain_grad: float32 [24], P('tensor')
- gate_gain_grad: float32 [24, 128], P('tensor', 'dp')
- mixer_out_grad: float32 [3072, 2048], P('tensor', 'dp')
- query_weight_grad: float32 [2048, 1024], P('dp', 'tensor')
- keys_values_grad: float32 [2048, 2, 256], P('dp', None, 'tensor')
- attend_out_grad: float32 [1024, 2048], P('tensor', 'dp')
- second_gain_grad: float32 [2048], P('dp')
- gate_up_grad: float32 [2048, 2, 4096], P('dp', None, 'tensor')
- down_weight_grad: float32 [4096, 2048], P('tensor', 'dp')
The draws below stay inside these ranges and needn't reach their ends.
Inputs may be any that keep to these rules, and one draw needn't show every extreme that they name: `segments`: in each group of 256 slots the live slots come first and hold one whole sequence numbered 0, then -1 in the empty slots; every group has at least 64 live slots, and in every draw some group is one sequence of 256 tokens.
All inputs are finite; a program needn't handle non-finite values.
Results may differ from the reference program's by a relative error of at most 0.015.
Values may be sent and summed in bfloat16 or wider, within the bound.
No kernel may reach another device: no remote copies, remote signals or barrier semaphores. Data moves between devices by JAX's collectives and lax.ppermute only.
A program may use at most 256 MiB of HBM per device.

```python
import jax
import jax.numpy as jnp
from jax import lax

MODEL_WIDTH = 2048
HM = 24
HEAD_DIMENSION = 128
NS = 256
CONV = 4
QUERY_HEADS = 8
KEY_VALUE_HEADS = 2
FF = 4096
TOK_GRP = 256
TOKENS = 4096
N_DP = 16


def draw_segments(key, part):
    key_rows = jax.random.split(key, 2)
    spread = jax.random.randint(key_rows[0], (N_DP,), 0, TOK_GRP + 1)
    filled = TOK_GRP // 4 + 3 * spread * spread // (4 * TOK_GRP)
    chosen = jax.random.randint(key_rows[1], (), 0, N_DP)
    groups = jnp.arange(N_DP)
    filled = jnp.where(groups == chosen, TOK_GRP, filled)
    order = jnp.arange(TOK_GRP)[None, :]
    number = jnp.zeros((N_DP, TOK_GRP), jnp.int32)
    return jnp.where(order < filled[:, None], number, -1).reshape(N_DP * TOK_GRP).astype(jnp.int32)


def draw_tokens(key, part):
    key_rows = jax.random.split(jax.random.fold_in(key, 5), 1)
    result = jax.random.truncated_normal(key_rows[0], -6.0, 6.0, (N_DP, TOK_GRP, MODEL_WIDTH), jnp.float32)
    return result.reshape(N_DP * TOK_GRP, MODEL_WIDTH).astype(jnp.bfloat16)


def attention_draw(key):
    key_rows = jax.random.split(jax.random.fold_in(key, 11), 2)
    query_rows = jax.random.truncated_normal(key_rows[0], -4.0, 4.0, (MODEL_WIDTH, QUERY_HEADS * HEAD_DIMENSION), jnp.float32) * MODEL_WIDTH ** (-0.5)
    paired_halves = jax.random.truncated_normal(key_rows[1], -4.0, 4.0, (MODEL_WIDTH, 2, KEY_VALUE_HEADS * HEAD_DIMENSION), jnp.float32) * MODEL_WIDTH ** (-0.5)
    return (query_rows.astype(jnp.bfloat16), paired_halves.astype(jnp.bfloat16))


def draw_query_weight(key, part):
    return attention_draw(key)[0]


def draw_key_value_matrix(key, part):
    return attention_draw(key)[1]


def spiked(array, rng, source, target, blocks, factor):
    owner, partner = [(jnp.arange(array.shape[dim]) // (array.shape[dim] // blocks)).reshape([-1 if axis == dim else 1 for axis in range(array.ndim)]) for dim in (source, target)]
    chosen = jax.random.permutation(rng, blocks)[partner]
    strong = (owner == chosen) | (owner == (partner + blocks // 2) % blocks)
    return jnp.where(strong, factor * array, array)


def steps_of(rng, shape, shards, least, top_value):
    loudness, own = 1.0, jax.random.fold_in(rng, 6)
    for axis_at, shards_of in shards:
        heights = jnp.exp(jax.random.uniform(jax.random.fold_in(own, axis_at), (shards_of,), jnp.float32, least / len(shards), top_value / len(shards)))
        loudness = loudness * jnp.repeat(heights, shape[axis_at] // shards_of).reshape([-1 if axis == axis_at else 1 for axis in range(len(shape))])
    return loudness


def bell_draw(stream_key, shape, deviation, most, cuts=(), kind=jnp.bfloat16):
    level = steps_of(stream_key, shape, cuts, -0.22, 0.18) if cuts else 1.0
    values = jax.random.normal(stream_key, shape, jnp.float32) * deviation * level
    return jnp.minimum(jnp.maximum(values, -most), most).astype(kind)


def gaussian_with(own_key, dims, width, limit, shards, heavy, held_as=jnp.bfloat16):
    entries = width * jax.random.normal(own_key, dims, jnp.float32)
    if shards:
        entries = entries * steps_of(own_key, dims, shards, -0.22, 0.18)
    return jnp.clip(spiked(entries, jax.random.fold_in(own_key, 3), *heavy), -limit, limit).astype(held_as)


def setup_inputs(seed: int = 0) -> dict:
    arg_keys = jax.random.split(jax.random.key(seed), 21)
    tokens = draw_tokens(jax.random.fold_in(arg_keys[20], 71), 0)
    segments = draw_segments(jax.random.fold_in(arg_keys[20], 71), 0)
    cotangent = gaussian_with(arg_keys[2], (TOKENS, MODEL_WIDTH), 1.0, 6.0, ((0, 32),), (0, 1, 32, 2.75))
    first_gain = jnp.clip(1.0 + 0.1 * jax.random.normal(arg_keys[3], (MODEL_WIDTH,), jnp.float32), 0.5, 1.5).astype(jnp.bfloat16)
    mixer_in = bell_draw(arg_keys[4], (MODEL_WIDTH, 2, HM * HEAD_DIMENSION), MODEL_WIDTH ** -0.5, 0.125, ((0, 16), (2, 2)))
    state_weight = bell_draw(arg_keys[5], (MODEL_WIDTH, 2 * NS), MODEL_WIDTH ** -0.5, 0.125, ((0, 16),))
    step_weight = bell_draw(arg_keys[6], (MODEL_WIDTH, HM), MODEL_WIDTH ** -0.5, 0.125, ((0, 16), (1, 2)))
    filter_taps = bell_draw(arg_keys[7], (CONV + 1, HM, HEAD_DIMENSION), CONV ** -0.5, 3.0, ((1, 2), (2, 16)))
    state_taps = bell_draw(arg_keys[8], (CONV + 1, 2 * NS), CONV ** -0.5, 3.0, ((1, 16),))
    decay_log = jnp.clip(-2.0 + 3.5 * jax.random.uniform(arg_keys[9], (HM,), jnp.float32) ** steps_of(arg_keys[9], (HM,), ((0, 2),), -0.2, 0.2), -2.0, 1.5)
    step_bias = jnp.clip(-6.0 + 4.0 * jax.random.uniform(arg_keys[10], (HM,), jnp.float32) ** steps_of(arg_keys[10], (HM,), ((0, 2),), -0.2, 0.2), -6.0, -2.0)
    skip_gain = jnp.clip(0.5 + 1.0 * jax.random.uniform(arg_keys[11], (HM,), jnp.float32) ** steps_of(arg_keys[11], (HM,), ((0, 2),), -0.2, 0.2), 0.5, 1.5)
    gate_gain = jnp.clip(1.0 + 0.1 * jax.random.normal(arg_keys[12], (HM, HEAD_DIMENSION), jnp.float32), 0.5, 1.5).astype(jnp.bfloat16)
    mixer_out = bell_draw(arg_keys[13], (HM * HEAD_DIMENSION, MODEL_WIDTH), (HM * HEAD_DIMENSION) ** -0.5, 0.109375, ((0, 2), (1, 16)))
    query_weight = draw_query_weight(jax.random.fold_in(arg_keys[20], 71), 0)
    key_value_matrix = draw_key_value_matrix(jax.random.fold_in(arg_keys[20], 71), 0)
    attend_out = bell_draw(arg_keys[16], (QUERY_HEADS * HEAD_DIMENSION, MODEL_WIDTH), (QUERY_HEADS * HEAD_DIMENSION * 4 // TOK_GRP) ** -0.5, 1.5, ((0, 2), (1, 16)))
    second_gain = jnp.clip(1.0 + 0.1 * jax.random.normal(arg_keys[17], (MODEL_WIDTH,), jnp.float32), 0.5, 1.5).astype(jnp.bfloat16)
    gate_up = bell_draw(arg_keys[18], (MODEL_WIDTH, 2, FF), MODEL_WIDTH ** -0.5, 0.125, ((0, 16), (2, 2)))
    down_weight = bell_draw(arg_keys[19], (FF, MODEL_WIDTH), FF ** -0.5, 0.09375, ((0, 2), (1, 16)))
    return {"tokens": tokens, "segments": segments, "cotangent": cotangent, "first_gain": first_gain, "mixer_in": mixer_in, "state_weight": state_weight, "step_weight": step_weight, "filter_taps": filter_taps, "state_taps": state_taps, "decay_log": decay_log, "step_bias": step_bias, "skip_gain": skip_gain, "gate_gain": gate_gain, "mixer_out": mixer_out, "query_weight": query_weight, "key_value_matrix": key_value_matrix, "attend_out": attend_out, "second_gain": second_gain, "gate_up": gate_up, "down_weight": down_weight}


EPS = 1e-05
ROPE_BASE = 100000000000.0
HIGH = lax.Precision.HIGHEST

@jax.custom_vjp
def reduced_precision(v):
    return lax.optimization_barrier(v.astype(jnp.bfloat16)).astype(jnp.float32)

@jax.custom_vjp
def reduced_backward(v):
    return v

def low_keep(v):
    return (reduced_precision(v), None)

def low_pass(kept, grad):
    return (grad,)

def back_keep(v):
    return (v, None)

def back_low(kept, grad):
    return (reduced_precision(grad),)
reduced_precision.defvjp(low_keep, low_pass)
reduced_backward.defvjp(back_keep, back_low)

def product_result(left, right):
    return jnp.dot(left, right, precision=HIGH)

def norm_rows(values, gain):
    return values * lax.rsqrt(lax.optimization_barrier(jnp.mean(values * values, axis=-1, keepdims=True)) + EPS) * gain

def shift_down(values, offset):
    return jnp.concatenate([jnp.zeros((offset,) + values.shape[1:], values.dtype), values[:-offset]], axis=0)

def tap_masks(segments, count):
    masks = [jnp.ones(segments.shape, jnp.float32)]
    for offset in range(1, count):
        earlier = jnp.concatenate([jnp.full((offset,), -2, jnp.int32), segments[:-offset]])
        masks.append((earlier == segments).astype(jnp.float32))
    return jnp.stack(masks)

def causal_filter(values, weights, masks):
    total = weights[-1] + weights[0] * values
    for offset in range(1, weights.shape[0] - 1):
        total = total + weights[offset] * shift_down(values, offset) * masks[offset][:, None]
    return total

def rotary_tables(position, head_size):
    half = head_size // 2
    frequency = ROPE_BASE ** (-2.0 * jnp.arange(half).astype(jnp.float32) / head_size)
    angle = position[:, None] * frequency[None, :]
    return (jnp.cos(angle)[:, None, :], jnp.sin(angle)[:, None, :])

def rotate_halves(values, cosine_table, sine_table):
    half = values.shape[-1] // 2
    first = values[..., :half]
    second = values[..., half:]
    return jnp.concatenate([first * cosine_table - second * sine_table, second * cosine_table + first * sine_table], axis=-1)

def group_forward(tokens, segments, weight_set):
    first_gain, mixer_in, state_weight, step_weight, filter_taps, state_taps, decay_log, step_bias, skip_gain, gate_gain, mixer_out, query_weight, key_value_matrix, attend_out, second_gain, gate_up, down_weight = weight_set
    count_of_rows = tokens.shape[0]
    channels = HM * HEAD_DIMENSION
    order = jnp.arange(count_of_rows)
    live = (segments >= 0).astype(jnp.float32)[:, None]
    causal = (segments[:, None] == segments[None, :]) & (order[None, :] <= order[:, None])
    position = lax.optimization_barrier(jnp.sum(causal.astype(jnp.float32), axis=1)) - 1.0
    masks = tap_masks(segments, CONV)
    normed_input = reduced_precision(norm_rows(tokens, first_gain))
    mix_proj = reduced_backward(product_result(normed_input, mixer_in.reshape(MODEL_WIDTH, 2 * channels)))
    gate_value = mix_proj[:, :channels]
    filter_input = mix_proj[:, channels:]
    state_raw = reduced_backward(product_result(normed_input, state_weight))
    step_raw = reduced_backward(product_result(normed_input, step_weight))
    filtered = jax.nn.silu(causal_filter(filter_input, filter_taps.reshape(CONV + 1, channels), masks))
    state_act = jax.nn.silu(causal_filter(state_raw, state_taps, masks))
    state_write = reduced_precision(state_act[:, :NS])
    state_read = reduced_precision(state_act[:, NS:])
    step = jax.nn.softplus(step_raw + step_bias)
    rate = -jnp.exp(decay_log) * step
    level = jnp.cumsum(rate, axis=0)
    affinity = product_result(state_read, state_write.T)
    spread = level.T[:, :, None] - level.T[:, None, :]
    decay = jnp.where(causal[None], jnp.exp(jnp.where(causal[None], spread, 0.0)), 0.0)
    mixing = reduced_precision(affinity[None] * decay)
    filtered_heads = filtered.reshape(count_of_rows, HM, HEAD_DIMENSION)
    inner = reduced_precision(filtered_heads * step[:, :, None])
    scanned = reduced_backward(jnp.einsum('hts,shd->thd', mixing, inner, precision=HIGH))
    state_mix = (scanned + skip_gain[None, :, None] * filtered_heads).reshape(count_of_rows, channels)
    gated = state_mix * jax.nn.silu(gate_value)
    state_norm = reduced_precision(norm_rows(gated, gate_gain.reshape(channels)))
    head_group = QUERY_HEADS // KEY_VALUE_HEADS
    cosine_table, sine_table = rotary_tables(position, HEAD_DIMENSION)
    query_unrotated = reduced_backward(product_result(normed_input, query_weight)).reshape(count_of_rows, QUERY_HEADS, HEAD_DIMENSION)
    key_unrotated = reduced_backward(product_result(normed_input, key_value_matrix.reshape(MODEL_WIDTH, 2 * KEY_VALUE_HEADS * HEAD_DIMENSION))).reshape(count_of_rows, 2, KEY_VALUE_HEADS, HEAD_DIMENSION)
    query_rows = reduced_precision(rotate_halves(query_unrotated, cosine_table, sine_table)).reshape(count_of_rows, KEY_VALUE_HEADS, head_group, HEAD_DIMENSION)
    key_rows = reduced_precision(rotate_halves(key_unrotated[:, 0], cosine_table, sine_table))
    values = reduced_precision(key_unrotated[:, 1])
    scores = reduced_backward(jnp.einsum('tkgd,skd->kgts', query_rows, key_rows, precision=HIGH) * HEAD_DIMENSION ** (-0.5))
    scores = jnp.where(causal, scores, -1e+30)
    top = lax.optimization_barrier(jnp.max(scores, axis=-1, keepdims=True))
    raised = jnp.exp(scores - top)
    shares = reduced_precision(raised / lax.optimization_barrier(jnp.sum(raised, axis=-1, keepdims=True)))
    attended = reduced_precision(reduced_backward(jnp.einsum('kgts,skd->tkgd', shares, values, precision=HIGH)))
    attended = attended.reshape(count_of_rows, QUERY_HEADS * HEAD_DIMENSION)
    branch = product_result(state_norm, mixer_out) + product_result(attended, attend_out)
    hidden = tokens + reduced_backward(live * branch)
    second = reduced_precision(norm_rows(hidden, second_gain))
    gate_proj = reduced_backward(product_result(second, gate_up.reshape(MODEL_WIDTH, 2 * FF))).reshape(count_of_rows, 2, FF)
    activation = reduced_precision(jax.nn.silu(gate_proj[:, 0]) * gate_proj[:, 1])
    return hidden + reduced_backward(live * product_result(activation, down_weight))

def reference(tokens, segments, cotangent, first_gain, mixer_in, state_weight, step_weight, filter_taps, state_taps, decay_log, step_bias, skip_gain, gate_gain, mixer_out, query_weight, key_value_matrix, attend_out, second_gain, gate_up, down_weight):
    weight_set = tuple((initial.astype(jnp.float32) for initial in (first_gain, mixer_in, state_weight, step_weight, filter_taps, state_taps, decay_log, step_bias, skip_gain, gate_gain, mixer_out, query_weight, key_value_matrix, attend_out, second_gain, gate_up, down_weight)))
    inputs = tokens.astype(jnp.float32).reshape(N_DP, TOK_GRP, MODEL_WIDTH)
    grouped = segments.reshape(N_DP, TOK_GRP)

    def forward(values, weights_now):

        def one_group(group_pair):
            return group_forward(group_pair[0], group_pair[1], weights_now)
        return lax.map(jax.checkpoint(one_group), (values, grouped))
    result, pullback = jax.vjp(forward, inputs, weight_set)
    inputs_grad, gradients = pullback(cotangent.astype(jnp.float32).reshape(N_DP, TOK_GRP, MODEL_WIDTH))
    return (result.reshape(N_DP * TOK_GRP, MODEL_WIDTH).astype(jnp.bfloat16), inputs_grad.reshape(N_DP * TOK_GRP, MODEL_WIDTH), gradients[0], gradients[1], gradients[2], gradients[3], gradients[4], gradients[5], gradients[6], gradients[7], gradients[8], gradients[9], gradients[10], gradients[11], gradients[12], gradients[13], gradients[14], gradients[15], gradients[16])
```

```python
import jax
import jax.numpy as jnp
from jax import lax
from jax.sharding import Mesh, PartitionSpec as P

HEAD = 128
NS = 256
CONV = 4
EPS = 1e-05
ROPE_BASE = 100000000000.0
BF = jnp.bfloat16
F32 = jnp.float32


def dot(left, right):
    return jnp.dot(left, right, preferred_element_type=F32)


def contract(form, left, right):
    return jnp.einsum(form, left, right, preferred_element_type=F32)


def silu_slope(values):
    sigma = jax.nn.sigmoid(values)
    return sigma * (1.0 + values * (1.0 - sigma))


def norm_rows(values, gain):
    scale = lax.rsqrt(jnp.mean(values * values, axis=-1, keepdims=True) + EPS)
    return values * scale * gain, scale


def norm_rows_back(values, gain, scale, grad):
    normal = values * scale
    weighted = grad * gain
    back = scale * (weighted - normal * jnp.mean(weighted * normal, axis=-1, keepdims=True))
    return back, jnp.sum(grad * normal, axis=0)


def swap_c(v):
    return lax.ppermute(v, "c", [(0, 1), (1, 0)])


def swap_x(v):
    return lax.ppermute(v, "x", [(0, 1), (1, 0)])


def swap_t(v):
    return lax.ppermute(v, "t", [(0, 1), (1, 0)])


def swap_xt(v):
    return lax.ppermute(v, ("x", "t"), [(0, 3), (1, 2), (2, 1), (3, 0)])


def swap_xc(v):
    return lax.ppermute(v, ("x", "c"), [(0, 3), (1, 2), (2, 1), (3, 0)])


def pick(rel, j, xi, ci):
    low = jnp.where(ci == 0, rel[j], rel[j ^ 1])
    high = jnp.where(ci == 0, rel[j ^ 2], rel[j ^ 3])
    return jnp.where(xi == 0, low, high)


def deal(blocks, axis, xi, ci):
    rel = [
        pick(blocks, 0, xi, ci),
        swap_c(pick(blocks, 1, xi, ci)),
        swap_x(pick(blocks, 2, xi, ci)),
        swap_xc(pick(blocks, 3, xi, ci)),
    ]
    return [pick(rel, j, xi, ci) for j in range(4)]


def order_t(mine, other, ti, axis=0):
    return jnp.where(
        ti == 0,
        jnp.concatenate([mine, other], axis=axis),
        jnp.concatenate([other, mine], axis=axis),
    )


def act_gather(v, ti):
    near = order_t(v, swap_t(v), ti)
    far = order_t(swap_x(v), swap_xt(v), ti)
    pair = jnp.stack([near, far])
    return jnp.concatenate([pair, swap_c(pair)])


def act_scatter(keep, send, ti):
    total = keep + swap_c(send.astype(BF)).astype(F32)
    rows = total.shape[1] // 2
    mine = lax.dynamic_slice_in_dim(total, ti * rows, rows, 1)
    other = lax.dynamic_slice_in_dim(total, (1 - ti) * rows, rows, 1)
    low = other.astype(BF)
    far = mine[1].astype(BF)
    got = (swap_t(low[0]), swap_x(far), swap_xt(low[1]))
    return mine[0] + got[0].astype(F32) + got[1].astype(F32) + got[2].astype(F32)


def z_gather(v, zi, depth):
    if depth != 4:
        whole = lax.all_gather(v, "z", axis=0, tiled=False)
        whole = jnp.roll(whole, -zi, axis=0)
        return [whole[k] for k in range(depth)]
    below = lax.ppermute(v, "z", [(0, 1), (1, 2), (2, 3)])
    above = lax.ppermute(v, "z", [(1, 0), (2, 1), (3, 2)])
    two = lax.ppermute(v, "z", [(0, 2), (1, 3), (2, 0), (3, 1)])
    last = lax.ppermute(two, "z", [(2, 3), (1, 0)])
    return [v, jnp.where(zi == 3, last, above), two, jnp.where(zi == 0, last, below)]


def z_scatter(parts, zi, depth):
    if depth != 4:
        whole = jnp.roll(jnp.stack([p.astype(BF) for p in parts]), zi, axis=0)
        return lax.psum_scatter(whole, "z", scatter_dimension=0, tiled=False).astype(F32)
    one, three = parts[1].astype(BF), parts[3].astype(BF)
    corner = lax.ppermute(jnp.where(zi == 3, one, three), "z", [(3, 2), (0, 1)])
    down = lax.ppermute(three, "z", [(1, 0), (2, 1), (3, 2)])
    up = lax.ppermute(one, "z", [(0, 1), (1, 2), (2, 3)])
    mid = (parts[2].astype(F32) + corner.astype(F32)).astype(BF)
    far = lax.ppermute(mid, "z", [(0, 2), (1, 3), (2, 0), (3, 1)])
    return parts[0].astype(F32) + down.astype(F32) + up.astype(F32) + far.astype(F32)


def sum_all(v, depth):
    v = v + swap_c(v)
    v = v + swap_x(v)
    v = v + swap_t(v)
    if depth != 4:
        return lax.psum(v, "z")
    v = v + lax.ppermute(v, "z", [(0, 1), (1, 0), (2, 3), (3, 2)])
    return v + lax.ppermute(v, "z", [(0, 2), (2, 0), (1, 3), (3, 1)])


def sum_group(v):
    v = v + jnp.roll(swap_c(v), 2, axis=0)
    got = swap_x(v)
    v = v + jnp.stack([got[1], got[0], got[3], got[2]])
    return v + swap_t(v)


def shift_down(values, offset):
    zero = jnp.zeros((values.shape[0], offset, values.shape[2]), values.dtype)
    return jnp.concatenate([zero, values[:, :-offset]], axis=1)


def shift_up(values, offset):
    zero = jnp.zeros((values.shape[0], offset, values.shape[2]), values.dtype)
    return jnp.concatenate([values[:, offset:], zero], axis=1)


def causal_filter(values, weights, masks):
    total = weights[CONV] + weights[0] * values
    for offset in range(1, CONV):
        total = total + weights[offset] * shift_down(values, offset) * masks[offset]
    return total


def filter_back(values, weights, masks, grad):
    taps = [jnp.sum(grad * values, axis=(0, 1))]
    back = weights[0] * grad
    for offset in range(1, CONV):
        masked = grad * masks[offset]
        taps.append(jnp.sum(masked * shift_down(values, offset), axis=(0, 1)))
        back = back + weights[offset] * shift_up(masked, offset)
    taps.append(jnp.sum(grad, axis=(0, 1)))
    return back, jnp.stack(taps)


def rotate_halves(values, cosine, sine):
    half = values.shape[-1] // 2
    first, second = values[..., :half], values[..., half:]
    return jnp.concatenate(
        [first * cosine - second * sine, second * cosine + first * sine], axis=-1
    )


def rotate_columns(v, start):
    width = v.shape[1]
    return lax.dynamic_slice_in_dim(jnp.concatenate([v, v], axis=1), start, width, 1)


def on_device(
    depth,
    tokens,
    segments,
    cotangent,
    first_gain,
    mixer_in,
    state_weight,
    step_weight,
    filter_taps,
    state_taps,
    decay_log,
    step_bias,
    skip_gain,
    gate_gain,
    mixer_out,
    query_weight,
    key_value_matrix,
    attend_out,
    second_gain,
    gate_up,
    down_weight,
):
    zi, xi = lax.axis_index("z"), lax.axis_index("x")
    ci, ti = lax.axis_index("c"), lax.axis_index("t")
    me = xi * 2 + ci
    rows, width = tokens.shape
    group = segments.shape[0]
    shard = mixer_in.shape[0]
    block = 4 * shard
    heads_in = decay_log.shape[0]
    heads = heads_in // 4
    chans = heads * HEAD
    total_chans = 2 * heads_in * HEAD
    ffn = gate_up.shape[2] // 4
    count = 4 * group
    scale = HEAD ** (-0.5)

    pieces = [first_gain, second_gain, filter_taps, state_taps, gate_gain, segments]
    sizes = [p.size for p in pieces]
    vec = jnp.concatenate([p.astype(BF).reshape(-1) for p in pieces])
    pad = -vec.size % 1024
    vec = jnp.pad(vec, (0, pad)).reshape(-1, 128)
    near = jnp.stack([vec, swap_x(vec)])
    quad = jnp.concatenate([near, swap_c(near)])
    by_offset = [quad[0], quad[2], quad[1], quad[3]]
    natural = jnp.stack([pick(by_offset, j, xi, ci) for j in range(4)])
    small = jnp.stack(z_gather(natural, zi, depth)).reshape(depth, 4, -1)
    segs = quad.reshape(4, -1)[:, sum(sizes[:5]) : sum(sizes)].astype(F32)
    offsets = [sum(sizes[:i]) for i in range(6)]
    cut = [small[:, :, offsets[i] : offsets[i] + sizes[i]] for i in range(5)]
    first_full = cut[0].reshape(-1).astype(F32)
    second_full = cut[1].reshape(-1).astype(F32)
    by_z = [jnp.roll(c, zi, axis=0) for c in cut[2:]]
    eighth = filter_taps.shape[2]
    taps_all = jnp.transpose(
        by_z[0].reshape(depth, 4, CONV + 1, heads_in, eighth), (2, 3, 0, 1, 4)
    ).reshape(CONV + 1, 4, chans)
    taps = lax.dynamic_index_in_dim(taps_all, me, 1, keepdims=False).astype(F32)
    staps = (
        jnp.transpose(by_z[1].reshape(depth, 4, CONV + 1, -1), (2, 0, 1, 3))
        .reshape(CONV + 1, 2 * NS)
        .astype(F32)
    )
    gate_all = jnp.transpose(
        by_z[2].reshape(depth, 4, heads_in, eighth), (2, 0, 1, 3)
    ).reshape(4, chans)
    gate_gain_mine = lax.dynamic_index_in_dim(gate_all, me, 0, keepdims=False).astype(F32)

    def quarters(v, axis):
        n = v.shape[axis] // 4
        return [lax.slice_in_dim(v, j * n, (j + 1) * n, axis=axis) for j in range(4)]

    state_half = lax.dynamic_slice_in_dim(state_weight, ti * NS, NS, 1)
    step_pad = jnp.pad(step_weight, ((0, 0), (0, 128 - heads_in)))
    row_pack = jnp.concatenate(
        [state_half, key_value_matrix.reshape(shard, -1), step_pad], axis=1
    )
    row_z = jnp.stack(z_gather(row_pack, zi, depth))
    state_other = swap_t(row_z[:, :, :NS])
    state_both = order_t(row_z[:, :, :NS], state_other, ti, axis=2)
    row_mine = jnp.concatenate([state_both, row_z[:, :, NS:]], axis=2)
    row_near = jnp.stack([row_mine, swap_x(row_mine)])
    row_quad = jnp.concatenate([row_near, swap_c(row_near)])
    row_by = [row_quad[0], row_quad[2], row_quad[1], row_quad[3]]
    row_full = jnp.stack([pick(row_by, j, xi, ci) for j in range(4)], axis=1).reshape(
        width, -1
    )
    state_full = row_full[:, : 2 * NS]
    kv_at, step_at = 2 * NS, 2 * NS + 2 * HEAD
    step_full = lax.dynamic_slice_in_dim(row_full[:, step_at:], me * heads, heads, 1)

    mix_q = [
        jnp.concatenate([a, b, q], axis=1)
        for a, b, q in zip(
            quarters(mixer_in[:, 0], 1), quarters(mixer_in[:, 1], 1), quarters(query_weight, 1)
        )
    ]
    mix_w = jnp.concatenate(
        z_gather(jnp.concatenate(deal(mix_q, 0, xi, ci), axis=0), zi, depth), axis=0
    )
    out_q = [
        jnp.concatenate([a, b], axis=0)
        for a, b in zip(quarters(mixer_out, 0), quarters(attend_out, 0))
    ]
    out_w = jnp.concatenate(
        z_gather(jnp.concatenate(deal(out_q, 1, xi, ci), axis=1), zi, depth), axis=1
    )
    gu_q = [
        jnp.concatenate([a, b], axis=1)
        for a, b in zip(quarters(gate_up[:, 0], 1), quarters(gate_up[:, 1], 1))
    ]
    gu_w = jnp.concatenate(
        z_gather(jnp.concatenate(deal(gu_q, 0, xi, ci), axis=0), zi, depth), axis=0
    )
    down_w = jnp.concatenate(
        z_gather(jnp.concatenate(deal(quarters(down_weight, 0), 1, xi, ci), axis=1), zi, depth),
        axis=1,
    )

    order = jnp.arange(group)
    live_all = (segs >= 0).astype(F32)
    causal = (segs[:, :, None] == segs[:, None, :]) & (order[None, None, :] <= order[None, :, None])
    position = jnp.sum(causal.astype(F32), axis=2) - 1.0
    masks = [None]
    for offset in range(1, CONV):
        earlier = jnp.concatenate(
            [jnp.full((4, offset), -2.0, F32), segs[:, :-offset]], axis=1
        )
        masks.append((earlier == segs).astype(F32)[:, :, None])
    half = HEAD // 2
    frequency = ROPE_BASE ** (-2.0 * jnp.arange(half).astype(F32) / HEAD)
    angle = position[:, :, None] * frequency[None, None, :]
    cosine, sine = jnp.cos(angle), jnp.sin(angle)
    live_mine = lax.dynamic_slice_in_dim(
        (segments >= 0).astype(F32), ti * rows, rows
    )[:, None]

    start = zi * block
    resid = rotate_columns(tokens, start).astype(F32)
    normed_input, scale_one = norm_rows(resid, first_full)
    normed_low = normed_input.astype(BF)
    normed = act_gather(normed_low, ti).reshape(count, width)
    row_out = dot(normed, row_full[:, :step_at])
    state_raw = row_out[:, : 2 * NS].reshape(4, group, 2 * NS)
    kv_raw = row_out[:, kv_at:].reshape(4, group, 2 * HEAD)
    step_raw = dot(normed, step_full).reshape(4, group, heads)
    mix_out = dot(normed, mix_w)
    gate_value = mix_out[:, :chans].reshape(4, group, chans)
    filter_input = mix_out[:, chans : 2 * chans].reshape(4, group, chans)
    query_raw = mix_out[:, 2 * chans :].reshape(4, group, HEAD)

    filter_pre = causal_filter(filter_input, taps, masks)
    filtered = jax.nn.silu(filter_pre)
    state_pre = causal_filter(state_raw, staps, masks)
    state_act = jax.nn.silu(state_pre)
    state_write = state_act[:, :, :NS].astype(BF)
    state_read = state_act[:, :, NS:].astype(BF)
    my_log = lax.dynamic_slice_in_dim(decay_log, me * heads, heads)
    my_bias = lax.dynamic_slice_in_dim(step_bias, me * heads, heads)
    my_skip = lax.dynamic_slice_in_dim(skip_gain, me * heads, heads)
    step = jax.nn.softplus(step_raw + my_bias)
    decay_rate = -jnp.exp(my_log)
    rate = decay_rate * step
    level = jnp.cumsum(rate, axis=1)
    level_t = jnp.transpose(level, (0, 2, 1))
    affinity = contract("gtn,gsn->gts", state_read, state_write)
    spread = level_t[:, :, :, None] - level_t[:, :, None, :]
    causal_h = causal[:, None]
    decay = jnp.where(causal_h, jnp.exp(jnp.where(causal_h, spread, 0.0)), 0.0)
    mixing_full = affinity[:, None] * decay
    mixing = mixing_full.astype(BF)
    step_wide = jnp.repeat(step, HEAD, axis=2)
    skip_wide = jnp.repeat(my_skip, HEAD)
    inner = (filtered * step_wide).astype(BF)

    def head(v, h):
        return v[:, :, h * HEAD : (h + 1) * HEAD]

    scanned = jnp.concatenate(
        [contract("gts,gsd->gtd", mixing[:, h], head(inner, h)) for h in range(heads)], axis=2
    )
    state_mix = scanned + skip_wide * filtered
    gate_act = jax.nn.silu(gate_value)
    gated = state_mix * gate_act
    squares = sum_group(jnp.sum(gated * gated, axis=-1))
    gate_scale = lax.rsqrt(squares / total_chans + EPS)[:, :, None]
    gate_normal = gated * gate_scale
    state_norm = (gate_normal * gate_gain_mine).astype(BF)

    query = rotate_halves(query_raw, cosine, sine).astype(BF)
    keys = rotate_halves(kv_raw[:, :, :HEAD], cosine, sine).astype(BF)
    values = kv_raw[:, :, HEAD:].astype(BF)
    scores = jnp.where(causal, contract("gtd,gsd->gts", query, keys) * scale, -1e30)
    top = jnp.max(scores, axis=-1, keepdims=True)
    raised = jnp.exp(scores - top)
    shares = raised / jnp.sum(raised, axis=-1, keepdims=True)
    shares_low = shares.astype(BF)
    attended = contract("gts,gsd->gtd", shares_low, values).astype(BF)

    branch = jnp.concatenate([state_norm, attended], axis=2)
    mixed = act_scatter(
        contract("gtk,kc->gtc", branch[:2], out_w) * live_all[:2, :, None],
        contract("gtk,kc->gtc", branch[2:], out_w) * live_all[2:, :, None],
        ti,
    )
    hidden = resid + mixed
    second, scale_two = norm_rows(hidden, second_full)
    second_all = act_gather(second.astype(BF), ti).reshape(count, width)
    gate_up_out = dot(second_all, gu_w)
    gate_part, up_part = gate_up_out[:, :ffn], gate_up_out[:, ffn:]
    activation = (jax.nn.silu(gate_part) * up_part).astype(BF)
    act_g = activation.reshape(4, group, ffn)
    feed_out = act_scatter(
        contract("gtk,kc->gtc", act_g[:2], down_w) * live_all[:2, :, None],
        contract("gtk,kc->gtc", act_g[2:], down_w) * live_all[2:, :, None],
        ti,
    )
    output = rotate_columns((hidden + feed_out).astype(BF), width - start)

    grad_out = rotate_columns(cotangent, start).astype(F32)
    feed_grad = act_gather((live_mine * grad_out).astype(BF), ti).reshape(count, width)
    act_grad = contract("td,fd->tf", feed_grad, down_w)
    gate_grad = act_grad * up_part * silu_slope(gate_part)
    up_grad = act_grad * jax.nn.silu(gate_part)
    gu_low = jnp.concatenate([gate_grad, up_grad], axis=1).astype(BF)
    gu_low_g = gu_low.reshape(4, group, 2 * ffn)
    second_grad = act_scatter(
        contract("gtk,ck->gtc", gu_low_g[:2], gu_w),
        contract("gtk,ck->gtc", gu_low_g[2:], gu_w),
        ti,
    )

    def column(v, k):
        return v[:, k * block : (k + 1) * block]

    down_sum = z_scatter(
        [contract("tf,td->fd", activation, column(feed_grad, k)) for k in range(depth)], zi, depth
    )
    gu_sum = z_scatter(
        [contract("tc,tk->ck", column(second_all, k), gu_low) for k in range(depth)], zi, depth
    )
    down_back = deal(quarters(down_sum.astype(BF), 1), 0, xi, ci)
    down_weight_grad = jnp.concatenate(down_back, axis=0).astype(F32)
    gu_back = deal(quarters(gu_sum.astype(BF), 0), 0, xi, ci)
    gate_up_grad = jnp.stack(
        [
            jnp.concatenate([b[:, :ffn] for b in gu_back], axis=1),
            jnp.concatenate([b[:, ffn:] for b in gu_back], axis=1),
        ],
        axis=1,
    ).astype(F32)

    hidden_part, second_gain_grad = norm_rows_back(hidden, second_full, scale_two, second_grad)
    hidden_grad = grad_out + hidden_part
    mix_grad = act_gather((live_mine * hidden_grad).astype(BF), ti).reshape(count, width)
    branch_flat = branch.reshape(count, chans + HEAD)
    branch_grad = contract("td,cd->tc", mix_grad, out_w)
    out_sum = z_scatter(
        [contract("tc,td->cd", branch_flat, column(mix_grad, k)) for k in range(depth)], zi, depth
    )
    out_back = deal(quarters(out_sum.astype(BF), 1), 0, xi, ci)
    mixer_out_grad = jnp.concatenate([b[:chans] for b in out_back], axis=0).astype(F32)
    attend_out_grad = jnp.concatenate([b[chans:] for b in out_back], axis=0).astype(F32)

    norm_grad = branch_grad[:, :chans].reshape(4, group, chans)
    attend_grad = branch_grad[:, chans:].astype(BF).reshape(4, group, HEAD)
    weighted = norm_grad * gate_gain_mine
    inner_sum = sum_group(jnp.sum(weighted * gate_normal, axis=-1))
    gated_grad = gate_scale * (weighted - gate_normal * (inner_sum / total_chans)[:, :, None])
    gate_gain_grad = jnp.sum(norm_grad * gate_normal, axis=(0, 1))
    mix_state_grad = gated_grad * gate_act
    gate_value_grad = gated_grad * state_mix * silu_slope(gate_value)
    skip_gain_grad = jnp.sum(
        (mix_state_grad * filtered).reshape(count, heads, HEAD), axis=(0, 2)
    )
    scanned_low = mix_state_grad.astype(BF)

    mixing_grad = jnp.stack(
        [contract("gtd,gsd->gts", head(scanned_low, h), head(inner, h)) for h in range(heads)],
        axis=1,
    )
    inner_grad = jnp.concatenate(
        [contract("gts,gtd->gsd", mixing[:, h], head(scanned_low, h)) for h in range(heads)],
        axis=2,
    )
    flow = mixing_grad * mixing_full
    level_grad = jnp.sum(flow, axis=3) - jnp.sum(flow, axis=2)
    rate_grad = jnp.transpose(
        lax.cumsum(level_grad, axis=2, reverse=True), (0, 2, 1)
    )
    decay_log_grad = jnp.sum(rate_grad * rate, axis=(0, 1))
    step_grad = rate_grad * decay_rate + jnp.sum(
        (inner_grad * filtered).reshape(4, group, heads, HEAD), axis=3
    )
    filtered_grad = skip_wide * mix_state_grad + inner_grad * step_wide
    affinity_grad = jnp.sum(mixing_grad * decay, axis=1).astype(BF)
    read_grad = contract("gts,gsn->gtn", affinity_grad, state_write)
    write_grad = contract("gts,gtn->gsn", affinity_grad, state_read)
    state_act_grad = jnp.concatenate([write_grad, read_grad], axis=2) * silu_slope(state_pre)
    state_raw_grad, state_taps_grad = filter_back(state_raw, staps, masks, state_act_grad)
    step_pre_grad = step_grad * jax.nn.sigmoid(step_raw + my_bias)
    step_bias_grad = jnp.sum(step_pre_grad, axis=(0, 1))
    step_low = step_pre_grad.astype(BF).reshape(count, heads)
    filter_input_grad, filter_taps_grad = filter_back(
        filter_input, taps, masks, filtered_grad * silu_slope(filter_pre)
    )

    values_grad = contract("gts,gtd->gsd", shares_low, attend_grad)
    shares_grad = contract("gtd,gsd->gts", attend_grad, values)
    scores_low = (
        shares * (shares_grad - jnp.sum(shares_grad * shares, axis=-1, keepdims=True))
    ).astype(BF)
    query_grad = contract("gts,gsd->gtd", scores_low, keys) * scale
    keys_grad = contract("gts,gtd->gsd", scores_low, query) * scale
    query_low = rotate_halves(query_grad, cosine, -sine)
    keys_low = jnp.concatenate([rotate_halves(keys_grad, cosine, -sine), values_grad], axis=2)
    mix_low = (
        jnp.concatenate([gate_value_grad, filter_input_grad, query_low], axis=2)
        .astype(BF)
        .reshape(count, 2 * chans + HEAD)
    )
    step_wide_low = lax.dynamic_update_slice_in_dim(
        jnp.zeros((count, 128), BF), step_low, me * heads, 1
    )
    kv_low = jnp.concatenate(
        [keys_low.astype(BF).reshape(count, 2 * HEAD), step_wide_low], axis=1
    )
    back_w = jnp.concatenate([mix_w, row_full[:, kv_at:]], axis=1)
    back_low = jnp.concatenate([mix_low, kv_low], axis=1).reshape(4, group, -1)
    summed = act_scatter(
        jnp.concatenate(
            [contract("gtk,ck->gtc", back_low[:2], back_w), state_raw_grad[:2]], axis=2
        ),
        jnp.concatenate(
            [contract("gtk,ck->gtc", back_low[2:], back_w), state_raw_grad[2:]], axis=2
        ),
        ti,
    )
    state_low = summed[:, width:].astype(BF)
    normed_grad = summed[:, :width] + contract("tn,cn->tc", state_low, state_full)
    resid_part, first_gain_grad = norm_rows_back(resid, first_full, scale_one, normed_grad)
    tokens_grad = rotate_columns(hidden_grad + resid_part, width - start)

    mix_sum = z_scatter(
        [contract("tc,tk->ck", column(normed, k), mix_low) for k in range(depth)], zi, depth
    )
    mix_back = deal(quarters(mix_sum.astype(BF), 0), 0, xi, ci)
    mixer_in_grad = jnp.stack(
        [
            jnp.concatenate([b[:, :chans] for b in mix_back], axis=1),
            jnp.concatenate([b[:, chans : 2 * chans] for b in mix_back], axis=1),
        ],
        axis=1,
    ).astype(F32)
    query_weight_grad = jnp.concatenate([b[:, 2 * chans :] for b in mix_back], axis=1).astype(F32)

    kv_part = contract("tc,tk->ck", normed, kv_low).reshape(depth, 2, 2, shard, 3 * HEAD)
    kv_mine = lax.dynamic_index_in_dim(kv_part, ci, 2, keepdims=False)
    kv_send = lax.dynamic_index_in_dim(kv_part, 1 - ci, 2, keepdims=False)
    kv_sum = kv_mine + swap_c(kv_send.astype(BF)).astype(F32)
    kv_mine = lax.dynamic_index_in_dim(kv_sum, xi, 1, keepdims=False)
    kv_send = lax.dynamic_index_in_dim(kv_sum, 1 - xi, 1, keepdims=False)
    kv_sum = kv_mine + swap_x(kv_send.astype(BF)).astype(F32)
    state_low_all = act_gather(state_low, ti).reshape(count, 2 * NS)
    state_cols = lax.dynamic_slice_in_dim(state_low_all, ti * NS, NS, 1)
    normed_mine = lax.dynamic_index_in_dim(
        normed.reshape(count, depth, 4, shard), me, 2, keepdims=False
    ).reshape(count, depth * shard)
    state_part = contract("tc,tk->ck", normed_mine, state_cols).reshape(depth, shard, NS)
    row_part = jnp.concatenate([kv_sum, state_part], axis=2)
    row_sum = z_scatter([row_part[k] for k in range(depth)], zi, depth)
    keys_values_grad = row_sum[:, : 2 * HEAD].reshape(shard, 2, HEAD)
    step_weight_grad = row_sum[:, 2 * HEAD : 2 * HEAD + heads_in]
    state_mine = row_sum[:, 3 * HEAD :]
    state_weight_grad = order_t(
        state_mine, swap_t(state_mine.astype(BF)).astype(F32), ti, axis=1
    )

    slot = ti * 4 + me

    def spread_out(v):
        wide = jnp.zeros((8,) + v.shape, F32)
        return lax.dynamic_update_index_in_dim(wide, v, slot, 0).reshape(-1)

    shapes = [
        second_gain_grad.shape,
        state_taps_grad.shape,
        (8, CONV + 1, chans),
        (8, chans),
        (8, heads),
        (8, heads),
        (8, heads),
        first_gain_grad.shape,
    ]

    def unrotate(v):
        return lax.dynamic_slice_in_dim(jnp.concatenate([v, v]), width - start, width)

    parts = [
        unrotate(second_gain_grad),
        state_taps_grad.reshape(-1),
        spread_out(filter_taps_grad),
        spread_out(gate_gain_grad),
        spread_out(decay_log_grad),
        spread_out(step_bias_grad),
        spread_out(skip_gain_grad),
        unrotate(first_gain_grad),
    ]
    lengths = [p.size for p in parts]
    packed = jnp.concatenate(parts)
    packed = jnp.pad(packed, (0, -packed.size % 1024)).reshape(-1, 128)
    packed = sum_all(packed, depth).reshape(-1)
    done, at = [], 0
    for shape, length in zip(shapes, lengths):
        done.append(packed[at : at + length].reshape(shape))
        at += length
    dp_at = zi * 4 + me
    second_mine = lax.dynamic_slice_in_dim(done[0], dp_at * shard, shard)
    first_mine = lax.dynamic_slice_in_dim(done[7], dp_at * shard, shard)
    state_shard = state_taps.shape[1]
    state_taps_mine = lax.dynamic_slice_in_dim(done[1], dp_at * state_shard, state_shard, 1)
    mine = [lax.dynamic_slice_in_dim(d, ti * 4, 4, 0) for d in done[2:7]]
    taps_out = jnp.transpose(mine[0], (1, 0, 2)).reshape(CONV + 1, heads_in, HEAD)
    taps_out = lax.dynamic_slice_in_dim(taps_out, dp_at * eighth, eighth, 2)
    gate_out = lax.dynamic_slice_in_dim(
        mine[1].reshape(heads_in, HEAD), dp_at * eighth, eighth, 1
    )
    return (
        output,
        tokens_grad,
        first_mine,
        mixer_in_grad,
        state_weight_grad,
        step_weight_grad,
        taps_out,
        state_taps_mine,
        mine[2].reshape(-1),
        mine[3].reshape(-1),
        mine[4].reshape(-1),
        gate_out,
        mixer_out_grad,
        query_weight_grad,
        keys_values_grad,
        attend_out_grad,
        second_mine,
        gate_up_grad,
        down_weight_grad,
    )


def solution(mesh):
    dp, tensor = mesh.shape["dp"], mesh.shape["tensor"]
    depth = dp // 4
    split = Mesh(mesh.devices.reshape(depth, 2, 2, tensor), ("z", "x", "c", "t"))
    D = ("z", "x", "c")
    T = "t"
    R = ("z", "x", "c", "t")
    weights = (
        P(D),
        P(D, None, T),
        P(D, None),
        P(D, T),
        P(None, T, D),
        P(None, D),
        P(T),
        P(T),
        P(T),
        P(T, D),
        P(T, D),
        P(D, T),
        P(D, None, T),
        P(T, D),
        P(D),
        P(D, None, T),
        P(T, D),
    )

    def run(*args):
        return on_device(depth, *args)

    return jax.shard_map(
        run,
        mesh=split,
        in_specs=(P(R, None), P(D), P(R, None)) + weights,
        out_specs=(P(R, None), P(R, None)) + weights,
        check_vma=False,
    )
```

```python
import functools

import jax
import jax.numpy as jnp
from jax import lax
from jax.experimental import pallas as pl
from jax.experimental.pallas import tpu as pltpu
from jax.sharding import Mesh, PartitionSpec as P

HEAD = 128
NS = 256
CONV = 4
EPS = 1e-05
ROPE_BASE = 100000000000.0
BF = jnp.bfloat16
F32 = jnp.float32
VMEM = pl.BlockSpec(memory_space=pltpu.VMEM)
SMEM = pl.BlockSpec(memory_space=pltpu.SMEM)


def grant(mebibytes):
    return pltpu.CompilerParams(vmem_limit_bytes=mebibytes << 20)


def dot(left, right):
    return jnp.dot(left, right, preferred_element_type=F32)


def contract(form, left, right):
    return jnp.einsum(form, left, right, preferred_element_type=F32)


def silu_slope(values):
    sigma = jax.nn.sigmoid(values)
    return sigma * (1.0 + values * (1.0 - sigma))


def after(v, *earlier):
    return lax.optimization_barrier((v, earlier))[0]


def norm_rows(values, gain):
    scale = lax.rsqrt(jnp.mean(values * values, axis=-1, keepdims=True) + EPS)
    return values * scale * gain, scale


def norm_rows_back(values, gain, scale, grad):
    normal = values * scale
    weighted = grad * gain
    back = scale * (weighted - normal * jnp.mean(weighted * normal, axis=-1, keepdims=True))
    return back, jnp.sum(grad * normal, axis=0)


def swap_c(v):
    return lax.ppermute(v, "c", [(0, 1), (1, 0)])


def swap_x(v):
    return lax.ppermute(v, "x", [(0, 1), (1, 0)])


def swap_t(v):
    return lax.ppermute(v, "t", [(0, 1), (1, 0)])


def swap_xt(v):
    return lax.ppermute(v, ("x", "t"), [(0, 3), (1, 2), (2, 1), (3, 0)])


def swap_xc(v):
    return lax.ppermute(v, ("x", "c"), [(0, 3), (1, 2), (2, 1), (3, 0)])


def pair(mine, other, index, axis):
    return jnp.where(
        index == 0, jnp.stack([mine, other], axis=axis), jnp.stack([other, mine], axis=axis)
    )


def spread_xc(v, xi, ci):
    v = pair(v, swap_x(v), xi, 0)
    return pair(v, swap_c(v), ci, 1)


def order_t(mine, other, ti, axis=0):
    return jnp.where(
        ti == 0,
        jnp.concatenate([mine, other], axis=axis),
        jnp.concatenate([other, mine], axis=axis),
    )


def act_gather(v, ti):
    rows, n = v.shape
    near = pl.pallas_call(
        place_pair,
        in_specs=[SMEM] + [VMEM] * 4,
        out_specs=VMEM,
        out_shape=jax.ShapeDtypeStruct((4 * rows, n), v.dtype),
        compiler_params=grant(8),
    )(ti.reshape(1), v, swap_t(v), swap_x(v), swap_xt(v))
    return near, swap_c(near)


def z_gather(v):
    return lax.all_gather(v, "z", axis=0, tiled=True)


def z_scatter(v):
    return lax.psum_scatter(v, "z", scatter_dimension=0, tiled=True)


def z_gather_first(v, depth):
    if depth != 4:
        return (lax.all_gather(v, "z", axis=0, tiled=False),)
    return (
        lax.ppermute(v, "z", [(0, 2), (1, 3), (2, 0), (3, 1)]),
        lax.ppermute(v, "z", [(0, 1), (1, 2), (2, 3)]),
        lax.ppermute(v, "z", [(1, 0), (2, 1), (3, 2)]),
    )


def z_gather_rel(v, got, zi, depth):
    if depth != 4:
        return jnp.roll(got[0], -zi, axis=0)
    two, below, above = got
    last = lax.ppermute(two, "z", [(2, 3), (1, 0)])
    return jnp.stack([v, jnp.where(zi == 3, last, above), two, jnp.where(zi == 0, last, below)])


def z_scatter_small(parts, zi, depth):
    if depth != 4:
        return lax.psum_scatter(parts.astype(BF), "z", scatter_dimension=0, tiled=False).astype(F32)

    def part(k):
        return lax.dynamic_index_in_dim(parts, (zi + k) % 4, 0, keepdims=False)

    one, two, three = part(1).astype(BF), part(2), part(3).astype(BF)
    corner = lax.ppermute(jnp.where(zi == 3, one, three), "z", [(3, 2), (0, 1)])
    down = lax.ppermute(three, "z", [(1, 0), (2, 1), (3, 2)])
    up = lax.ppermute(one, "z", [(0, 1), (1, 2), (2, 3)])
    mid = (two + corner.astype(F32)).astype(BF)
    far = lax.ppermute(mid, "z", [(0, 2), (1, 3), (2, 0), (3, 1)])
    return part(0) + down.astype(F32) + up.astype(F32) + far.astype(F32)


def sum_z(v, depth):
    if depth != 4:
        return lax.psum(v, "z")
    v = v + lax.ppermute(v, "z", [(0, 1), (1, 0), (2, 3), (3, 2)])
    return v + lax.ppermute(v, "z", [(0, 2), (2, 0), (1, 3), (3, 1)])


def sum_all(v, depth):
    v = v + swap_c(v)
    v = v + swap_x(v)
    v = v + swap_t(v)
    return sum_z(v, depth)


def sum_group(v):
    v = v + jnp.roll(swap_c(v), 2, axis=0)
    got = swap_x(v)
    v = v + jnp.stack([got[1], got[0], got[3], got[2]])
    return v + swap_t(v)


HIGH = lax.Precision.HIGHEST


def mm(left, right):
    return lax.dot_general(left, right, (((1,), (0,)), ((), ())), preferred_element_type=F32)


def mm_rt(left, right):
    return lax.dot_general(left, right, (((1,), (1,)), ((), ())), preferred_element_type=F32)


def mm_lt(left, right):
    return lax.dot_general(left, right, (((0,), (0,)), ((), ())), preferred_element_type=F32)


def mm_exact(left, right):
    return lax.dot_general(
        left, right, (((1,), (0,)), ((), ())), precision=HIGH, preferred_element_type=F32
    )


def sigmoid(v):
    return 1.0 / (1.0 + jnp.exp(-v))


def tap_masks(seg_col, rows):
    at = lax.broadcasted_iota(jnp.int32, (rows, HEAD), 0)
    masks = [None]
    for offset in range(1, CONV):
        same = (pltpu.roll(seg_col, offset, 0) == seg_col) & (at >= offset)
        masks.append(jnp.where(same, 1.0, 0.0)[:, :1])
    return masks


def filter_rows(values, taps, masks):
    total = taps[CONV : CONV + 1] + taps[0:1] * values
    for offset in range(1, CONV):
        total = total + taps[offset : offset + 1] * (pltpu.roll(values, offset, 0) * masks[offset])
    return total


def filter_rows_back(values, taps, masks, grad):
    rows = values.shape[0]
    tap_grads = [jnp.sum(grad * values, axis=0, keepdims=True)]
    back = taps[0:1] * grad
    for offset in range(1, CONV):
        masked = grad * masks[offset]
        tap_grads.append(
            jnp.sum(masked * pltpu.roll(values, offset, 0), axis=0, keepdims=True)
        )
        back = back + taps[offset : offset + 1] * pltpu.roll(masked, rows - offset, 0)
    tap_grads.append(jnp.sum(grad, axis=0, keepdims=True))
    return back, tap_grads


def causal_of(seg_col, seg_row, rows):
    down = lax.broadcasted_iota(jnp.int32, (rows, rows), 0)
    across = lax.broadcasted_iota(jnp.int32, (rows, rows), 1)
    wide = jnp.broadcast_to(seg_col[:, :1], (rows, rows))
    return (wide == seg_row[0:1]) & (across <= down)


def wide_steps(step_cols, pick_ref, head_ref, rows):
    raw = mm_exact(step_cols, pick_ref[...]) + head_ref[1:2]
    step = jnp.maximum(raw, 0.0) + jnp.log1p(jnp.exp(-jnp.abs(raw)))
    rate = head_ref[0:1] * step
    down = lax.broadcasted_iota(jnp.int32, (rows, rows), 0)
    across = lax.broadcasted_iota(jnp.int32, (rows, rows), 1)
    lower = jnp.where(across <= down, 1.0, 0.0)
    return raw, step, rate, mm_exact(lower, rate)


def decay_of(level, h, causal, rows):
    part = level[:, h * HEAD : (h + 1) * HEAD]
    across = jnp.transpose(part)[0:1]
    diff = jnp.broadcast_to(part[:, :1], (rows, rows)) - across
    return jnp.where(causal, jnp.exp(jnp.where(causal, diff, 0.0)), 0.0)


def rope(v, cosine, sine):
    return v * cosine + pltpu.roll(v, HEAD // 2, 1) * sine


def mixer_forward(heads, mix_ref, row_ref, seg_ref, seg_row_ref, taps_ref, staps_ref, pick_ref,
                  head_ref, cos_ref, sin_ref, gated_ref, square_ref, attended_ref):
    rows = mix_ref.shape[0]
    chans = heads * HEAD
    seg_col, seg_row = seg_ref[...], seg_row_ref[0]
    causal = causal_of(seg_col, seg_row, rows)
    masks = tap_masks(seg_col, rows)
    gate = mix_ref[:, :chans]
    pre = filter_rows(mix_ref[:, chans : 2 * chans], taps_ref[...], masks)
    filtered = pre * sigmoid(pre)
    spre = filter_rows(row_ref[:, : 2 * NS], staps_ref[...], masks)
    sact = (spre * sigmoid(spre)).astype(BF)
    affinity = mm_rt(sact[:, NS:], sact[:, :NS])
    _, step, _, level = wide_steps(row_ref[:, 2 * NS + 2 * HEAD :], pick_ref, head_ref, rows)
    inner = (filtered * step).astype(BF)
    gate_act = gate * sigmoid(gate)
    squares = jnp.zeros((rows, 1), F32)
    for h in range(heads):
        at = slice(h * HEAD, (h + 1) * HEAD)
        mixing = (affinity * decay_of(level, h, causal, rows)).astype(BF)
        scanned = mm(mixing, inner[:, at])
        gated = (scanned + head_ref[2:3, at] * filtered[:, at]) * gate_act[:, at]
        gated_ref[:, at] = gated
        squares = squares + jnp.sum(gated * gated, axis=1, keepdims=True)
    square_ref[0] = jnp.transpose(jnp.broadcast_to(squares, (rows, HEAD)))[:8]
    cosine, sine = cos_ref[...], sin_ref[...]
    query = rope(mix_ref[:, 2 * chans :], cosine, sine).astype(BF)
    keys = rope(row_ref[:, 2 * NS : 2 * NS + HEAD], cosine, sine).astype(BF)
    values = row_ref[:, 2 * NS + HEAD : 2 * NS + 2 * HEAD].astype(BF)
    scores = jnp.where(causal, mm_rt(query, keys) * (HEAD ** -0.5), -1e30)
    raised = jnp.exp(scores - jnp.max(scores, axis=1, keepdims=True))
    shares = (raised / jnp.sum(raised, axis=1, keepdims=True)).astype(BF)
    attended_ref[...] = mm(shares, values).astype(BF)


def mixer_backward(heads, total_chans, mix_ref, row_ref, seg_ref, seg_row_ref, taps_ref, staps_ref,
                   pick_ref, head_ref, cos_ref, sin_ref, slot_ref, grad_ref, gated_ref, scale_ref,
                   gain_ref, sum_ref, mix_low_ref, kv_low_ref, state_ref, small_ref, staps_out_ref):
    rows = mix_ref.shape[0]
    chans = heads * HEAD
    seg_col, seg_row = seg_ref[...], seg_row_ref[0]
    causal = causal_of(seg_col, seg_row, rows)
    masks = tap_masks(seg_col, rows)
    gate = mix_ref[:, :chans]
    filter_input = mix_ref[:, chans : 2 * chans]
    taps, staps = taps_ref[...], staps_ref[...]
    pre = filter_rows(filter_input, taps, masks)
    sig = sigmoid(pre)
    filtered = pre * sig
    state_raw = row_ref[:, : 2 * NS]
    spre = filter_rows(state_raw, staps, masks)
    ssig = sigmoid(spre)
    sact = (spre * ssig).astype(BF)
    affinity = mm_rt(sact[:, NS:], sact[:, :NS])
    raw, step, rate, level = wide_steps(row_ref[:, 2 * NS + 2 * HEAD :], pick_ref, head_ref, rows)
    inner = (filtered * step).astype(BF)
    gsig = sigmoid(gate)
    gate_act = gate * gsig
    norm_grad = grad_ref[:, :chans]
    scale = jnp.transpose(scale_ref[0])[:, :1]
    normal = gated_ref[...] * scale
    mean = jnp.transpose(sum_ref[0])[:, :1] * (1.0 / total_chans)
    gated_grad = scale * (norm_grad * gain_ref[0:1] - normal * mean)
    mix_state_grad = gated_grad * gate_act
    scanned_low = mix_state_grad.astype(BF)
    skip = head_ref[2:3]
    state_mix, inner_grads, level_grads, step_sums = [], [], [], []
    affinity_grad = jnp.zeros((rows, rows), F32)
    for h in range(heads):
        at = slice(h * HEAD, (h + 1) * HEAD)
        decay = decay_of(level, h, causal, rows)
        mixing_full = affinity * decay
        mixing = mixing_full.astype(BF)
        state_mix.append(mm(mixing, inner[:, at]) + skip[:, at] * filtered[:, at])
        mixing_grad = mm_rt(scanned_low[:, at], inner[:, at])
        inner_grad = mm_lt(mixing, scanned_low[:, at])
        flow = mixing_grad * mixing_full
        change = jnp.sum(flow - jnp.transpose(flow), axis=1, keepdims=True)
        level_grads.append(jnp.broadcast_to(change, (rows, HEAD)))
        affinity_grad = affinity_grad + mixing_grad * decay
        inner_grads.append(inner_grad)
        reach = jnp.sum(inner_grad * filtered[:, at], axis=1, keepdims=True)
        step_sums.append(jnp.broadcast_to(reach, (rows, HEAD)))
    state_mix = jnp.concatenate(state_mix, axis=1)
    inner_grad = jnp.concatenate(inner_grads, axis=1)
    mix_low_ref[:, :chans] = (
        gated_grad * state_mix * (gsig * (1.0 + gate * (1.0 - gsig)))
    ).astype(BF)
    down = lax.broadcasted_iota(jnp.int32, (rows, rows), 0)
    across = lax.broadcasted_iota(jnp.int32, (rows, rows), 1)
    upper = jnp.where(across >= down, 1.0, 0.0)
    rate_grad = mm_exact(upper, jnp.concatenate(level_grads, axis=1))
    step_grad = rate_grad * head_ref[0:1] + jnp.concatenate(step_sums, axis=1)
    step_pre_grad = step_grad * sigmoid(raw)
    filtered_grad = skip * mix_state_grad + inner_grad * step
    input_grad, tap_grads = filter_rows_back(
        filter_input, taps, masks, filtered_grad * (sig * (1.0 + pre * (1.0 - sig)))
    )
    mix_low_ref[:, chans : 2 * chans] = input_grad.astype(BF)
    extra = [
        jnp.sum(norm_grad * normal, axis=0, keepdims=True),
        jnp.sum(mix_state_grad * filtered, axis=0, keepdims=True),
        jnp.sum(rate_grad * rate, axis=0, keepdims=True),
        jnp.sum(step_pre_grad, axis=0, keepdims=True),
    ]
    small_ref[0] = jnp.zeros(small_ref.shape[1:], F32)
    for i, v in enumerate(tap_grads + extra):
        small_ref[0, i : i + 1] = v
    low = affinity_grad.astype(BF)
    read_grad = mm(low, sact[:, :NS])
    write_grad = mm_lt(low, sact[:, NS:])
    act_grad = jnp.concatenate([write_grad, read_grad], axis=1)
    state_grad, stap_grads = filter_rows_back(
        state_raw, staps, masks, act_grad * (ssig * (1.0 + spre * (1.0 - ssig)))
    )
    state_ref[...] = state_grad
    staps_out_ref[0] = jnp.zeros(staps_out_ref.shape[1:], F32)
    for i, v in enumerate(stap_grads):
        staps_out_ref[0, i : i + 1] = v
    cosine, sine = cos_ref[...], sin_ref[...]
    query = rope(mix_ref[:, 2 * chans :], cosine, sine).astype(BF)
    keys = rope(row_ref[:, 2 * NS : 2 * NS + HEAD], cosine, sine).astype(BF)
    values = row_ref[:, 2 * NS + HEAD : 2 * NS + 2 * HEAD].astype(BF)
    root = HEAD ** -0.5
    scores = jnp.where(causal, mm_rt(query, keys) * root, -1e30)
    raised = jnp.exp(scores - jnp.max(scores, axis=1, keepdims=True))
    shares = raised / jnp.sum(raised, axis=1, keepdims=True)
    attend_grad = grad_ref[:, chans:].astype(BF)
    values_grad = mm_lt(shares.astype(BF), attend_grad)
    shares_grad = mm_rt(attend_grad, values)
    scores_low = (
        shares * (shares_grad - jnp.sum(shares_grad * shares, axis=1, keepdims=True))
    ).astype(BF)
    query_grad = mm(scores_low, keys) * root
    keys_grad = mm_lt(scores_low, query) * root
    mix_low_ref[:, 2 * chans :] = rope(query_grad, cosine, -sine).astype(BF)
    kv_low_ref[:, :HEAD] = rope(keys_grad, cosine, -sine).astype(BF)
    kv_low_ref[:, HEAD : 2 * HEAD] = values_grad.astype(BF)
    kv_low_ref[:, 2 * HEAD :] = mm(step_pre_grad.astype(BF), slot_ref[...]).astype(BF)


def over_groups(kernel, groups, rows, args, whole, outs):
    def spec(shape):
        if len(shape) == 3:
            return pl.BlockSpec((1,) + shape[1:], lambda g: (g, 0, 0))
        return pl.BlockSpec((rows, shape[1]), lambda g: (g, 0))

    def fixed(shape):
        return pl.BlockSpec(shape, lambda g: (0, 0))

    specs = [
        fixed(v.shape) if w else spec(v.shape) for v, w in zip(args, whole)
    ]
    return pl.pallas_call(
        kernel,
        grid=(groups,),
        in_specs=specs,
        out_specs=[spec(o.shape) for o in outs],
        out_shape=outs,
        compiler_params=grant(24),
    )(*args)


def place_pair(ti_ref, own_ref, t_ref, x_ref, xt_ref, out_ref):
    rows = own_ref.shape[0]
    at = ti_ref[0]
    for i, ref in ((at, own_ref), (1 - at, t_ref), (2 + at, x_ref), (3 - at, xt_ref)):
        out_ref[pl.ds(pl.multiple_of(i * rows, rows), rows)] = ref[...]


def place_rows(at_ref, own_ref, x_ref, c_ref, xc_ref, out_ref, small_ref):
    z, me = at_ref[0], at_ref[1]
    depth, rows = out_ref.shape[0], out_ref.shape[2]
    for k in range(depth):
        to = lax.rem(z + k, depth)
        for offset, src in ((0, own_ref), (2, x_ref), (1, c_ref), (3, xc_ref)):
            out_ref[to, me ^ offset] = src[k, :rows]
            small_ref[to, me ^ offset] = src[k, rows:]


def times(rows, w):
    return tuple(dot(r, w) for r in rows)


def grads(left, right):
    near, far = (contract("tc,tk->ck", a, b) for a, b in zip(left, right))
    return (near + far).astype(BF)


def split_kernel(ti_ref, total_ref, got_ref, mine_ref, t_ref, x_ref, xt_ref):
    rows = mine_ref.shape[0]
    at = ti_ref[0]

    def part(i):
        where = pl.ds(pl.multiple_of(i * rows, rows), rows)
        return total_ref[where] + got_ref[where].astype(F32)

    mine_ref[...] = part(at)
    t_ref[...] = part(1 - at).astype(BF)
    x_ref[...] = part(2 + at).astype(BF)
    xt_ref[...] = part(3 - at).astype(BF)


def split_rows(keep, send, ti):
    got = swap_c(send.astype(BF))
    count, width = keep.shape
    rows, tile = count // 4, 512
    part = pl.BlockSpec((rows, tile), lambda j: (0, j))
    full = pl.BlockSpec((count, tile), lambda j: (0, j))
    return pl.pallas_call(
        split_kernel,
        grid=(width // tile,),
        in_specs=[SMEM, full, full],
        out_specs=[part] * 4,
        out_shape=[jax.ShapeDtypeStruct((rows, width), F32)]
        + [jax.ShapeDtypeStruct((rows, width), BF)] * 3,
        compiler_params=grant(8),
    )(ti.reshape(1), keep, got)


def join_rows(mine, to_t, to_x, to_xt):
    got = (swap_t(to_t), swap_x(to_x), swap_xt(to_xt))
    return mine + got[0].astype(F32) + got[1].astype(F32) + got[2].astype(F32)


def split_back(terms, ti):
    keep, send = (sum(contract("tk,ck->tc", a[i], w) for a, w in terms) for i in (0, 1))
    return split_rows(keep, send, ti)


def times_back(terms, ti):
    return join_rows(*split_back(terms, ti))


def turned(block):
    return jnp.transpose(block.astype(F32)).astype(BF)


def prepare_kernel(plan, xi_ref, *refs):
    sources, keep_ref, send_ref = refs[:-2], refs[-2], refs[-1]
    first = xi_ref[0] == 0
    for c in range(2):
        at = 0
        for ref, is_turned in zip(sources, plan):
            if is_turned:
                n = ref.shape[0] // 4
                low, high = (turned(ref[(x * 2 + c) * n : (x * 2 + c + 1) * n]) for x in range(2))
            else:
                n = ref.shape[1] // 4
                low, high = (ref[:, (x * 2 + c) * n : (x * 2 + c + 1) * n] for x in range(2))
            keep_ref[c, :, at : at + n] = jnp.where(first, low, high)
            send_ref[c, :, at : at + n] = jnp.where(first, high, low)
            at += n


def middle_kernel(ci_ref, keep_ref, got_ref, keep_out, send_out):
    c = ci_ref[0]
    for i, ref in enumerate((keep_ref, got_ref)):
        keep_out[i] = ref[c]
        send_out[i] = ref[1 - c]


def end_kernel(at_ref, keep_ref, got_ref, out_ref):
    x, c = at_ref[0], at_ref[1]
    for i, ref in enumerate((keep_ref, got_ref)):
        out_ref[x, c ^ i] = ref[0]
        out_ref[1 - x, c ^ i] = ref[1]


def simple(kernel, args, outs, scalars=1, grant_of=8):
    single = not isinstance(outs, list)
    return pl.pallas_call(
        kernel,
        in_specs=[SMEM] * scalars + [VMEM] * (len(args) - scalars),
        out_specs=VMEM if single else [VMEM] * len(outs),
        out_shape=outs,
        compiler_params=grant(grant_of),
    )(*args)


def middle(keep, send, xi, ci):
    shape = jax.ShapeDtypeStruct(keep.shape, BF)
    keep, send = simple(middle_kernel, (ci.reshape(1), keep, swap_x(send)), [shape, shape])
    return keep, swap_c(send)


def prepare(sources, plan, xi):
    rows = [s.shape[1] if t else s.shape[0] for s, t in zip(sources, plan)][0]
    wide = sum((s.shape[0] if t else s.shape[1]) // 4 for s, t in zip(sources, plan))
    shape = jax.ShapeDtypeStruct((2, rows, wide), BF)
    return simple(
        functools.partial(prepare_kernel, plan), (xi.reshape(1), *sources), [shape, shape]
    )


def deal_out(keep, send, xi, ci):
    keep, got = middle(keep, send, xi, ci)
    out = jax.ShapeDtypeStruct((2,) + keep.shape, BF)
    return simple(end_kernel, (jnp.stack([xi, ci]), keep, got), out).reshape(
        -1, keep.shape[-1]
    )


def start_kernel(xi_ref, blocks_ref, keep_ref, send_ref):
    keep_ref[...] = blocks_ref[xi_ref[0]]
    send_ref[...] = blocks_ref[1 - xi_ref[0]]


def finish_kernel(plan, at_ref, keep_ref, got_ref, *outs):
    x, c = at_ref[0], at_ref[1]
    for q in range(4):
        own = c == q % 2
        offset = x ^ (q // 2)
        at = 0
        for ref, kind in zip(outs, plan):
            n = (ref.shape[0] if kind == "turned" else ref.shape[-1]) // 4
            for i in range(2 if kind == "two" else 1):
                block = jnp.where(
                    own, keep_ref[offset, :, at : at + n], got_ref[offset, :, at : at + n]
                ).astype(F32)
                if kind == "turned":
                    ref[q * n : (q + 1) * n] = jnp.transpose(block)
                elif kind == "two":
                    ref[:, i, q * n : (q + 1) * n] = block
                else:
                    ref[:, q * n : (q + 1) * n] = block
                at += n


def deal_back(summed, plan, widths, xi, ci):
    shard = summed.shape[0] // 4
    blocks = summed.reshape(2, 2, shard, -1)
    shape = jax.ShapeDtypeStruct(blocks.shape[1:], BF)
    keep, send = simple(start_kernel, (xi.reshape(1), blocks), [shape, shape])
    keep, got = middle(keep, send, xi, ci)
    shapes = {"turned": lambda n: (4 * n, shard), "two": lambda n: (shard, 2, 4 * n)}
    outs = [
        jax.ShapeDtypeStruct(shapes.get(k, lambda n: (shard, 4 * n))(n), F32)
        for n, k in zip(widths, plan)
    ]
    return simple(
        functools.partial(finish_kernel, plan), (jnp.stack([xi, ci]), keep, got), outs
    )


def kv_first_kernel(ci_ref, part_ref, keep_ref, send_ref):
    c = ci_ref[0]
    for k in range(part_ref.shape[0]):
        for x in range(2):
            keep_ref[x, k] = part_ref[k, x, c]
            send_ref[x, k] = part_ref[k, x, 1 - c]


def kv_second_kernel(xi_ref, keep_ref, got_ref, keep_out, send_out):
    x = xi_ref[0]
    keep_out[...] = keep_ref[x].astype(F32) + got_ref[x].astype(F32)
    send_out[...] = (keep_ref[1 - x].astype(F32) + got_ref[1 - x].astype(F32)).astype(BF)


def on_device(
    depth,
    tokens,
    segments,
    cotangent,
    first_gain,
    mixer_in,
    state_weight,
    step_weight,
    filter_taps,
    state_taps,
    decay_log,
    step_bias,
    skip_gain,
    gate_gain,
    mixer_out,
    query_weight,
    key_value_matrix,
    attend_out,
    second_gain,
    gate_up,
    down_weight,
):
    zi, xi = lax.axis_index("z"), lax.axis_index("x")
    ci, ti = lax.axis_index("c"), lax.axis_index("t")
    me = xi * 2 + ci
    rows, width = tokens.shape
    group = segments.shape[0]
    shard = mixer_in.shape[0]
    block = 4 * shard
    heads_in = decay_log.shape[0]
    heads = heads_in // 4
    chans = heads * HEAD
    total_chans = 2 * heads_in * HEAD
    ffn = gate_up.shape[2] // 4
    count = 4 * group
    scale = HEAD ** (-0.5)

    pieces = [first_gain, second_gain, filter_taps, state_taps, gate_gain, segments]
    sizes = [p.size for p in pieces]
    step_pad = jnp.pad(step_weight, ((0, 0), (0, 128 - heads_in)))
    row_pack = jnp.concatenate(
        [state_weight, key_value_matrix.reshape(shard, -1), step_pad], axis=1
    )
    row_wide = row_pack.shape[1]
    vec = jnp.concatenate([p.astype(BF).reshape(-1) for p in pieces])
    vec = jnp.pad(vec, (0, 16 * row_wide - vec.size)).reshape(16, row_wide)
    row_own = jnp.concatenate([row_pack, vec])
    row_got = z_gather_first(row_own, depth)

    first_plan = (True, True, False, False, False)
    first_keep, first_send = prepare(
        (mixer_out, attend_out, mixer_in[:, 0], mixer_in[:, 1], query_weight), first_plan, xi
    )
    first_keep = after(first_keep, *row_got)
    first_mine = deal_out(first_keep, first_send, xi, ci)
    wide = chans + HEAD

    row_z = z_gather_rel(row_own, row_got, zi, depth)
    first_mine = after(first_mine, row_z)
    first_w = z_gather(first_mine)
    row_x = swap_x(row_z)
    row_full, small = simple(
        place_rows,
        (jnp.stack([zi, me]), row_z, row_x, swap_c(row_z), swap_c(row_x)),
        [
            jax.ShapeDtypeStruct((depth, 4, shard, row_wide), BF),
            jax.ShapeDtypeStruct((depth, 4, 16, row_wide), BF),
        ],
        grant_of=16,
    )
    row_full = row_full.reshape(width, row_wide)
    kv_at = 2 * NS
    state_full = row_full[:, :kv_at]
    small = small.reshape(depth, 4, -1)
    offsets = [sum(sizes[:i]) for i in range(6)]
    cut = [small[:, :, at : at + size] for at, size in zip(offsets, sizes)]
    seg_all = lax.dynamic_index_in_dim(cut[5], zi, 0, keepdims=False).astype(F32)
    segs = jnp.stack(
        [lax.dynamic_index_in_dim(seg_all, me ^ k, 0, keepdims=False) for k in (0, 2, 1, 3)]
    )
    first_full = cut[0].reshape(-1).astype(F32)
    second_full = cut[1].reshape(-1).astype(F32)
    eighth = filter_taps.shape[2]
    taps_all = jnp.transpose(
        cut[2].reshape(depth, 4, CONV + 1, heads_in, eighth), (2, 3, 0, 1, 4)
    ).reshape(CONV + 1, 4, chans)
    taps = lax.dynamic_index_in_dim(taps_all, me, 1, keepdims=False).astype(F32)
    staps = (
        jnp.transpose(cut[3].reshape(depth, 4, CONV + 1, -1), (2, 0, 1, 3))
        .reshape(CONV + 1, 2 * NS)
        .astype(F32)
    )
    gate_all = jnp.transpose(
        cut[4].reshape(depth, 4, heads_in, eighth), (2, 0, 1, 3)
    ).reshape(4, chans)
    gate_gain_mine = lax.dynamic_index_in_dim(gate_all, me, 0, keepdims=False).astype(F32)

    order = jnp.arange(group)
    live_all = (segs >= 0).astype(F32)
    same = (segs[:, :, None] == segs[:, None, :]) & (order[None, None, :] <= order[None, :, None])
    position = jnp.sum(same.astype(F32), axis=2) - 1.0
    half = HEAD // 2
    frequency = ROPE_BASE ** (-2.0 * jnp.arange(half).astype(F32) / HEAD)
    angle = position.reshape(count, 1) * frequency[None, :]
    cosine, sine = jnp.cos(angle), jnp.sin(angle)
    cosine = jnp.concatenate([cosine, cosine], axis=1)
    sine = jnp.concatenate([-sine, sine], axis=1)
    live_mine = lax.dynamic_slice_in_dim(
        (segments >= 0).astype(F32), ti * rows, rows
    )[:, None]
    seg_cols = jnp.broadcast_to(segs.reshape(count, 1), (count, HEAD))
    seg_rows = jnp.broadcast_to(segs[:, None, :], (4, 8, group))

    def halves(v):
        n = v.shape[0] // 2
        return v[:n], v[n:]

    my_log = lax.dynamic_slice_in_dim(decay_log, me * heads, heads)
    my_bias = lax.dynamic_slice_in_dim(step_bias, me * heads, heads)
    my_skip = lax.dynamic_slice_in_dim(skip_gain, me * heads, heads)
    head_rows = jnp.pad(
        jnp.repeat(jnp.stack([-jnp.exp(my_log), my_bias, my_skip]), HEAD, axis=1), ((0, 5), (0, 0))
    )
    lane_head = me * heads + jnp.arange(chans) // HEAD
    picker = (jnp.arange(128)[:, None] == lane_head[None, :]).astype(F32)
    first_lane = (jnp.arange(chans) % HEAD == 0)[:, None]
    slots = ((jnp.arange(128)[None, :] == lane_head[:, None]) & first_lane).astype(BF)
    taps_pad = jnp.pad(taps, ((0, 3), (0, 0)))
    staps_pad = jnp.pad(staps, ((0, 3), (0, 0)))
    gain_pad = jnp.pad(gate_gain_mine[None], ((0, 7), (0, 0)))

    resid = tokens.astype(F32)
    normed_input, scale_one = norm_rows(resid, first_full)
    normed_low = normed_input.astype(BF)
    normed = act_gather(normed_low, ti)
    then_plan = (False, False, True)
    then_keep, then_send = prepare(
        (gate_up[:, 0], gate_up[:, 1], down_weight), then_plan, xi
    )
    then_send = after(then_send, normed[0], row_x)
    then_mine = deal_out(then_keep, then_send, xi, ci)
    gu_w, down_w = z_gather(then_mine[:, : 2 * ffn]), z_gather(then_mine[:, 2 * ffn :])
    grad_out = cotangent.astype(F32)
    feed_low = after((live_mine * grad_out).astype(BF), then_mine)
    feed_grad = act_gather(feed_low, ti)
    row_out = times(normed, row_full)
    first_w = after(first_w, row_out)
    out_w, mix_w = first_w[:, :wide], first_w[:, wide:]
    mix_out = times(normed, mix_w)

    per_half = list(
        zip(mix_out, row_out, halves(seg_cols), halves(seg_rows), halves(cosine), halves(sine))
    )
    near_far, whole = [], (False,) * 4 + (True,) * 4 + (False,) * 2
    for m, r, sc, sr, co, si in per_half:
        near_far.append((m, r, sc, sr, taps_pad, staps_pad, picker, head_rows, co, si))
    ahead = [
        over_groups(
            functools.partial(mixer_forward, heads),
            2,
            group,
            common,
            whole,
            [
                jax.ShapeDtypeStruct((count // 2, chans), F32),
                jax.ShapeDtypeStruct((2, 8, group), F32),
                jax.ShapeDtypeStruct((count // 2, HEAD), BF),
            ],
        )
        for common in near_far
    ]
    squares = jnp.concatenate([ahead[0][1], ahead[1][1]])
    gate_scale = halves(lax.rsqrt(sum_group(squares) / total_chans + EPS))
    gate_normal = [
        a[0] * g[:, 0].reshape(count // 2, 1) for a, g in zip(ahead, gate_scale)
    ]

    out_w = after(out_w, feed_grad)
    branch = [
        jnp.concatenate([(n * gate_gain_mine).astype(BF), a[2]], axis=1)
        for n, a in zip(gate_normal, ahead)
    ]
    hidden = resid + live_mine * times_back([(branch, out_w)], ti)
    second, scale_two = norm_rows(hidden, second_full)

    second_all = act_gather(second.astype(BF), ti)
    gu_low, activation = [], []
    for second_half, feed_half in zip(second_all, feed_grad):
        gate_up_out = dot(second_half, gu_w)
        gate_part, up_part = gate_up_out[:, :ffn], gate_up_out[:, ffn:]
        act_grad = dot(feed_half, down_w)
        act = jax.nn.silu(gate_part)
        activation.append((act * up_part).astype(BF))
        gu_low.append(
            jnp.concatenate([act_grad * up_part * silu_slope(gate_part), act_grad * act], axis=1)
            .astype(BF)
        )
    down_sum = z_scatter(grads(feed_grad, activation))
    gu_sum = z_scatter(grads(second_all, gu_low))
    second_split = split_back([(gu_low, gu_w)], ti)
    second_grad = join_rows(*second_split)
    feed_split = split_back([(after(activation, second_split), down_w)], ti)
    hidden_part, second_gain_grad = norm_rows_back(hidden, second_full, scale_two, second_grad)
    hidden_grad = grad_out + hidden_part
    mix_grad = act_gather((live_mine * hidden_grad).astype(BF), ti)
    feed_split = after(feed_split, mix_grad[0])
    output = (hidden + live_mine * join_rows(*feed_split)).astype(BF)
    (down_weight_grad,) = deal_back(
        after(down_sum, mix_grad[0]), ("turned",), (ffn,), xi, ci
    )
    branch_grad = times(mix_grad, after(out_w, feed_split))
    out_term = grads(mix_grad, branch)
    out_sum = z_scatter(out_term)

    inner_sum = jnp.concatenate(
        [
            jnp.sum(b[:, :chans] * gate_gain_mine * n, axis=-1).reshape(2, 1, group)
            for b, n in zip(branch_grad, gate_normal)
        ]
    )
    inner_sum = sum_group(jnp.broadcast_to(inner_sum, (4, 8, group)))
    inner_sum = halves(after(inner_sum, out_term))
    inner_sum = (inner_sum[0], after(inner_sum[1], gu_sum))
    back = [
        over_groups(
            functools.partial(mixer_backward, heads, total_chans),
            2,
            group,
            common + (slots, branch_grad[i], ahead[i][0], gate_scale[i], gain_pad, inner_sum[i]),
            whole + (True, False, False, False, True, False),
            [
                jax.ShapeDtypeStruct((count // 2, 2 * chans + HEAD), BF),
                jax.ShapeDtypeStruct((count // 2, 3 * HEAD), BF),
                jax.ShapeDtypeStruct((count // 2, 2 * NS), F32),
                jax.ShapeDtypeStruct((2, 16, chans), F32),
                jax.ShapeDtypeStruct((2, 8, 2 * NS), F32),
            ],
        )
        for i, common in enumerate(near_far)
    ]
    mix_low, kv_low, state_raw_grad, small_rows, small_state = zip(*back)
    normed_late = after(normed, output, down_weight_grad)
    mix_term = grads(normed_late, mix_low)
    mix_sum = z_scatter(mix_term)

    small_rows = jnp.concatenate(small_rows)
    small_state = jnp.concatenate(small_state)
    state_taps_grad = jnp.sum(small_state, axis=0)[: CONV + 1]
    state_near = after(state_raw_grad[0], mix_term)
    state_split = split_rows(state_near, state_raw_grad[1], ti)
    summed_split = split_back(
        [(after(mix_low, state_split), mix_w), (kv_low, row_full[:, kv_at:])], ti
    )
    head_rows_sum = jnp.sum(after(small_rows, summed_split), axis=0)
    head_all = spread_xc(sum_z(head_rows_sum, depth), xi, ci).reshape(4, 16, chans)
    state_low = join_rows(*state_split).astype(BF)
    summed = join_rows(*summed_split)
    (gate_up_grad,) = deal_back(after(gu_sum, summed_split), ("two",), (ffn,), xi, ci)
    mixer_out_grad, attend_out_grad = deal_back(
        after(out_sum, summed_split), ("turned",) * 2, (chans, HEAD), xi, ci
    )
    state_low_all = act_gather(state_low, ti)
    normed_grad = summed + contract("tn,cn->tc", state_low, state_full)
    resid_part, first_gain_grad = norm_rows_back(resid, first_full, scale_one, normed_grad)
    tokens_grad = hidden_grad + resid_part

    mixer_in_grad, query_weight_grad = deal_back(
        mix_sum, ("two", ""), (chans, HEAD), xi, ci
    )
    kv_part = grads(normed, after(kv_low, summed_split)).reshape(depth, 2, 2, shard, 3 * HEAD)
    shape = jax.ShapeDtypeStruct((2, depth, shard, 3 * HEAD), BF)
    kv_keep, kv_send = simple(kv_first_kernel, (ci.reshape(1), kv_part), [shape, shape])
    kv_keep, kv_send = simple(
        kv_second_kernel,
        (xi.reshape(1), kv_keep, swap_c(kv_send)),
        [jax.ShapeDtypeStruct(shape.shape[1:], F32), jax.ShapeDtypeStruct(shape.shape[1:], BF)],
    )
    kv_sum = kv_keep + swap_x(kv_send).astype(F32)
    state_part = grads(normed, state_low_all).reshape(depth, 4, shard, 2 * NS)
    state_part = lax.dynamic_slice(
        state_part, (0, me, 0, ti * NS), (depth, 1, shard, NS)
    )[:, 0].astype(F32)
    row_part = jnp.concatenate([kv_sum, state_part], axis=2)
    row_sum = z_scatter_small(row_part, zi, depth)
    keys_values_grad = row_sum[:, : 2 * HEAD].reshape(shard, 2, HEAD)
    step_weight_grad = row_sum[:, 2 * HEAD : 2 * HEAD + heads_in]
    state_mine = row_sum[:, 3 * HEAD :]
    state_weight_grad = order_t(
        state_mine, swap_t(state_mine.astype(BF)).astype(F32), ti, axis=1
    )

    dp_at = zi * 4 + me
    parts = [second_gain_grad, state_taps_grad.reshape(-1), first_gain_grad]
    packed = sum_all(jnp.concatenate(parts).reshape(-1, 128), depth).reshape(-1)
    second_mine = lax.dynamic_slice_in_dim(packed, dp_at * shard, shard)
    first_mine = lax.dynamic_slice_in_dim(
        packed[packed.size - width :], dp_at * shard, shard
    )
    state_shard = state_taps.shape[1]
    state_taps_mine = lax.dynamic_slice_in_dim(
        packed[width : packed.size - width].reshape(CONV + 1, 2 * NS),
        dp_at * state_shard,
        state_shard,
        1,
    )
    by_head = jnp.transpose(
        head_all[:, :9].reshape(4, 9, heads, HEAD), (1, 0, 2, 3)
    ).reshape(9, heads_in, HEAD)
    taps_out = lax.dynamic_slice_in_dim(by_head[: CONV + 1], dp_at * eighth, eighth, 2)
    gate_out = lax.dynamic_slice_in_dim(by_head[5], dp_at * eighth, eighth, 1)
    return (
        output,
        tokens_grad,
        first_mine,
        mixer_in_grad,
        state_weight_grad,
        step_weight_grad,
        taps_out,
        state_taps_mine,
        by_head[7, :, 0],
        by_head[8, :, 0],
        jnp.sum(by_head[6], axis=1),
        gate_out,
        mixer_out_grad,
        query_weight_grad,
        keys_values_grad,
        attend_out_grad,
        second_mine,
        gate_up_grad,
        down_weight_grad,
    )


def solution(mesh):
    dp, tensor = mesh.shape["dp"], mesh.shape["tensor"]
    depth = dp // 4
    split = Mesh(mesh.devices.reshape(depth, 2, 2, tensor), ("z", "x", "c", "t"))
    D = ("z", "x", "c")
    T = "t"
    R = ("z", "x", "c", "t")
    weights = (
        P(D),
        P(D, None, T),
        P(D, None),
        P(D, T),
        P(None, T, D),
        P(None, D),
        P(T),
        P(T),
        P(T),
        P(T, D),
        P(T, D),
        P(D, T),
        P(D, None, T),
        P(T, D),
        P(D),
        P(D, None, T),
        P(T, D),
    )

    def run(*args):
        return on_device(depth, *args)

    return jax.shard_map(
        run,
        mesh=split,
        in_specs=(P(R, None), P(D), P(R, None)) + weights,
        out_specs=(P(R, None), P(R, None)) + weights,
        check_vma=False,
    )
```

```python
import functools

import jax
import jax.numpy as jnp
from jax import lax
from jax.experimental import pallas as pl
from jax.experimental.pallas import tpu as pltpu
from jax.sharding import Mesh, PartitionSpec as P

HEAD = 128
NS = 256
CONV = 4
EPS = 1e-05
ROPE_BASE = 100000000000.0
BF = jnp.bfloat16
F32 = jnp.float32
VMEM = pl.BlockSpec(memory_space=pltpu.VMEM)
SMEM = pl.BlockSpec(memory_space=pltpu.SMEM)


def grant(mebibytes):
    return pltpu.CompilerParams(vmem_limit_bytes=mebibytes << 20)


def dot(left, right):
    return jnp.dot(left, right, preferred_element_type=F32)


def contract(form, left, right):
    return jnp.einsum(form, left, right, preferred_element_type=F32)


def silu_slope(values):
    sigma = jax.nn.sigmoid(values)
    return sigma * (1.0 + values * (1.0 - sigma))


def after(v, *earlier):
    return lax.optimization_barrier((v, earlier))[0]


def norm_rows(values, gain):
    scale = lax.rsqrt(jnp.mean(values * values, axis=-1, keepdims=True) + EPS)
    return values * scale * gain, scale


def norm_rows_back(values, gain, scale, grad):
    normal = values * scale
    weighted = grad * gain
    back = scale * (weighted - normal * jnp.mean(weighted * normal, axis=-1, keepdims=True))
    return back, jnp.sum(grad * normal, axis=0)


def swap_c(v):
    return lax.ppermute(v, "c", [(0, 1), (1, 0)])


def swap_x(v):
    return lax.ppermute(v, "x", [(0, 1), (1, 0)])


def swap_t(v):
    return lax.ppermute(v, "t", [(0, 1), (1, 0)])


def swap_xt(v):
    return lax.ppermute(v, ("x", "t"), [(0, 3), (1, 2), (2, 1), (3, 0)])


def swap_xc(v):
    return lax.ppermute(v, ("x", "c"), [(0, 3), (1, 2), (2, 1), (3, 0)])


def pair(mine, other, index, axis):
    return jnp.where(
        index == 0, jnp.stack([mine, other], axis=axis), jnp.stack([other, mine], axis=axis)
    )


def spread_xc(v, xi, ci):
    v = pair(v, swap_x(v), xi, 0)
    return pair(v, swap_c(v), ci, 1)


def order_t(mine, other, ti, axis=0):
    return jnp.where(
        ti == 0,
        jnp.concatenate([mine, other], axis=axis),
        jnp.concatenate([other, mine], axis=axis),
    )


def act_gather(v, ti, *earlier):
    rows, n = v.shape
    got = (swap_t(v), swap_x(v), swap_xt(v))
    if earlier:
        v = after(v, *earlier)
    near = pl.pallas_call(
        place_pair,
        in_specs=[SMEM] + [VMEM] * 4,
        out_specs=VMEM,
        out_shape=jax.ShapeDtypeStruct((4 * rows, n), v.dtype),
        compiler_params=grant(8),
    )(ti.reshape(1), v, *got)
    return near, swap_c(near)


def z_gather(v):
    return lax.all_gather(v, "z", axis=0, tiled=True)


def z_scatter(v):
    return lax.psum_scatter(v, "z", scatter_dimension=0, tiled=True)


def z_gather_first(v, depth):
    if depth != 4:
        return (lax.all_gather(v, "z", axis=0, tiled=False),)
    return (
        lax.ppermute(v, "z", [(0, 2), (1, 3), (2, 0), (3, 1)]),
        lax.ppermute(v, "z", [(0, 1), (1, 2), (2, 3)]),
        lax.ppermute(v, "z", [(1, 0), (2, 1), (3, 2)]),
    )


def z_gather_rel(v, got, zi, depth):
    if depth != 4:
        return jnp.roll(got[0], -zi, axis=0)
    two, below, above = got
    last = lax.ppermute(two, "z", [(2, 3), (1, 0)])
    return jnp.stack([v, jnp.where(zi == 3, last, above), two, jnp.where(zi == 0, last, below)])


def sum_z(v, depth):
    if depth != 4:
        return lax.psum(v, "z")
    one = lax.ppermute(v, "z", [(0, 1), (1, 0), (2, 3), (3, 2)])
    two = lax.ppermute(v, "z", [(0, 2), (2, 0), (1, 3), (3, 1)])
    three = lax.ppermute(v, "z", [(0, 3), (3, 0), (1, 2), (2, 1)])
    return (v + one) + (two + three)


def sum_all(v, depth, *earlier):
    v = v + swap_c(v)
    v = (v + swap_t(v)) + (swap_x(v) + swap_xt(v))
    v = after(v, *earlier)
    return sum_z(v, depth)


def sum_group(v):
    v = v + jnp.roll(swap_c(v), 2, axis=0)
    far = swap_x(v) + swap_xt(v)
    return (v + swap_t(v)) + jnp.stack([far[1], far[0], far[3], far[2]])


HIGH = lax.Precision.HIGHEST


def mm(left, right):
    return lax.dot_general(left, right, (((1,), (0,)), ((), ())), preferred_element_type=F32)


def mm_rt(left, right):
    return lax.dot_general(left, right, (((1,), (1,)), ((), ())), preferred_element_type=F32)


def mm_lt(left, right):
    return lax.dot_general(left, right, (((0,), (0,)), ((), ())), preferred_element_type=F32)


def mm_exact(left, right):
    return lax.dot_general(
        left, right, (((1,), (0,)), ((), ())), precision=HIGH, preferred_element_type=F32
    )


def sigmoid(v):
    return 1.0 / (1.0 + jnp.exp(-v))


def tap_masks(seg_col, rows):
    at = lax.broadcasted_iota(jnp.int32, (rows, HEAD), 0)
    masks = [None]
    for offset in range(1, CONV):
        same = (pltpu.roll(seg_col, offset, 0) == seg_col) & (at >= offset)
        masks.append(jnp.where(same, 1.0, 0.0)[:, :1])
    return masks


def filter_rows(values, taps, masks):
    total = taps[CONV : CONV + 1] + taps[0:1] * values
    for offset in range(1, CONV):
        total = total + taps[offset : offset + 1] * (pltpu.roll(values, offset, 0) * masks[offset])
    return total


def filter_rows_back(values, taps, masks, grad):
    rows = values.shape[0]
    tap_grads = [jnp.sum(grad * values, axis=0, keepdims=True)]
    back = taps[0:1] * grad
    for offset in range(1, CONV):
        masked = grad * masks[offset]
        tap_grads.append(
            jnp.sum(masked * pltpu.roll(values, offset, 0), axis=0, keepdims=True)
        )
        back = back + taps[offset : offset + 1] * pltpu.roll(masked, rows - offset, 0)
    tap_grads.append(jnp.sum(grad, axis=0, keepdims=True))
    return back, tap_grads


def causal_of(seg_col, seg_row, rows):
    down = lax.broadcasted_iota(jnp.int32, (rows, rows), 0)
    across = lax.broadcasted_iota(jnp.int32, (rows, rows), 1)
    wide = jnp.broadcast_to(seg_col[:, :1], (rows, rows))
    return (wide == seg_row[0:1]) & (across <= down)


def wide_steps(step_cols, pick_ref, head_ref, rows):
    raw = mm_exact(step_cols, pick_ref[...]) + head_ref[1:2]
    step = jnp.maximum(raw, 0.0) + jnp.log1p(jnp.exp(-jnp.abs(raw)))
    rate = head_ref[0:1] * step
    down = lax.broadcasted_iota(jnp.int32, (rows, rows), 0)
    across = lax.broadcasted_iota(jnp.int32, (rows, rows), 1)
    lower = jnp.where(across <= down, 1.0, 0.0)
    return raw, step, rate, mm_exact(lower, rate)


def decay_of(level, h, causal, rows):
    part = level[:, h * HEAD : (h + 1) * HEAD]
    across = jnp.transpose(part)[0:1]
    diff = jnp.broadcast_to(part[:, :1], (rows, rows)) - across
    return jnp.where(causal, jnp.exp(jnp.where(causal, diff, 0.0)), 0.0)


def rope(v, cosine, sine):
    return v * cosine + pltpu.roll(v, HEAD // 2, 1) * sine


def mixer_forward(heads, mix_ref, row_ref, seg_ref, seg_row_ref, taps_ref, staps_ref, pick_ref,
                  head_ref, cos_ref, sin_ref, gated_ref, square_ref, attended_ref):
    rows = mix_ref.shape[0]
    chans = heads * HEAD
    seg_col, seg_row = seg_ref[...], seg_row_ref[0]
    causal = causal_of(seg_col, seg_row, rows)
    masks = tap_masks(seg_col, rows)
    gate = mix_ref[:, :chans]
    pre = filter_rows(mix_ref[:, chans : 2 * chans], taps_ref[...], masks)
    filtered = pre * sigmoid(pre)
    spre = filter_rows(row_ref[:, : 2 * NS], staps_ref[...], masks)
    sact = (spre * sigmoid(spre)).astype(BF)
    affinity = mm_rt(sact[:, NS:], sact[:, :NS])
    _, step, _, level = wide_steps(row_ref[:, 2 * NS + 2 * HEAD :], pick_ref, head_ref, rows)
    inner = (filtered * step).astype(BF)
    gate_act = gate * sigmoid(gate)
    squares = jnp.zeros((rows, 1), F32)
    for h in range(heads):
        at = slice(h * HEAD, (h + 1) * HEAD)
        mixing = (affinity * decay_of(level, h, causal, rows)).astype(BF)
        scanned = mm(mixing, inner[:, at])
        gated = (scanned + head_ref[2:3, at] * filtered[:, at]) * gate_act[:, at]
        gated_ref[:, at] = gated
        squares = squares + jnp.sum(gated * gated, axis=1, keepdims=True)
    square_ref[0] = jnp.transpose(jnp.broadcast_to(squares, (rows, HEAD)))[:8]
    cosine, sine = cos_ref[...], sin_ref[...]
    query = rope(mix_ref[:, 2 * chans :], cosine, sine).astype(BF)
    keys = rope(row_ref[:, 2 * NS : 2 * NS + HEAD], cosine, sine).astype(BF)
    values = row_ref[:, 2 * NS + HEAD : 2 * NS + 2 * HEAD].astype(BF)
    scores = jnp.where(causal, mm_rt(query, keys) * (HEAD ** -0.5), -1e30)
    raised = jnp.exp(scores - jnp.max(scores, axis=1, keepdims=True))
    shares = (raised / jnp.sum(raised, axis=1, keepdims=True)).astype(BF)
    attended_ref[...] = mm(shares, values).astype(BF)


def mixer_backward(heads, total_chans, mix_ref, row_ref, seg_ref, seg_row_ref, taps_ref, staps_ref,
                   pick_ref, head_ref, cos_ref, sin_ref, slot_ref, grad_ref, gated_ref, scale_ref,
                   gain_ref, sum_ref, mix_low_ref, row_low_ref, small_ref, staps_out_ref):
    rows = mix_ref.shape[0]
    chans = heads * HEAD
    seg_col, seg_row = seg_ref[...], seg_row_ref[0]
    causal = causal_of(seg_col, seg_row, rows)
    masks = tap_masks(seg_col, rows)
    gate = mix_ref[:, :chans]
    filter_input = mix_ref[:, chans : 2 * chans]
    taps, staps = taps_ref[...], staps_ref[...]
    pre = filter_rows(filter_input, taps, masks)
    sig = sigmoid(pre)
    filtered = pre * sig
    state_raw = row_ref[:, : 2 * NS]
    spre = filter_rows(state_raw, staps, masks)
    ssig = sigmoid(spre)
    sact = (spre * ssig).astype(BF)
    affinity = mm_rt(sact[:, NS:], sact[:, :NS])
    raw, step, rate, level = wide_steps(row_ref[:, 2 * NS + 2 * HEAD :], pick_ref, head_ref, rows)
    inner = (filtered * step).astype(BF)
    gsig = sigmoid(gate)
    gate_act = gate * gsig
    norm_grad = grad_ref[:, :chans]
    scale = jnp.transpose(scale_ref[0])[:, :1]
    normal = gated_ref[...] * scale
    mean = jnp.transpose(sum_ref[0])[:, :1] * (1.0 / total_chans)
    gated_grad = scale * (norm_grad * gain_ref[0:1] - normal * mean)
    mix_state_grad = gated_grad * gate_act
    scanned_low = mix_state_grad.astype(BF)
    skip = head_ref[2:3]
    state_mix, inner_grads, level_grads, step_sums = [], [], [], []
    affinity_grad = jnp.zeros((rows, rows), F32)
    for h in range(heads):
        at = slice(h * HEAD, (h + 1) * HEAD)
        decay = decay_of(level, h, causal, rows)
        mixing_full = affinity * decay
        mixing = mixing_full.astype(BF)
        state_mix.append(mm(mixing, inner[:, at]) + skip[:, at] * filtered[:, at])
        mixing_grad = mm_rt(scanned_low[:, at], inner[:, at])
        inner_grad = mm_lt(mixing, scanned_low[:, at])
        flow = mixing_grad * mixing_full
        change = jnp.sum(flow - jnp.transpose(flow), axis=1, keepdims=True)
        level_grads.append(jnp.broadcast_to(change, (rows, HEAD)))
        affinity_grad = affinity_grad + mixing_grad * decay
        inner_grads.append(inner_grad)
        reach = jnp.sum(inner_grad * filtered[:, at], axis=1, keepdims=True)
        step_sums.append(jnp.broadcast_to(reach, (rows, HEAD)))
    state_mix = jnp.concatenate(state_mix, axis=1)
    inner_grad = jnp.concatenate(inner_grads, axis=1)
    mix_low_ref[:, :chans] = (
        gated_grad * state_mix * (gsig * (1.0 + gate * (1.0 - gsig)))
    ).astype(BF)
    down = lax.broadcasted_iota(jnp.int32, (rows, rows), 0)
    across = lax.broadcasted_iota(jnp.int32, (rows, rows), 1)
    upper = jnp.where(across >= down, 1.0, 0.0)
    rate_grad = mm_exact(upper, jnp.concatenate(level_grads, axis=1))
    step_grad = rate_grad * head_ref[0:1] + jnp.concatenate(step_sums, axis=1)
    step_pre_grad = step_grad * sigmoid(raw)
    filtered_grad = skip * mix_state_grad + inner_grad * step
    input_grad, tap_grads = filter_rows_back(
        filter_input, taps, masks, filtered_grad * (sig * (1.0 + pre * (1.0 - sig)))
    )
    mix_low_ref[:, chans : 2 * chans] = input_grad.astype(BF)
    extra = [
        jnp.sum(norm_grad * normal, axis=0, keepdims=True),
        jnp.sum(mix_state_grad * filtered, axis=0, keepdims=True),
        jnp.sum(rate_grad * rate, axis=0, keepdims=True),
        jnp.sum(step_pre_grad, axis=0, keepdims=True),
    ]
    small_ref[0] = jnp.zeros(small_ref.shape[1:], F32)
    for i, v in enumerate(tap_grads + extra):
        small_ref[0, i : i + 1] = v
    low = affinity_grad.astype(BF)
    read_grad = mm(low, sact[:, :NS])
    write_grad = mm_lt(low, sact[:, NS:])
    act_grad = jnp.concatenate([write_grad, read_grad], axis=1)
    state_grad, stap_grads = filter_rows_back(
        state_raw, staps, masks, act_grad * (ssig * (1.0 + spre * (1.0 - ssig)))
    )
    row_low_ref[:, : 2 * NS] = state_grad.astype(BF)
    staps_out_ref[0] = jnp.zeros(staps_out_ref.shape[1:], F32)
    for i, v in enumerate(stap_grads):
        staps_out_ref[0, i : i + 1] = v
    cosine, sine = cos_ref[...], sin_ref[...]
    query = rope(mix_ref[:, 2 * chans :], cosine, sine).astype(BF)
    keys = rope(row_ref[:, 2 * NS : 2 * NS + HEAD], cosine, sine).astype(BF)
    values = row_ref[:, 2 * NS + HEAD : 2 * NS + 2 * HEAD].astype(BF)
    root = HEAD ** -0.5
    scores = jnp.where(causal, mm_rt(query, keys) * root, -1e30)
    raised = jnp.exp(scores - jnp.max(scores, axis=1, keepdims=True))
    shares = raised / jnp.sum(raised, axis=1, keepdims=True)
    attend_grad = grad_ref[:, chans:].astype(BF)
    values_grad = mm_lt(shares.astype(BF), attend_grad)
    shares_grad = mm_rt(attend_grad, values)
    scores_low = (
        shares * (shares_grad - jnp.sum(shares_grad * shares, axis=1, keepdims=True))
    ).astype(BF)
    query_grad = mm(scores_low, keys) * root
    keys_grad = mm_lt(scores_low, query) * root
    mix_low_ref[:, 2 * chans :] = rope(query_grad, cosine, -sine).astype(BF)
    at = 2 * NS
    row_low_ref[:, at : at + HEAD] = rope(keys_grad, cosine, -sine).astype(BF)
    row_low_ref[:, at + HEAD : at + 2 * HEAD] = values_grad.astype(BF)
    row_low_ref[:, at + 2 * HEAD :] = mm(step_pre_grad.astype(BF), slot_ref[...]).astype(BF)


def over_groups(kernel, groups, rows, args, whole, outs):
    def spec(shape):
        if len(shape) == 3:
            return pl.BlockSpec((1,) + shape[1:], lambda g: (g, 0, 0))
        return pl.BlockSpec((rows, shape[1]), lambda g: (g, 0))

    def fixed(shape):
        return pl.BlockSpec(shape, lambda g: (0, 0))

    specs = [
        fixed(v.shape) if w else spec(v.shape) for v, w in zip(args, whole)
    ]
    return pl.pallas_call(
        kernel,
        grid=(groups,),
        in_specs=specs,
        out_specs=[spec(o.shape) for o in outs],
        out_shape=outs,
        compiler_params=grant(24),
    )(*args)


def place_pair(ti_ref, own_ref, t_ref, x_ref, xt_ref, out_ref):
    rows = own_ref.shape[0]
    at = ti_ref[0]
    for i, ref in ((at, own_ref), (1 - at, t_ref), (2 + at, x_ref), (3 - at, xt_ref)):
        out_ref[pl.ds(pl.multiple_of(i * rows, rows), rows)] = ref[...]


def place_rows(at_ref, own_ref, x_ref, c_ref, xc_ref, out_ref, small_ref):
    z, me = at_ref[0], at_ref[1]
    depth, rows = out_ref.shape[0], out_ref.shape[2]
    for k in range(depth):
        to = lax.rem(z + k, depth)
        for offset, src in ((0, own_ref), (2, x_ref), (1, c_ref), (3, xc_ref)):
            out_ref[to, me ^ offset] = src[k, :rows]
            small_ref[to, me ^ offset] = src[k, rows:]


def times(rows, w):
    return tuple(dot(r, w) for r in rows)


def grads(left, right):
    near, far = (contract("tc,tk->ck", a, b) for a, b in zip(left, right))
    return (near + far).astype(BF)


def split_kernel(ti_ref, total_ref, got_ref, mine_ref, t_ref, x_ref, xt_ref):
    rows = mine_ref.shape[0]
    at = ti_ref[0]

    def part(i):
        where = pl.ds(pl.multiple_of(i * rows, rows), rows)
        return total_ref[where] + got_ref[where].astype(F32)

    mine_ref[...] = part(at)
    t_ref[...] = part(1 - at).astype(BF)
    x_ref[...] = part(2 + at).astype(BF)
    xt_ref[...] = part(3 - at).astype(BF)


def split_rows(keep, send, ti):
    got = swap_c(send.astype(BF))
    count, width = keep.shape
    rows, tile = count // 4, 512
    part = pl.BlockSpec((rows, tile), lambda j: (0, j))
    full = pl.BlockSpec((count, tile), lambda j: (0, j))
    return pl.pallas_call(
        split_kernel,
        grid=(width // tile,),
        in_specs=[SMEM, full, full],
        out_specs=[part] * 4,
        out_shape=[jax.ShapeDtypeStruct((rows, width), F32)]
        + [jax.ShapeDtypeStruct((rows, width), BF)] * 3,
        compiler_params=grant(8),
    )(ti.reshape(1), keep, got)


def join_rows(mine, to_t, to_x, to_xt, earlier=()):
    got = (swap_t(to_t), swap_x(to_x), swap_xt(to_xt))
    if earlier:
        mine = after(mine, *earlier)
    return mine + got[0].astype(F32) + got[1].astype(F32) + got[2].astype(F32)


def split_back(terms, ti):
    keep, send = (sum(contract("tk,ck->tc", a[i], w) for a, w in terms) for i in (0, 1))
    return split_rows(keep, send, ti)


def times_back(terms, ti):
    return join_rows(*split_back(terms, ti))


def turned(block):
    return jnp.transpose(block.astype(F32)).astype(BF)


def prepare_kernel(plan, xi_ref, *refs):
    sources, keep_ref, send_ref = refs[:-2], refs[-2], refs[-1]
    first = xi_ref[0] == 0
    for c in range(2):
        at = 0
        for ref, is_turned in zip(sources, plan):
            if is_turned:
                n = ref.shape[0] // 4
                low, high = (turned(ref[(x * 2 + c) * n : (x * 2 + c + 1) * n]) for x in range(2))
            else:
                n = ref.shape[1] // 4
                low, high = (ref[:, (x * 2 + c) * n : (x * 2 + c + 1) * n] for x in range(2))
            keep_ref[c, :, at : at + n] = jnp.where(first, low, high)
            send_ref[c, :, at : at + n] = jnp.where(first, high, low)
            at += n


def middle_kernel(ci_ref, keep_ref, got_ref, keep_out, send_out):
    c = ci_ref[0]
    for i, ref in enumerate((keep_ref, got_ref)):
        keep_out[i] = ref[c]
        send_out[i] = ref[1 - c]


def end_kernel(at_ref, keep_ref, got_ref, out_ref):
    x, c = at_ref[0], at_ref[1]
    for i, ref in enumerate((keep_ref, got_ref)):
        out_ref[x, c ^ i] = ref[0]
        out_ref[1 - x, c ^ i] = ref[1]


def simple(kernel, args, outs, scalars=1, grant_of=8):
    single = not isinstance(outs, list)
    return pl.pallas_call(
        kernel,
        in_specs=[SMEM] * scalars + [VMEM] * (len(args) - scalars),
        out_specs=VMEM if single else [VMEM] * len(outs),
        out_shape=outs,
        compiler_params=grant(grant_of),
    )(*args)


def middle(keep, send, xi, ci):
    shape = jax.ShapeDtypeStruct(keep.shape, BF)
    keep, send = simple(middle_kernel, (ci.reshape(1), keep, swap_x(send)), [shape, shape])
    return keep, swap_c(send)


def prepare(sources, plan, xi):
    rows = [s.shape[1] if t else s.shape[0] for s, t in zip(sources, plan)][0]
    wide = sum((s.shape[0] if t else s.shape[1]) // 4 for s, t in zip(sources, plan))
    shape = jax.ShapeDtypeStruct((2, rows, wide), BF)
    return simple(
        functools.partial(prepare_kernel, plan), (xi.reshape(1), *sources), [shape, shape]
    )


def deal_out(keep, send, xi, ci):
    keep, got = middle(keep, send, xi, ci)
    out = jax.ShapeDtypeStruct((2,) + keep.shape, BF)
    return simple(end_kernel, (jnp.stack([xi, ci]), keep, got), out).reshape(
        -1, keep.shape[-1]
    )


def start_kernel(xi_ref, *refs):
    keep_ref, send_ref = refs[-2:]
    x, at = xi_ref[0], 0
    for ref in refs[:-2]:
        n = ref.shape[-1]
        keep_ref[:, :, at : at + n] = ref[x]
        send_ref[:, :, at : at + n] = ref[1 - x]
        at += n


def finish_kernel(plan, at_ref, keep_ref, got_ref, *outs):
    x, c = at_ref[0], at_ref[1]
    for q in range(4):
        own = c == q % 2
        offset = x ^ (q // 2)
        at = 0
        for ref, kind in zip(outs, plan):
            n = (ref.shape[0] if kind == "turned" else ref.shape[-1]) // 4
            for i in range(2 if kind == "two" else 1):
                block = jnp.where(
                    own, keep_ref[offset, :, at : at + n], got_ref[offset, :, at : at + n]
                ).astype(F32)
                if kind == "turned":
                    ref[q * n : (q + 1) * n] = jnp.transpose(block)
                elif kind == "two":
                    ref[:, i, q * n : (q + 1) * n] = block
                else:
                    ref[:, q * n : (q + 1) * n] = block
                at += n


def deal_start(summed, xi):
    shard = summed[0].shape[0] // 4
    blocks = [v.reshape(2, 2, shard, -1) for v in summed]
    shape = jax.ShapeDtypeStruct((2, shard, sum(v.shape[-1] for v in blocks)), BF)
    return simple(start_kernel, (xi.reshape(1), *blocks), [shape, shape])


def deal_middle(keep, send, ci):
    shape = jax.ShapeDtypeStruct(keep.shape, BF)
    return simple(middle_kernel, (ci.reshape(1), keep, swap_x(send)), [shape, shape])


def deal_finish(keep, send, plan, widths, xi, ci):
    shard = keep.shape[1]
    shapes = {"turned": lambda n: (4 * n, shard), "two": lambda n: (shard, 2, 4 * n)}
    outs = [
        jax.ShapeDtypeStruct(shapes.get(k, lambda n: (shard, 4 * n))(n), F32)
        for n, k in zip(widths, plan)
    ]
    return simple(
        functools.partial(finish_kernel, plan),
        (jnp.stack([xi, ci]), keep, swap_c(send)),
        outs,
    )


def row_first_kernel(ci_ref, part_ref, keep_ref, send_ref):
    c = ci_ref[0]
    for k in range(part_ref.shape[0]):
        for x in range(2):
            keep_ref[x, k] = part_ref[k, x, c]
            send_ref[x, k] = part_ref[k, x, 1 - c]


def row_second_kernel(xi_ref, keep_ref, got_ref, keep_out, send_out):
    x = xi_ref[0]
    keep_out[...] = keep_ref[x].astype(F32) + got_ref[x].astype(F32)
    send_out[...] = (keep_ref[1 - x].astype(F32) + got_ref[1 - x].astype(F32)).astype(BF)


def on_device(
    depth,
    tokens,
    segments,
    cotangent,
    first_gain,
    mixer_in,
    state_weight,
    step_weight,
    filter_taps,
    state_taps,
    decay_log,
    step_bias,
    skip_gain,
    gate_gain,
    mixer_out,
    query_weight,
    key_value_matrix,
    attend_out,
    second_gain,
    gate_up,
    down_weight,
):
    zi, xi = lax.axis_index("z"), lax.axis_index("x")
    ci, ti = lax.axis_index("c"), lax.axis_index("t")
    me = xi * 2 + ci
    rows, width = tokens.shape
    group = segments.shape[0]
    shard = mixer_in.shape[0]
    block = 4 * shard
    heads_in = decay_log.shape[0]
    heads = heads_in // 4
    chans = heads * HEAD
    total_chans = 2 * heads_in * HEAD
    ffn = gate_up.shape[2] // 4
    count = 4 * group
    scale = HEAD ** (-0.5)

    pieces = [first_gain, second_gain, filter_taps, state_taps, gate_gain, segments]
    sizes = [p.size for p in pieces]
    step_pad = jnp.pad(step_weight, ((0, 0), (0, 128 - heads_in)))
    row_pack = jnp.concatenate(
        [state_weight, key_value_matrix.reshape(shard, -1), step_pad], axis=1
    )
    row_wide = row_pack.shape[1]
    vec = jnp.concatenate([p.astype(BF).reshape(-1) for p in pieces])
    vec = jnp.pad(vec, (0, 16 * row_wide - vec.size)).reshape(16, row_wide)
    row_own = jnp.concatenate([row_pack, vec])
    row_got = z_gather_first(row_own, depth)

    first_plan = (True, True, False, False, False)
    first_keep, first_send = prepare(
        (mixer_out, attend_out, mixer_in[:, 0], mixer_in[:, 1], query_weight), first_plan, xi
    )
    first_keep = after(first_keep, *row_got)
    first_mine = deal_out(first_keep, first_send, xi, ci)
    wide = chans + HEAD

    row_z = z_gather_rel(row_own, row_got, zi, depth)
    first_w = z_gather(first_mine)
    row_x = swap_x(row_z)
    row_full, small = simple(
        place_rows,
        (jnp.stack([zi, me]), row_z, row_x, swap_c(row_z), swap_c(row_x)),
        [
            jax.ShapeDtypeStruct((depth, 4, shard, row_wide), BF),
            jax.ShapeDtypeStruct((depth, 4, 16, row_wide), BF),
        ],
        grant_of=16,
    )
    row_full = row_full.reshape(width, row_wide)
    kv_at = 2 * NS
    state_full = row_full[:, :kv_at]
    small = small.reshape(depth, 4, -1)
    offsets = [sum(sizes[:i]) for i in range(6)]
    cut = [small[:, :, at : at + size] for at, size in zip(offsets, sizes)]
    seg_all = lax.dynamic_index_in_dim(cut[5], zi, 0, keepdims=False).astype(F32)
    segs = jnp.stack(
        [lax.dynamic_index_in_dim(seg_all, me ^ k, 0, keepdims=False) for k in (0, 2, 1, 3)]
    )
    first_full = cut[0].reshape(-1).astype(F32)
    second_full = cut[1].reshape(-1).astype(F32)
    eighth = filter_taps.shape[2]
    taps_all = jnp.transpose(
        cut[2].reshape(depth, 4, CONV + 1, heads_in, eighth), (2, 3, 0, 1, 4)
    ).reshape(CONV + 1, 4, chans)
    taps = lax.dynamic_index_in_dim(taps_all, me, 1, keepdims=False).astype(F32)
    staps = (
        jnp.transpose(cut[3].reshape(depth, 4, CONV + 1, -1), (2, 0, 1, 3))
        .reshape(CONV + 1, 2 * NS)
        .astype(F32)
    )
    gate_all = jnp.transpose(
        cut[4].reshape(depth, 4, heads_in, eighth), (2, 0, 1, 3)
    ).reshape(4, chans)
    gate_gain_mine = lax.dynamic_index_in_dim(gate_all, me, 0, keepdims=False).astype(F32)

    order = jnp.arange(group)
    live_all = (segs >= 0).astype(F32)
    same = (segs[:, :, None] == segs[:, None, :]) & (order[None, None, :] <= order[None, :, None])
    position = jnp.sum(same.astype(F32), axis=2) - 1.0
    half = HEAD // 2
    frequency = ROPE_BASE ** (-2.0 * jnp.arange(half).astype(F32) / HEAD)
    angle = position.reshape(count, 1) * frequency[None, :]
    cosine, sine = jnp.cos(angle), jnp.sin(angle)
    cosine = jnp.concatenate([cosine, cosine], axis=1)
    sine = jnp.concatenate([-sine, sine], axis=1)
    live_mine = lax.dynamic_slice_in_dim(
        (segments >= 0).astype(F32), ti * rows, rows
    )[:, None]
    seg_cols = jnp.broadcast_to(segs.reshape(count, 1), (count, HEAD))
    seg_rows = jnp.broadcast_to(segs[:, None, :], (4, 8, group))

    def halves(v):
        n = v.shape[0] // 2
        return v[:n], v[n:]

    my_log = lax.dynamic_slice_in_dim(decay_log, me * heads, heads)
    my_bias = lax.dynamic_slice_in_dim(step_bias, me * heads, heads)
    my_skip = lax.dynamic_slice_in_dim(skip_gain, me * heads, heads)
    head_rows = jnp.pad(
        jnp.repeat(jnp.stack([-jnp.exp(my_log), my_bias, my_skip]), HEAD, axis=1), ((0, 5), (0, 0))
    )
    lane_head = me * heads + jnp.arange(chans) // HEAD
    picker = (jnp.arange(128)[:, None] == lane_head[None, :]).astype(F32)
    first_lane = (jnp.arange(chans) % HEAD == 0)[:, None]
    slots = ((jnp.arange(128)[None, :] == lane_head[:, None]) & first_lane).astype(BF)
    taps_pad = jnp.pad(taps, ((0, 3), (0, 0)))
    staps_pad = jnp.pad(staps, ((0, 3), (0, 0)))
    gain_pad = jnp.pad(gate_gain_mine[None], ((0, 7), (0, 0)))

    resid = tokens.astype(F32)
    normed_input, scale_one = norm_rows(resid, first_full)
    normed_low = normed_input.astype(BF)
    normed = act_gather(normed_low, ti)
    then_plan = (False, False, True)
    then_keep, then_send = prepare(
        (gate_up[:, 0], gate_up[:, 1], down_weight), then_plan, xi
    )
    then_send = after(then_send, normed[0], row_x)
    then_mine = deal_out(then_keep, then_send, xi, ci)
    then_w = z_gather(then_mine)
    grad_out = cotangent.astype(F32)
    feed_low = after((live_mine * grad_out).astype(BF), then_mine)
    row_out = times(normed, row_full)
    first_w = after(first_w, row_out)
    out_w, mix_w = first_w[:, :wide], first_w[:, wide:]
    mix_out = times(normed, mix_w)
    feed_grad = act_gather(feed_low, ti, *mix_out)

    per_half = list(
        zip(mix_out, row_out, halves(seg_cols), halves(seg_rows), halves(cosine), halves(sine))
    )
    near_far, whole = [], (False,) * 4 + (True,) * 4 + (False,) * 2
    for m, r, sc, sr, co, si in per_half:
        near_far.append((m, r, sc, sr, taps_pad, staps_pad, picker, head_rows, co, si))
    ahead = [
        over_groups(
            functools.partial(mixer_forward, heads),
            2,
            group,
            common,
            whole,
            [
                jax.ShapeDtypeStruct((count // 2, chans), F32),
                jax.ShapeDtypeStruct((2, 8, group), F32),
                jax.ShapeDtypeStruct((count // 2, HEAD), BF),
            ],
        )
        for common in near_far
    ]
    squares = jnp.concatenate([ahead[0][1], ahead[1][1]])
    gate_scale = halves(lax.rsqrt(sum_group(squares) / total_chans + EPS))
    gate_normal = [
        a[0] * g[:, 0].reshape(count // 2, 1) for a, g in zip(ahead, gate_scale)
    ]

    out_w = after(out_w, feed_grad)
    branch = [
        jnp.concatenate([(n * gate_gain_mine).astype(BF), a[2]], axis=1)
        for n, a in zip(gate_normal, ahead)
    ]
    hidden = resid + live_mine * times_back([(branch, out_w)], ti)
    second, scale_two = norm_rows(hidden, second_full)

    second_all = act_gather(second.astype(BF), ti)
    gu_w, down_w = then_w[:, : 2 * ffn], then_w[:, 2 * ffn :]
    gate_up_out = times(second_all, gu_w)
    activation = [(jax.nn.silu(v[:, :ffn]) * v[:, ffn:]).astype(BF) for v in gate_up_out]
    down_term = grads(feed_grad, activation)
    down_w = after(down_w, down_term)
    gu_low = []
    for v, feed_half in zip(gate_up_out, feed_grad):
        gate_part, up_part = v[:, :ffn], v[:, ffn:]
        act_grad = dot(feed_half, down_w)
        gu_low.append(
            jnp.concatenate(
                [
                    act_grad * up_part * silu_slope(gate_part),
                    act_grad * jax.nn.silu(gate_part),
                ],
                axis=1,
            ).astype(BF)
        )
    down_sum = z_scatter(down_term)
    gu_sum = z_scatter(grads(second_all, gu_low))
    second_split = split_back([(gu_low, gu_w)], ti)
    second_grad = join_rows(*second_split)
    feed_split = split_back([(after(activation, second_split), down_w)], ti)
    hidden_part, second_gain_grad = norm_rows_back(hidden, second_full, scale_two, second_grad)
    hidden_grad = grad_out + hidden_part
    mix_low_rows = after((live_mine * hidden_grad).astype(BF), feed_split, down_sum)
    mix_grad = act_gather(mix_low_rows, ti)
    branch_grad = times(mix_grad, out_w)
    out_term = grads(mix_grad, branch)
    out_sum = z_scatter(out_term)

    inner_sum = jnp.concatenate(
        [
            jnp.sum(b[:, :chans] * gate_gain_mine * n, axis=-1).reshape(2, 1, group)
            for b, n in zip(branch_grad, gate_normal)
        ]
    )
    inner_sum = sum_group(jnp.broadcast_to(inner_sum, (4, 8, group)))
    inner_sum = after(inner_sum, out_term)
    feed_split = after(feed_split, inner_sum)
    output = (hidden + live_mine * join_rows(*feed_split)).astype(BF)
    inner_sum = halves(inner_sum)
    inner_sum = (inner_sum[0], after(inner_sum[1], gu_sum))
    back = [
        over_groups(
            functools.partial(mixer_backward, heads, total_chans),
            2,
            group,
            common + (slots, branch_grad[i], ahead[i][0], gate_scale[i], gain_pad, inner_sum[i]),
            whole + (True, False, False, False, True, False),
            [
                jax.ShapeDtypeStruct((count // 2, 2 * chans + HEAD), BF),
                jax.ShapeDtypeStruct((count // 2, row_wide), BF),
                jax.ShapeDtypeStruct((2, 16, chans), F32),
                jax.ShapeDtypeStruct((2, 8, 2 * NS), F32),
            ],
        )
        for i, common in enumerate(near_far)
    ]
    mix_low, row_low, small_rows, small_state = zip(*back)
    then_parts = deal_start(after((down_sum, gu_sum), output), xi)
    mix_term = grads(after(normed, then_parts), mix_low)
    then_parts = deal_middle(*then_parts, ci)
    mix_sum = z_scatter(mix_term)

    small_rows = jnp.concatenate(small_rows)
    small_state = jnp.concatenate(small_state)
    state_taps_grad = jnp.sum(small_state, axis=0)[: CONV + 1]
    summed_split = split_back(
        [(after(mix_low, mix_term, then_parts), mix_w), (row_low, row_full)], ti
    )
    row_part = grads(normed, after(row_low, summed_split)).reshape(depth, 2, 2, shard, row_wide)
    shape = jax.ShapeDtypeStruct((2, depth, shard, row_wide), BF)
    keep, send = simple(row_first_kernel, (ci.reshape(1), row_part), [shape, shape], grant_of=16)
    keep, send = simple(
        row_second_kernel,
        (xi.reshape(1), keep, swap_c(send)),
        [jax.ShapeDtypeStruct(shape.shape[1:], F32), jax.ShapeDtypeStruct(shape.shape[1:], BF)],
        grant_of=16,
    )
    row_x = swap_x(send)
    down_weight_grad, gate_up_grad = deal_finish(
        *then_parts, ("turned", "two"), (ffn, ffn), xi, ci
    )
    ready = (send, down_weight_grad, gate_up_grad)
    normed_grad = join_rows(*summed_split, earlier=ready)
    out_parts = deal_middle(*deal_start((after(out_sum, normed_grad),), xi), ci)
    mixer_out_grad, attend_out_grad = deal_finish(
        *out_parts, ("turned",) * 2, (chans, HEAD), xi, ci
    )
    row_sum_xc = after(keep, normed_grad) + row_x.astype(F32)
    row_sum = z_scatter(row_sum_xc.astype(BF).reshape(depth * shard, row_wide))
    resid_part, first_gain_grad = norm_rows_back(resid, first_full, scale_one, normed_grad)
    tokens_grad = hidden_grad + resid_part

    mix_parts = deal_middle(*deal_start((mix_sum,), xi), ci)
    mixer_in_grad, query_weight_grad = deal_finish(
        *mix_parts, ("two", ""), (chans, HEAD), xi, ci
    )
    state_sum = row_sum[:, :kv_at]
    state_weight_grad = state_sum.astype(F32) + swap_t(state_sum).astype(F32)
    row_sum = row_sum.astype(F32)
    keys_values_grad = row_sum[:, kv_at : kv_at + 2 * HEAD].reshape(shard, 2, HEAD)
    step_weight_grad = row_sum[:, kv_at + 2 * HEAD : kv_at + 2 * HEAD + heads_in]

    dp_at = zi * 4 + me
    head_sum = (small_rows[0] + small_rows[1] + small_rows[2] + small_rows[3])[:9]
    slots_of = jnp.arange(8)[:, None, None] == ti * 4 + me
    head_part = jnp.where(slots_of, head_sum[None], 0.0)
    parts = [second_gain_grad, state_taps_grad.reshape(-1), first_gain_grad]
    packed = jnp.concatenate(
        [head_part.reshape(-1, 128), jnp.concatenate(parts).reshape(-1, 128)]
    )
    packed = sum_all(packed, depth, row_sum_xc)
    head_all = lax.dynamic_slice_in_dim(
        packed[: head_part.size // 128], ti * (head_part.size // 256), head_part.size // 256
    )
    packed = packed[head_part.size // 128 :].reshape(-1)
    second_mine = lax.dynamic_slice_in_dim(packed, dp_at * shard, shard)
    first_mine = lax.dynamic_slice_in_dim(
        packed[packed.size - width :], dp_at * shard, shard
    )
    state_shard = state_taps.shape[1]
    state_taps_mine = lax.dynamic_slice_in_dim(
        packed[width : packed.size - width].reshape(CONV + 1, 2 * NS),
        dp_at * state_shard,
        state_shard,
        1,
    )
    by_head = jnp.transpose(
        head_all.reshape(4, 9, heads, HEAD), (1, 0, 2, 3)
    ).reshape(9, heads_in, HEAD)
    taps_out = lax.dynamic_slice_in_dim(by_head[: CONV + 1], dp_at * eighth, eighth, 2)
    gate_out = lax.dynamic_slice_in_dim(by_head[5], dp_at * eighth, eighth, 1)
    return (
        output,
        tokens_grad,
        first_mine,
        mixer_in_grad,
        state_weight_grad,
        step_weight_grad,
        taps_out,
        state_taps_mine,
        by_head[7, :, 0],
        by_head[8, :, 0],
        jnp.sum(by_head[6], axis=1),
        gate_out,
        mixer_out_grad,
        query_weight_grad,
        keys_values_grad,
        attend_out_grad,
        second_mine,
        gate_up_grad,
        down_weight_grad,
    )


def solution(mesh):
    dp, tensor = mesh.shape["dp"], mesh.shape["tensor"]
    depth = dp // 4
    split = Mesh(mesh.devices.reshape(depth, 2, 2, tensor), ("z", "x", "c", "t"))
    D = ("z", "x", "c")
    T = "t"
    R = ("z", "x", "c", "t")
    weights = (
        P(D),
        P(D, None, T),
        P(D, None),
        P(D, T),
        P(None, T, D),
        P(None, D),
        P(T),
        P(T),
        P(T),
        P(T, D),
        P(T, D),
        P(D, T),
        P(D, None, T),
        P(T, D),
        P(D),
        P(D, None, T),
        P(T, D),
    )

    def run(*args):
        return on_device(depth, *args)

    return jax.shard_map(
        run,
        mesh=split,
        in_specs=(P(R, None), P(D), P(R, None)) + weights,
        out_specs=(P(R, None), P(R, None)) + weights,
        check_vma=False,
    )
```

```python
import functools

import jax
import jax.numpy as jnp
from jax import lax
from jax.experimental import pallas as pl
from jax.experimental.pallas import tpu as pltpu
from jax.sharding import Mesh, PartitionSpec as P

HEAD = 128
NS = 256
CONV = 4
EPS = 1e-05
ROPE_BASE = 100000000000.0
BF = jnp.bfloat16
F32 = jnp.float32
VMEM = pl.BlockSpec(memory_space=pltpu.VMEM)
SMEM = pl.BlockSpec(memory_space=pltpu.SMEM)


def grant(mebibytes):
    return pltpu.CompilerParams(vmem_limit_bytes=mebibytes << 20)


def dot(left, right):
    return jnp.dot(left, right, preferred_element_type=F32)


def contract(form, left, right):
    return jnp.einsum(form, left, right, preferred_element_type=F32)


def silu_slope(values):
    sigma = jax.nn.sigmoid(values)
    return sigma * (1.0 + values * (1.0 - sigma))


def after(v, *earlier):
    return lax.optimization_barrier((v, earlier))[0]


def norm_rows(values, gain):
    scale = lax.rsqrt(jnp.mean(values * values, axis=-1, keepdims=True) + EPS)
    return values * scale * gain, scale


def norm_rows_back(values, gain, scale, grad):
    normal = values * scale
    weighted = grad * gain
    back = scale * (weighted - normal * jnp.mean(weighted * normal, axis=-1, keepdims=True))
    return back, jnp.sum(grad * normal, axis=0)


def swap_c(v):
    return lax.ppermute(v, "c", [(0, 1), (1, 0)])


def swap_x(v):
    return lax.ppermute(v, "x", [(0, 1), (1, 0)])


def swap_t(v):
    return lax.ppermute(v, "t", [(0, 1), (1, 0)])


def swap_xt(v):
    return lax.ppermute(v, ("x", "t"), [(0, 3), (1, 2), (2, 1), (3, 0)])


def swap_xc(v):
    return lax.ppermute(v, ("x", "c"), [(0, 3), (1, 2), (2, 1), (3, 0)])


def pair(mine, other, index, axis):
    return jnp.where(
        index == 0, jnp.stack([mine, other], axis=axis), jnp.stack([other, mine], axis=axis)
    )


def spread_xc(v, xi, ci):
    v = pair(v, swap_x(v), xi, 0)
    return pair(v, swap_c(v), ci, 1)


def order_t(mine, other, ti, axis=0):
    return jnp.where(
        ti == 0,
        jnp.concatenate([mine, other], axis=axis),
        jnp.concatenate([other, mine], axis=axis),
    )


def act_gather(v, ti, *earlier):
    rows, n = v.shape
    got = (swap_t(v), swap_x(v), swap_xt(v))
    if earlier:
        v = after(v, *earlier)
    near = pl.pallas_call(
        place_pair,
        in_specs=[SMEM] + [VMEM] * 4,
        out_specs=VMEM,
        out_shape=jax.ShapeDtypeStruct((4 * rows, n), v.dtype),
        compiler_params=grant(8),
    )(ti.reshape(1), v, *got)
    return near, swap_c(near)


def z_gather(v):
    return lax.all_gather(v, "z", axis=0, tiled=True)


def z_scatter(v):
    return lax.psum_scatter(v, "z", scatter_dimension=0, tiled=True)


def z_gather_first(v, depth):
    if depth != 4:
        return (lax.all_gather(v, "z", axis=0, tiled=False),)
    return (
        lax.ppermute(v, "z", [(0, 2), (1, 3), (2, 0), (3, 1)]),
        lax.ppermute(v, "z", [(0, 1), (1, 2), (2, 3)]),
        lax.ppermute(v, "z", [(1, 0), (2, 1), (3, 2)]),
    )


def z_gather_rel(v, got, zi, depth):
    if depth != 4:
        return jnp.roll(got[0], -zi, axis=0)
    two, below, above = got
    last = lax.ppermute(two, "z", [(2, 3), (1, 0)])
    return jnp.stack([v, jnp.where(zi == 3, last, above), two, jnp.where(zi == 0, last, below)])


def sum_z(v, depth):
    if depth != 4:
        return lax.psum(v, "z")
    one = lax.ppermute(v, "z", [(0, 1), (1, 0), (2, 3), (3, 2)])
    two = lax.ppermute(v, "z", [(0, 2), (2, 0), (1, 3), (3, 1)])
    three = lax.ppermute(v, "z", [(0, 3), (3, 0), (1, 2), (2, 1)])
    return (v + one) + (two + three)


def sum_all(v, depth, *earlier):
    v = v + swap_c(v)
    got = (swap_t(v), swap_x(v), swap_xt(v))
    v = (after(v, *earlier) + got[0]) + (got[1] + got[2])
    return sum_z(v, depth)


def sum_group(v):
    v = v + jnp.roll(swap_c(v), 2, axis=0)
    far = swap_x(v) + swap_xt(v)
    return (v + swap_t(v)) + jnp.stack([far[1], far[0], far[3], far[2]])


HIGH = lax.Precision.HIGHEST


def mm(left, right):
    return lax.dot_general(left, right, (((1,), (0,)), ((), ())), preferred_element_type=F32)


def mm_rt(left, right):
    return lax.dot_general(left, right, (((1,), (1,)), ((), ())), preferred_element_type=F32)


def mm_lt(left, right):
    return lax.dot_general(left, right, (((0,), (0,)), ((), ())), preferred_element_type=F32)


def mm_exact(left, right):
    return lax.dot_general(
        left, right, (((1,), (0,)), ((), ())), precision=HIGH, preferred_element_type=F32
    )


def sigmoid(v):
    return 1.0 / (1.0 + jnp.exp(-v))


def tap_masks(seg_col, rows):
    at = lax.broadcasted_iota(jnp.int32, (rows, HEAD), 0)
    masks = [None]
    for offset in range(1, CONV):
        same = (pltpu.roll(seg_col, offset, 0) == seg_col) & (at >= offset)
        masks.append(jnp.where(same, 1.0, 0.0)[:, :1])
    return masks


def filter_rows(values, taps, masks):
    total = taps[CONV : CONV + 1] + taps[0:1] * values
    for offset in range(1, CONV):
        total = total + taps[offset : offset + 1] * (pltpu.roll(values, offset, 0) * masks[offset])
    return total


def filter_rows_back(values, taps, masks, grad):
    rows = values.shape[0]
    tap_grads = [jnp.sum(grad * values, axis=0, keepdims=True)]
    back = taps[0:1] * grad
    for offset in range(1, CONV):
        masked = grad * masks[offset]
        tap_grads.append(
            jnp.sum(masked * pltpu.roll(values, offset, 0), axis=0, keepdims=True)
        )
        back = back + taps[offset : offset + 1] * pltpu.roll(masked, rows - offset, 0)
    tap_grads.append(jnp.sum(grad, axis=0, keepdims=True))
    return back, tap_grads


def causal_of(seg_col, seg_row, rows):
    down = lax.broadcasted_iota(jnp.int32, (rows, rows), 0)
    across = lax.broadcasted_iota(jnp.int32, (rows, rows), 1)
    wide = jnp.broadcast_to(seg_col[:, :1], (rows, rows))
    return (wide == seg_row[0:1]) & (across <= down)


def wide_steps(step_cols, pick_ref, head_ref, rows):
    raw = mm_exact(step_cols, pick_ref[...]) + head_ref[1:2]
    step = jnp.maximum(raw, 0.0) + jnp.log1p(jnp.exp(-jnp.abs(raw)))
    rate = head_ref[0:1] * step
    down = lax.broadcasted_iota(jnp.int32, (rows, rows), 0)
    across = lax.broadcasted_iota(jnp.int32, (rows, rows), 1)
    lower = jnp.where(across <= down, 1.0, 0.0)
    return raw, step, rate, mm_exact(lower, rate)


def decay_of(level, h, causal, rows):
    part = level[:, h * HEAD : (h + 1) * HEAD]
    across = jnp.transpose(part)[0:1]
    diff = jnp.broadcast_to(part[:, :1], (rows, rows)) - across
    return jnp.where(causal, jnp.exp(jnp.where(causal, diff, 0.0)), 0.0)


def rope(v, cosine, sine):
    return v * cosine + pltpu.roll(v, HEAD // 2, 1) * sine


def mixer_forward(heads, mix_ref, row_ref, seg_ref, seg_row_ref, taps_ref, staps_ref, pick_ref,
                  head_ref, cos_ref, sin_ref, gated_ref, square_ref, attended_ref):
    rows = mix_ref.shape[0]
    chans = heads * HEAD
    seg_col, seg_row = seg_ref[...], seg_row_ref[0]
    causal = causal_of(seg_col, seg_row, rows)
    masks = tap_masks(seg_col, rows)
    gate = mix_ref[:, :chans]
    pre = filter_rows(mix_ref[:, chans : 2 * chans], taps_ref[...], masks)
    filtered = pre * sigmoid(pre)
    spre = filter_rows(row_ref[:, : 2 * NS], staps_ref[...], masks)
    sact = (spre * sigmoid(spre)).astype(BF)
    affinity = mm_rt(sact[:, NS:], sact[:, :NS])
    _, step, _, level = wide_steps(row_ref[:, 2 * NS + 2 * HEAD :], pick_ref, head_ref, rows)
    inner = (filtered * step).astype(BF)
    gate_act = gate * sigmoid(gate)
    squares = jnp.zeros((rows, 1), F32)
    for h in range(heads):
        at = slice(h * HEAD, (h + 1) * HEAD)
        mixing = (affinity * decay_of(level, h, causal, rows)).astype(BF)
        scanned = mm(mixing, inner[:, at])
        gated = (scanned + head_ref[2:3, at] * filtered[:, at]) * gate_act[:, at]
        gated_ref[:, at] = gated
        squares = squares + jnp.sum(gated * gated, axis=1, keepdims=True)
    square_ref[0] = jnp.transpose(jnp.broadcast_to(squares, (rows, HEAD)))[:8]
    cosine, sine = cos_ref[...], sin_ref[...]
    query = rope(mix_ref[:, 2 * chans :], cosine, sine).astype(BF)
    keys = rope(row_ref[:, 2 * NS : 2 * NS + HEAD], cosine, sine).astype(BF)
    values = row_ref[:, 2 * NS + HEAD : 2 * NS + 2 * HEAD].astype(BF)
    scores = jnp.where(causal, mm_rt(query, keys) * (HEAD ** -0.5), -1e30)
    raised = jnp.exp(scores - jnp.max(scores, axis=1, keepdims=True))
    shares = (raised / jnp.sum(raised, axis=1, keepdims=True)).astype(BF)
    attended_ref[...] = mm(shares, values).astype(BF)


def mixer_backward(heads, total_chans, mix_ref, row_ref, seg_ref, seg_row_ref, taps_ref, staps_ref,
                   pick_ref, head_ref, cos_ref, sin_ref, slot_ref, grad_ref, gated_ref, scale_ref,
                   gain_ref, sum_ref, mix_low_ref, row_low_ref, small_ref, staps_out_ref):
    rows = mix_ref.shape[0]
    chans = heads * HEAD
    seg_col, seg_row = seg_ref[...], seg_row_ref[0]
    causal = causal_of(seg_col, seg_row, rows)
    masks = tap_masks(seg_col, rows)
    gate = mix_ref[:, :chans]
    filter_input = mix_ref[:, chans : 2 * chans]
    taps, staps = taps_ref[...], staps_ref[...]
    pre = filter_rows(filter_input, taps, masks)
    sig = sigmoid(pre)
    filtered = pre * sig
    state_raw = row_ref[:, : 2 * NS]
    spre = filter_rows(state_raw, staps, masks)
    ssig = sigmoid(spre)
    sact = (spre * ssig).astype(BF)
    affinity = mm_rt(sact[:, NS:], sact[:, :NS])
    raw, step, rate, level = wide_steps(row_ref[:, 2 * NS + 2 * HEAD :], pick_ref, head_ref, rows)
    inner = (filtered * step).astype(BF)
    gsig = sigmoid(gate)
    gate_act = gate * gsig
    norm_grad = grad_ref[:, :chans]
    scale = jnp.transpose(scale_ref[0])[:, :1]
    normal = gated_ref[...] * scale
    mean = jnp.transpose(sum_ref[0])[:, :1] * (1.0 / total_chans)
    gated_grad = scale * (norm_grad * gain_ref[0:1] - normal * mean)
    mix_state_grad = gated_grad * gate_act
    scanned_low = mix_state_grad.astype(BF)
    skip = head_ref[2:3]
    state_mix, inner_grads, level_grads, step_sums = [], [], [], []
    affinity_grad = jnp.zeros((rows, rows), F32)
    for h in range(heads):
        at = slice(h * HEAD, (h + 1) * HEAD)
        decay = decay_of(level, h, causal, rows)
        mixing_full = affinity * decay
        mixing = mixing_full.astype(BF)
        state_mix.append(mm(mixing, inner[:, at]) + skip[:, at] * filtered[:, at])
        mixing_grad = mm_rt(scanned_low[:, at], inner[:, at])
        inner_grad = mm_lt(mixing, scanned_low[:, at])
        flow = mixing_grad * mixing_full
        change = jnp.sum(flow - jnp.transpose(flow), axis=1, keepdims=True)
        level_grads.append(jnp.broadcast_to(change, (rows, HEAD)))
        affinity_grad = affinity_grad + mixing_grad * decay
        inner_grads.append(inner_grad)
        reach = jnp.sum(inner_grad * filtered[:, at], axis=1, keepdims=True)
        step_sums.append(jnp.broadcast_to(reach, (rows, HEAD)))
    state_mix = jnp.concatenate(state_mix, axis=1)
    inner_grad = jnp.concatenate(inner_grads, axis=1)
    mix_low_ref[:, :chans] = (
        gated_grad * state_mix * (gsig * (1.0 + gate * (1.0 - gsig)))
    ).astype(BF)
    down = lax.broadcasted_iota(jnp.int32, (rows, rows), 0)
    across = lax.broadcasted_iota(jnp.int32, (rows, rows), 1)
    upper = jnp.where(across >= down, 1.0, 0.0)
    rate_grad = mm_exact(upper, jnp.concatenate(level_grads, axis=1))
    step_grad = rate_grad * head_ref[0:1] + jnp.concatenate(step_sums, axis=1)
    step_pre_grad = step_grad * sigmoid(raw)
    filtered_grad = skip * mix_state_grad + inner_grad * step
    input_grad, tap_grads = filter_rows_back(
        filter_input, taps, masks, filtered_grad * (sig * (1.0 + pre * (1.0 - sig)))
    )
    mix_low_ref[:, chans : 2 * chans] = input_grad.astype(BF)
    extra = [
        jnp.sum(norm_grad * normal, axis=0, keepdims=True),
        jnp.sum(mix_state_grad * filtered, axis=0, keepdims=True),
        jnp.sum(rate_grad * rate, axis=0, keepdims=True),
        jnp.sum(step_pre_grad, axis=0, keepdims=True),
    ]
    small_ref[0] = jnp.zeros(small_ref.shape[1:], F32)
    for i, v in enumerate(tap_grads + extra):
        small_ref[0, i : i + 1] = v
    low = affinity_grad.astype(BF)
    read_grad = mm(low, sact[:, :NS])
    write_grad = mm_lt(low, sact[:, NS:])
    act_grad = jnp.concatenate([write_grad, read_grad], axis=1)
    state_grad, stap_grads = filter_rows_back(
        state_raw, staps, masks, act_grad * (ssig * (1.0 + spre * (1.0 - ssig)))
    )
    row_low_ref[:, : 2 * NS] = state_grad.astype(BF)
    staps_out_ref[0] = jnp.zeros(staps_out_ref.shape[1:], F32)
    for i, v in enumerate(stap_grads):
        staps_out_ref[0, i : i + 1] = v
    cosine, sine = cos_ref[...], sin_ref[...]
    query = rope(mix_ref[:, 2 * chans :], cosine, sine).astype(BF)
    keys = rope(row_ref[:, 2 * NS : 2 * NS + HEAD], cosine, sine).astype(BF)
    values = row_ref[:, 2 * NS + HEAD : 2 * NS + 2 * HEAD].astype(BF)
    root = HEAD ** -0.5
    scores = jnp.where(causal, mm_rt(query, keys) * root, -1e30)
    raised = jnp.exp(scores - jnp.max(scores, axis=1, keepdims=True))
    shares = raised / jnp.sum(raised, axis=1, keepdims=True)
    attend_grad = grad_ref[:, chans:].astype(BF)
    values_grad = mm_lt(shares.astype(BF), attend_grad)
    shares_grad = mm_rt(attend_grad, values)
    scores_low = (
        shares * (shares_grad - jnp.sum(shares_grad * shares, axis=1, keepdims=True))
    ).astype(BF)
    query_grad = mm(scores_low, keys) * root
    keys_grad = mm_lt(scores_low, query) * root
    mix_low_ref[:, 2 * chans :] = rope(query_grad, cosine, -sine).astype(BF)
    at = 2 * NS
    row_low_ref[:, at : at + HEAD] = rope(keys_grad, cosine, -sine).astype(BF)
    row_low_ref[:, at + HEAD : at + 2 * HEAD] = values_grad.astype(BF)
    row_low_ref[:, at + 2 * HEAD :] = mm(step_pre_grad.astype(BF), slot_ref[...]).astype(BF)


def over_groups(kernel, groups, rows, args, whole, outs):
    def spec(shape):
        if len(shape) == 3:
            return pl.BlockSpec((1,) + shape[1:], lambda g: (g, 0, 0))
        return pl.BlockSpec((rows, shape[1]), lambda g: (g, 0))

    def fixed(shape):
        return pl.BlockSpec(shape, lambda g: (0, 0))

    specs = [
        fixed(v.shape) if w else spec(v.shape) for v, w in zip(args, whole)
    ]
    return pl.pallas_call(
        kernel,
        grid=(groups,),
        in_specs=specs,
        out_specs=[spec(o.shape) for o in outs],
        out_shape=outs,
        compiler_params=grant(24),
    )(*args)


def place_pair(ti_ref, own_ref, t_ref, x_ref, xt_ref, out_ref):
    rows = own_ref.shape[0]
    at = ti_ref[0]
    for i, ref in ((at, own_ref), (1 - at, t_ref), (2 + at, x_ref), (3 - at, xt_ref)):
        out_ref[pl.ds(pl.multiple_of(i * rows, rows), rows)] = ref[...]


def place_rows(at_ref, own_ref, x_ref, c_ref, xc_ref, out_ref, small_ref):
    z, me = at_ref[0], at_ref[1]
    depth, rows = out_ref.shape[0], out_ref.shape[2]
    for k in range(depth):
        to = lax.rem(z + k, depth)
        for offset, src in ((0, own_ref), (2, x_ref), (1, c_ref), (3, xc_ref)):
            out_ref[to, me ^ offset] = src[k, :rows]
            small_ref[to, me ^ offset] = src[k, rows:]


def times(rows, w):
    return tuple(dot(r, w) for r in rows)


def grads(left, right):
    near, far = (contract("tc,tk->ck", a, b) for a, b in zip(left, right))
    return (near + far).astype(BF)


def split_kernel(ti_ref, total_ref, got_ref, mine_ref, t_ref, x_ref, xt_ref):
    rows = mine_ref.shape[0]
    at = ti_ref[0]

    def part(i):
        where = pl.ds(pl.multiple_of(i * rows, rows), rows)
        return total_ref[where] + got_ref[where].astype(F32)

    mine_ref[...] = part(at)
    t_ref[...] = part(1 - at).astype(BF)
    x_ref[...] = part(2 + at).astype(BF)
    xt_ref[...] = part(3 - at).astype(BF)


def split_rows(keep, send, ti):
    got = swap_c(send.astype(BF))
    count, width = keep.shape
    rows, tile = count // 4, 512
    part = pl.BlockSpec((rows, tile), lambda j: (0, j))
    full = pl.BlockSpec((count, tile), lambda j: (0, j))
    return pl.pallas_call(
        split_kernel,
        grid=(width // tile,),
        in_specs=[SMEM, full, full],
        out_specs=[part] * 4,
        out_shape=[jax.ShapeDtypeStruct((rows, width), F32)]
        + [jax.ShapeDtypeStruct((rows, width), BF)] * 3,
        compiler_params=grant(8),
    )(ti.reshape(1), keep, got)


def join_rows(mine, to_t, to_x, to_xt, earlier=()):
    got = (swap_t(to_t), swap_x(to_x), swap_xt(to_xt))
    if earlier:
        mine = after(mine, *earlier)
    return mine + got[0].astype(F32) + got[1].astype(F32) + got[2].astype(F32)


def split_back(terms, ti):
    keep, send = (sum(contract("tk,ck->tc", a[i], w) for a, w in terms) for i in (0, 1))
    return split_rows(keep, send, ti)


def times_back(terms, ti):
    return join_rows(*split_back(terms, ti))


def turned(block):
    return jnp.transpose(block.astype(F32)).astype(BF)


def prepare_kernel(plan, xi_ref, *refs):
    sources, keep_ref, send_ref = refs[:-2], refs[-2], refs[-1]
    first = xi_ref[0] == 0
    for c in range(2):
        at = 0
        for ref, is_turned in zip(sources, plan):
            if is_turned:
                n = ref.shape[0] // 4
                low, high = (turned(ref[(x * 2 + c) * n : (x * 2 + c + 1) * n]) for x in range(2))
            else:
                n = ref.shape[1] // 4
                low, high = (ref[:, (x * 2 + c) * n : (x * 2 + c + 1) * n] for x in range(2))
            keep_ref[c, :, at : at + n] = jnp.where(first, low, high)
            send_ref[c, :, at : at + n] = jnp.where(first, high, low)
            at += n


def middle_kernel(ci_ref, keep_ref, got_ref, keep_out, send_out):
    c = ci_ref[0]
    for i, ref in enumerate((keep_ref, got_ref)):
        keep_out[i] = ref[c]
        send_out[i] = ref[1 - c]


def end_kernel(at_ref, keep_ref, got_ref, out_ref):
    x, c = at_ref[0], at_ref[1]
    for i, ref in enumerate((keep_ref, got_ref)):
        out_ref[x, c ^ i] = ref[0]
        out_ref[1 - x, c ^ i] = ref[1]


def simple(kernel, args, outs, scalars=1, grant_of=8):
    single = not isinstance(outs, list)
    return pl.pallas_call(
        kernel,
        in_specs=[SMEM] * scalars + [VMEM] * (len(args) - scalars),
        out_specs=VMEM if single else [VMEM] * len(outs),
        out_shape=outs,
        compiler_params=grant(grant_of),
    )(*args)


def middle(keep, send, xi, ci):
    shape = jax.ShapeDtypeStruct(keep.shape, BF)
    keep, send = simple(middle_kernel, (ci.reshape(1), keep, swap_x(send)), [shape, shape])
    return keep, swap_c(send)


def prepare(sources, plan, xi):
    rows = [s.shape[1] if t else s.shape[0] for s, t in zip(sources, plan)][0]
    wide = sum((s.shape[0] if t else s.shape[1]) // 4 for s, t in zip(sources, plan))
    shape = jax.ShapeDtypeStruct((2, rows, wide), BF)
    return simple(
        functools.partial(prepare_kernel, plan), (xi.reshape(1), *sources), [shape, shape]
    )


def deal_out(keep, send, xi, ci):
    keep, got = middle(keep, send, xi, ci)
    out = jax.ShapeDtypeStruct((2,) + keep.shape, BF)
    return simple(end_kernel, (jnp.stack([xi, ci]), keep, got), out).reshape(
        -1, keep.shape[-1]
    )


def start_kernel(xi_ref, *refs):
    keep_ref, send_ref = refs[-2:]
    x, at = xi_ref[0], 0
    for ref in refs[:-2]:
        n = ref.shape[-1]
        keep_ref[:, :, at : at + n] = ref[x]
        send_ref[:, :, at : at + n] = ref[1 - x]
        at += n


def finish_kernel(plan, at_ref, keep_ref, got_ref, *outs):
    x, c = at_ref[0], at_ref[1]
    for q in range(4):
        own = c == q % 2
        offset = x ^ (q // 2)
        at = 0
        for ref, kind in zip(outs, plan):
            n = (ref.shape[0] if kind == "turned" else ref.shape[-1]) // 4
            for i in range(2 if kind == "two" else 1):
                block = jnp.where(
                    own, keep_ref[offset, :, at : at + n], got_ref[offset, :, at : at + n]
                ).astype(F32)
                if kind == "turned":
                    ref[q * n : (q + 1) * n] = jnp.transpose(block)
                elif kind == "two":
                    ref[:, i, q * n : (q + 1) * n] = block
                else:
                    ref[:, q * n : (q + 1) * n] = block
                at += n


def deal_start(summed, xi):
    shard = summed[0].shape[0] // 4
    blocks = [v.reshape(2, 2, shard, -1) for v in summed]
    shape = jax.ShapeDtypeStruct((2, shard, sum(v.shape[-1] for v in blocks)), BF)
    return simple(start_kernel, (xi.reshape(1), *blocks), [shape, shape])


def deal_middle(keep, send, ci):
    shape = jax.ShapeDtypeStruct(keep.shape, BF)
    return simple(middle_kernel, (ci.reshape(1), keep, swap_x(send)), [shape, shape])


def deal_finish(keep, send, plan, widths, xi, ci):
    shard = keep.shape[1]
    shapes = {"turned": lambda n: (4 * n, shard), "two": lambda n: (shard, 2, 4 * n)}
    outs = [
        jax.ShapeDtypeStruct(shapes.get(k, lambda n: (shard, 4 * n))(n), F32)
        for n, k in zip(widths, plan)
    ]
    return simple(
        functools.partial(finish_kernel, plan),
        (jnp.stack([xi, ci]), keep, swap_c(send)),
        outs,
    )


def row_first_kernel(ci_ref, part_ref, keep_ref, send_ref):
    c = ci_ref[0]
    for k in range(part_ref.shape[0]):
        for x in range(2):
            keep_ref[x, k] = part_ref[k, x, c]
            send_ref[x, k] = part_ref[k, x, 1 - c]


def row_second_kernel(xi_ref, keep_ref, got_ref, keep_out, send_out):
    x = xi_ref[0]
    keep_out[...] = keep_ref[x].astype(F32) + got_ref[x].astype(F32)
    send_out[...] = (keep_ref[1 - x].astype(F32) + got_ref[1 - x].astype(F32)).astype(BF)


def on_device(
    depth,
    tokens,
    segments,
    cotangent,
    first_gain,
    mixer_in,
    state_weight,
    step_weight,
    filter_taps,
    state_taps,
    decay_log,
    step_bias,
    skip_gain,
    gate_gain,
    mixer_out,
    query_weight,
    key_value_matrix,
    attend_out,
    second_gain,
    gate_up,
    down_weight,
):
    zi, xi = lax.axis_index("z"), lax.axis_index("x")
    ci, ti = lax.axis_index("c"), lax.axis_index("t")
    me = xi * 2 + ci
    rows, width = tokens.shape
    group = segments.shape[0]
    shard = mixer_in.shape[0]
    block = 4 * shard
    heads_in = decay_log.shape[0]
    heads = heads_in // 4
    chans = heads * HEAD
    total_chans = 2 * heads_in * HEAD
    ffn = gate_up.shape[2] // 4
    count = 4 * group
    scale = HEAD ** (-0.5)

    pieces = [first_gain, second_gain, filter_taps, state_taps, gate_gain, segments]
    sizes = [p.size for p in pieces]
    step_pad = jnp.pad(step_weight, ((0, 0), (0, 128 - heads_in)))
    row_pack = jnp.concatenate(
        [state_weight, key_value_matrix.reshape(shard, -1), step_pad], axis=1
    )
    row_wide = row_pack.shape[1]
    vec = jnp.concatenate([p.astype(BF).reshape(-1) for p in pieces])
    vec = jnp.pad(vec, (0, 16 * row_wide - vec.size)).reshape(16, row_wide)
    row_own = jnp.concatenate([row_pack, vec])
    row_got = z_gather_first(row_own, depth)

    first_plan = (True, True, False, False, False)
    first_keep, first_send = prepare(
        (mixer_out, attend_out, mixer_in[:, 0], mixer_in[:, 1], query_weight), first_plan, xi
    )
    first_keep = after(first_keep, *row_got)
    first_mine = deal_out(first_keep, first_send, xi, ci)
    wide = chans + HEAD

    row_z = z_gather_rel(row_own, row_got, zi, depth)
    first_w = z_gather(first_mine)
    row_x = swap_x(row_z)
    row_full, small = simple(
        place_rows,
        (jnp.stack([zi, me]), row_z, row_x, swap_c(row_z), swap_c(row_x)),
        [
            jax.ShapeDtypeStruct((depth, 4, shard, row_wide), BF),
            jax.ShapeDtypeStruct((depth, 4, 16, row_wide), BF),
        ],
        grant_of=16,
    )
    row_full = row_full.reshape(width, row_wide)
    kv_at = 2 * NS
    state_full = row_full[:, :kv_at]
    small = small.reshape(depth, 4, -1)
    offsets = [sum(sizes[:i]) for i in range(6)]
    cut = [small[:, :, at : at + size] for at, size in zip(offsets, sizes)]
    seg_all = lax.dynamic_index_in_dim(cut[5], zi, 0, keepdims=False).astype(F32)
    segs = jnp.stack(
        [lax.dynamic_index_in_dim(seg_all, me ^ k, 0, keepdims=False) for k in (0, 2, 1, 3)]
    )
    first_full = cut[0].reshape(-1).astype(F32)
    second_full = cut[1].reshape(-1).astype(F32)
    eighth = filter_taps.shape[2]
    taps_all = jnp.transpose(
        cut[2].reshape(depth, 4, CONV + 1, heads_in, eighth), (2, 3, 0, 1, 4)
    ).reshape(CONV + 1, 4, chans)
    taps = lax.dynamic_index_in_dim(taps_all, me, 1, keepdims=False).astype(F32)
    staps = (
        jnp.transpose(cut[3].reshape(depth, 4, CONV + 1, -1), (2, 0, 1, 3))
        .reshape(CONV + 1, 2 * NS)
        .astype(F32)
    )
    gate_all = jnp.transpose(
        cut[4].reshape(depth, 4, heads_in, eighth), (2, 0, 1, 3)
    ).reshape(4, chans)
    gate_gain_mine = lax.dynamic_index_in_dim(gate_all, me, 0, keepdims=False).astype(F32)

    order = jnp.arange(group)
    live_all = (segs >= 0).astype(F32)
    same = (segs[:, :, None] == segs[:, None, :]) & (order[None, None, :] <= order[None, :, None])
    position = jnp.sum(same.astype(F32), axis=2) - 1.0
    half = HEAD // 2
    frequency = ROPE_BASE ** (-2.0 * jnp.arange(half).astype(F32) / HEAD)
    angle = position.reshape(count, 1) * frequency[None, :]
    cosine, sine = jnp.cos(angle), jnp.sin(angle)
    cosine = jnp.concatenate([cosine, cosine], axis=1)
    sine = jnp.concatenate([-sine, sine], axis=1)
    live_mine = lax.dynamic_slice_in_dim(
        (segments >= 0).astype(F32), ti * rows, rows
    )[:, None]
    seg_cols = jnp.broadcast_to(segs.reshape(count, 1), (count, HEAD))
    seg_rows = jnp.broadcast_to(segs[:, None, :], (4, 8, group))

    def halves(v):
        n = v.shape[0] // 2
        return v[:n], v[n:]

    my_log = lax.dynamic_slice_in_dim(decay_log, me * heads, heads)
    my_bias = lax.dynamic_slice_in_dim(step_bias, me * heads, heads)
    my_skip = lax.dynamic_slice_in_dim(skip_gain, me * heads, heads)
    head_rows = jnp.pad(
        jnp.repeat(jnp.stack([-jnp.exp(my_log), my_bias, my_skip]), HEAD, axis=1), ((0, 5), (0, 0))
    )
    lane_head = me * heads + jnp.arange(chans) // HEAD
    picker = (jnp.arange(128)[:, None] == lane_head[None, :]).astype(F32)
    first_lane = (jnp.arange(chans) % HEAD == 0)[:, None]
    slots = ((jnp.arange(128)[None, :] == lane_head[:, None]) & first_lane).astype(BF)
    taps_pad = jnp.pad(taps, ((0, 3), (0, 0)))
    staps_pad = jnp.pad(staps, ((0, 3), (0, 0)))
    gain_pad = jnp.pad(gate_gain_mine[None], ((0, 7), (0, 0)))

    resid = tokens.astype(F32)
    normed_input, scale_one = norm_rows(resid, first_full)
    normed_low = normed_input.astype(BF)
    normed = act_gather(normed_low, ti)
    then_plan = (False, False, True)
    then_keep, then_send = prepare(
        (gate_up[:, 0], gate_up[:, 1], down_weight), then_plan, xi
    )
    then_send = after(then_send, normed[0], row_x)
    then_mine = deal_out(then_keep, then_send, xi, ci)
    then_w = z_gather(then_mine)
    grad_out = cotangent.astype(F32)
    feed_low = after((live_mine * grad_out).astype(BF), then_mine)
    row_out = times(normed, row_full)
    first_w = after(first_w, row_out)
    out_w, mix_w = first_w[:, :wide], first_w[:, wide:]
    mix_out = times(normed, mix_w)
    feed_grad = act_gather(feed_low, ti, *mix_out)

    per_half = list(
        zip(mix_out, row_out, halves(seg_cols), halves(seg_rows), halves(cosine), halves(sine))
    )
    near_far, whole = [], (False,) * 4 + (True,) * 4 + (False,) * 2
    for m, r, sc, sr, co, si in per_half:
        near_far.append((m, r, sc, sr, taps_pad, staps_pad, picker, head_rows, co, si))
    ahead = [
        over_groups(
            functools.partial(mixer_forward, heads),
            2,
            group,
            common,
            whole,
            [
                jax.ShapeDtypeStruct((count // 2, chans), F32),
                jax.ShapeDtypeStruct((2, 8, group), F32),
                jax.ShapeDtypeStruct((count // 2, HEAD), BF),
            ],
        )
        for common in near_far
    ]
    squares = jnp.concatenate([ahead[0][1], ahead[1][1]])
    gate_scale = halves(lax.rsqrt(sum_group(squares) / total_chans + EPS))
    gate_normal = [
        a[0] * g[:, 0].reshape(count // 2, 1) for a, g in zip(ahead, gate_scale)
    ]

    out_w = after(out_w, feed_grad)
    branch = [
        jnp.concatenate([(n * gate_gain_mine).astype(BF), a[2]], axis=1)
        for n, a in zip(gate_normal, ahead)
    ]
    hidden = resid + live_mine * times_back([(branch, out_w)], ti)
    second, scale_two = norm_rows(hidden, second_full)

    second_all = act_gather(second.astype(BF), ti)
    gu_w, down_w = then_w[:, : 2 * ffn], then_w[:, 2 * ffn :]
    gate_up_out = times(second_all, gu_w)
    activation = [(jax.nn.silu(v[:, :ffn]) * v[:, ffn:]).astype(BF) for v in gate_up_out]
    down_term = grads(feed_grad, activation)
    down_w = after(down_w, down_term)
    gu_low = []
    for v, feed_half in zip(gate_up_out, feed_grad):
        gate_part, up_part = v[:, :ffn], v[:, ffn:]
        act_grad = dot(feed_half, down_w)
        gu_low.append(
            jnp.concatenate(
                [
                    act_grad * up_part * silu_slope(gate_part),
                    act_grad * jax.nn.silu(gate_part),
                ],
                axis=1,
            ).astype(BF)
        )
    down_sum = z_scatter(down_term)
    gu_sum = z_scatter(grads(second_all, gu_low))
    second_split = split_back([(gu_low, gu_w)], ti)
    second_grad = join_rows(*second_split)
    feed_split = split_back([(after(activation, second_split), down_w)], ti)
    hidden_part, second_gain_grad = norm_rows_back(hidden, second_full, scale_two, second_grad)
    hidden_grad = grad_out + hidden_part
    mix_low_rows = after((live_mine * hidden_grad).astype(BF), feed_split, down_sum)
    mix_grad = act_gather(mix_low_rows, ti)
    branch_grad = times(mix_grad, out_w)
    out_term = grads(mix_grad, branch)
    out_sum = z_scatter(out_term)

    inner_sum = jnp.concatenate(
        [
            jnp.sum(b[:, :chans] * gate_gain_mine * n, axis=-1).reshape(2, 1, group)
            for b, n in zip(branch_grad, gate_normal)
        ]
    )
    inner_sum = sum_group(jnp.broadcast_to(inner_sum, (4, 8, group)))
    inner_sum = after(inner_sum, out_term)
    feed_split = after(feed_split, inner_sum)
    output = (hidden + live_mine * join_rows(*feed_split)).astype(BF)
    inner_sum = halves(inner_sum)
    inner_sum = (inner_sum[0], after(inner_sum[1], gu_sum))
    back = [
        over_groups(
            functools.partial(mixer_backward, heads, total_chans),
            2,
            group,
            common + (slots, branch_grad[i], ahead[i][0], gate_scale[i], gain_pad, inner_sum[i]),
            whole + (True, False, False, False, True, False),
            [
                jax.ShapeDtypeStruct((count // 2, 2 * chans + HEAD), BF),
                jax.ShapeDtypeStruct((count // 2, row_wide), BF),
                jax.ShapeDtypeStruct((2, 16, chans), F32),
                jax.ShapeDtypeStruct((2, 8, 2 * NS), F32),
            ],
        )
        for i, common in enumerate(near_far)
    ]
    mix_low, row_low, small_rows, small_state = zip(*back)
    then_parts = deal_start(after((down_sum, gu_sum), output), xi)
    mix_term = grads(after(normed, then_parts), mix_low)
    then_parts = deal_middle(*then_parts, ci)
    mix_sum = z_scatter(mix_term)

    small_rows = jnp.concatenate(small_rows)
    small_state = jnp.concatenate(small_state)
    state_taps_grad = jnp.sum(small_state, axis=0)[: CONV + 1]
    summed_split = split_back(
        [(after(mix_low, mix_term, then_parts), mix_w), (row_low, row_full)], ti
    )
    row_part = grads(normed, after(row_low, summed_split)).reshape(depth, 2, 2, shard, row_wide)
    shape = jax.ShapeDtypeStruct((2, depth, shard, row_wide), BF)
    keep, send = simple(row_first_kernel, (ci.reshape(1), row_part), [shape, shape], grant_of=16)
    keep, send = simple(
        row_second_kernel,
        (xi.reshape(1), keep, swap_c(send)),
        [jax.ShapeDtypeStruct(shape.shape[1:], F32), jax.ShapeDtypeStruct(shape.shape[1:], BF)],
        grant_of=16,
    )
    row_x = swap_x(send)
    down_weight_grad, gate_up_grad = deal_finish(
        *then_parts, ("turned", "two"), (ffn, ffn), xi, ci
    )
    ready = (send, down_weight_grad, gate_up_grad)
    normed_grad = join_rows(*summed_split, earlier=ready)
    row_sum_xc = after(keep, normed_grad) + row_x.astype(F32)
    row_sum_xc = row_sum_xc.astype(BF)
    row_sum = z_scatter(row_sum_xc.reshape(depth * shard, row_wide))
    out_keep, out_send = deal_start((after(out_sum, normed_grad),), xi)
    out_parts = deal_middle(out_keep, after(out_send, row_sum_xc), ci)
    mixer_out_grad, attend_out_grad = deal_finish(
        *out_parts, ("turned",) * 2, (chans, HEAD), xi, ci
    )
    resid_part, first_gain_grad = norm_rows_back(resid, first_full, scale_one, normed_grad)
    tokens_grad = hidden_grad + resid_part

    mix_parts = deal_middle(*deal_start((mix_sum,), xi), ci)
    mixer_in_grad, query_weight_grad = deal_finish(
        *mix_parts, ("two", ""), (chans, HEAD), xi, ci
    )
    state_sum = row_sum[:, :kv_at]
    state_weight_grad = state_sum.astype(F32) + swap_t(state_sum).astype(F32)
    row_sum = row_sum.astype(F32)
    keys_values_grad = row_sum[:, kv_at : kv_at + 2 * HEAD].reshape(shard, 2, HEAD)
    step_weight_grad = row_sum[:, kv_at + 2 * HEAD : kv_at + 2 * HEAD + heads_in]

    dp_at = zi * 4 + me
    head_sum = (small_rows[0] + small_rows[1] + small_rows[2] + small_rows[3])[:9]
    slots_of = jnp.arange(8)[:, None, None] == ti * 4 + me
    head_part = jnp.where(slots_of, head_sum[None], 0.0)
    parts = [second_gain_grad, state_taps_grad.reshape(-1), first_gain_grad]
    packed = jnp.concatenate(
        [head_part.reshape(-1, 128), jnp.concatenate(parts).reshape(-1, 128)]
    )
    packed = sum_all(packed, depth, row_sum_xc)
    head_all = lax.dynamic_slice_in_dim(
        packed[: head_part.size // 128], ti * (head_part.size // 256), head_part.size // 256
    )
    packed = packed[head_part.size // 128 :].reshape(-1)
    second_mine = lax.dynamic_slice_in_dim(packed, dp_at * shard, shard)
    first_mine = lax.dynamic_slice_in_dim(
        packed[packed.size - width :], dp_at * shard, shard
    )
    state_shard = state_taps.shape[1]
    state_taps_mine = lax.dynamic_slice_in_dim(
        packed[width : packed.size - width].reshape(CONV + 1, 2 * NS),
        dp_at * state_shard,
        state_shard,
        1,
    )
    by_head = jnp.transpose(
        head_all.reshape(4, 9, heads, HEAD), (1, 0, 2, 3)
    ).reshape(9, heads_in, HEAD)
    taps_out = lax.dynamic_slice_in_dim(by_head[: CONV + 1], dp_at * eighth, eighth, 2)
    gate_out = lax.dynamic_slice_in_dim(by_head[5], dp_at * eighth, eighth, 1)
    return (
        output,
        tokens_grad,
        first_mine,
        mixer_in_grad,
        state_weight_grad,
        step_weight_grad,
        taps_out,
        state_taps_mine,
        by_head[7, :, 0],
        by_head[8, :, 0],
        jnp.sum(by_head[6], axis=1),
        gate_out,
        mixer_out_grad,
        query_weight_grad,
        keys_values_grad,
        attend_out_grad,
        second_mine,
        gate_up_grad,
        down_weight_grad,
    )


def solution(mesh):
    dp, tensor = mesh.shape["dp"], mesh.shape["tensor"]
    depth = dp // 4
    split = Mesh(mesh.devices.reshape(depth, 2, 2, tensor), ("z", "x", "c", "t"))
    D = ("z", "x", "c")
    T = "t"
    R = ("z", "x", "c", "t")
    weights = (
        P(D),
        P(D, None, T),
        P(D, None),
        P(D, T),
        P(None, T, D),
        P(None, D),
        P(T),
        P(T),
        P(T),
        P(T, D),
        P(T, D),
        P(D, T),
        P(D, None, T),
        P(T, D),
        P(D),
        P(D, None, T),
        P(T, D),
    )

    def run(*args):
        return on_device(depth, *args)

    return jax.shard_map(
        run,
        mesh=split,
        in_specs=(P(R, None), P(D), P(R, None)) + weights,
        out_specs=(P(R, None), P(R, None)) + weights,
        check_vma=False,
    )
```

```python
import functools

import jax
import jax.numpy as jnp
from jax import lax
from jax.experimental import pallas as pl
from jax.experimental.pallas import tpu as pltpu
from jax.sharding import Mesh, PartitionSpec as P

HEAD = 128
NS = 256
CONV = 4
EPS = 1e-05
ROPE_BASE = 100000000000.0
BF = jnp.bfloat16
F32 = jnp.float32
VMEM = pl.BlockSpec(memory_space=pltpu.VMEM)
SMEM = pl.BlockSpec(memory_space=pltpu.SMEM)


def grant(mebibytes):
    return pltpu.CompilerParams(vmem_limit_bytes=mebibytes << 20)


def dot(left, right):
    return jnp.dot(left, right, preferred_element_type=F32)


def contract(form, left, right):
    return jnp.einsum(form, left, right, preferred_element_type=F32)


def silu_slope(values):
    sigma = jax.nn.sigmoid(values)
    return sigma * (1.0 + values * (1.0 - sigma))


def after(v, *earlier):
    return lax.optimization_barrier((v, earlier))[0]


def norm_rows(values, gain):
    scale = lax.rsqrt(jnp.mean(values * values, axis=-1, keepdims=True) + EPS)
    return values * scale * gain, scale


def norm_rows_back(values, gain, scale, grad):
    normal = values * scale
    weighted = grad * gain
    back = scale * (weighted - normal * jnp.mean(weighted * normal, axis=-1, keepdims=True))
    return back, jnp.sum(grad * normal, axis=0)


def swap_c(v):
    return lax.ppermute(v, "c", [(0, 1), (1, 0)])


def swap_x(v):
    return lax.ppermute(v, "x", [(0, 1), (1, 0)])


def swap_t(v):
    return lax.ppermute(v, "t", [(0, 1), (1, 0)])


def swap_xt(v):
    return lax.ppermute(v, ("x", "t"), [(0, 3), (1, 2), (2, 1), (3, 0)])


def swap_xc(v):
    return lax.ppermute(v, ("x", "c"), [(0, 3), (1, 2), (2, 1), (3, 0)])


def pair(mine, other, index, axis):
    return jnp.where(
        index == 0, jnp.stack([mine, other], axis=axis), jnp.stack([other, mine], axis=axis)
    )


def spread_xc(v, xi, ci):
    v = pair(v, swap_x(v), xi, 0)
    return pair(v, swap_c(v), ci, 1)


def order_t(mine, other, ti, axis=0):
    return jnp.where(
        ti == 0,
        jnp.concatenate([mine, other], axis=axis),
        jnp.concatenate([other, mine], axis=axis),
    )


def act_gather(v, ti, *earlier):
    rows, n = v.shape
    got = (swap_t(v), swap_x(v), swap_xt(v))
    if earlier:
        v = after(v, *earlier)
    near = pl.pallas_call(
        place_pair,
        in_specs=[SMEM] + [VMEM] * 4,
        out_specs=VMEM,
        out_shape=jax.ShapeDtypeStruct((4 * rows, n), v.dtype),
        compiler_params=grant(8),
    )(ti.reshape(1), v, *got)
    return near, swap_c(near)


def z_gather(v):
    return lax.all_gather(v, "z", axis=0, tiled=True)


def z_scatter(v):
    return lax.psum_scatter(v, "z", scatter_dimension=0, tiled=True)


def z_gather_first(v, depth):
    if depth != 4:
        return (lax.all_gather(v, "z", axis=0, tiled=False),)
    return (
        lax.ppermute(v, "z", [(0, 2), (1, 3), (2, 0), (3, 1)]),
        lax.ppermute(v, "z", [(0, 1), (1, 2), (2, 3)]),
        lax.ppermute(v, "z", [(1, 0), (2, 1), (3, 2)]),
    )


def z_gather_rel(v, got, zi, depth):
    if depth != 4:
        return jnp.roll(got[0], -zi, axis=0)
    two, below, above = got
    last = lax.ppermute(two, "z", [(2, 3), (1, 0)])
    return jnp.stack([v, jnp.where(zi == 3, last, above), two, jnp.where(zi == 0, last, below)])


def sum_z(v, depth):
    if depth != 4:
        return lax.psum(v, "z")
    one = lax.ppermute(v, "z", [(0, 1), (1, 0), (2, 3), (3, 2)])
    two = lax.ppermute(v, "z", [(0, 2), (2, 0), (1, 3), (3, 1)])
    three = lax.ppermute(v, "z", [(0, 3), (3, 0), (1, 2), (2, 1)])
    return (v + one) + (two + three)


def sum_all(v, depth, *earlier):
    v = v + swap_c(v)
    got = (swap_t(v), swap_x(v), swap_xt(v))
    v = (after(v, *earlier) + got[0]) + (got[1] + got[2])
    return sum_z(v, depth)


def sum_group(v):
    v = v + jnp.roll(swap_c(v), 2, axis=0)
    far = swap_x(v) + swap_xt(v)
    return (v + swap_t(v)) + jnp.stack([far[1], far[0], far[3], far[2]])


HIGH = lax.Precision.HIGHEST


def mm(left, right):
    return lax.dot_general(left, right, (((1,), (0,)), ((), ())), preferred_element_type=F32)


def mm_rt(left, right):
    return lax.dot_general(left, right, (((1,), (1,)), ((), ())), preferred_element_type=F32)


def mm_lt(left, right):
    return lax.dot_general(left, right, (((0,), (0,)), ((), ())), preferred_element_type=F32)


def mm_exact(left, right):
    return lax.dot_general(
        left, right, (((1,), (0,)), ((), ())), precision=HIGH, preferred_element_type=F32
    )


def sigmoid(v):
    return 1.0 / (1.0 + jnp.exp(-v))


def tap_masks(seg_col, rows):
    at = lax.broadcasted_iota(jnp.int32, (rows, HEAD), 0)
    masks = [None]
    for offset in range(1, CONV):
        same = (pltpu.roll(seg_col, offset, 0) == seg_col) & (at >= offset)
        masks.append(jnp.where(same, 1.0, 0.0)[:, :1])
    return masks


def filter_rows(values, taps, masks):
    total = taps[CONV : CONV + 1] + taps[0:1] * values
    for offset in range(1, CONV):
        total = total + taps[offset : offset + 1] * (pltpu.roll(values, offset, 0) * masks[offset])
    return total


def filter_rows_back(values, taps, masks, grad):
    rows = values.shape[0]
    tap_grads = [jnp.sum(grad * values, axis=0, keepdims=True)]
    back = taps[0:1] * grad
    for offset in range(1, CONV):
        masked = grad * masks[offset]
        tap_grads.append(
            jnp.sum(masked * pltpu.roll(values, offset, 0), axis=0, keepdims=True)
        )
        back = back + taps[offset : offset + 1] * pltpu.roll(masked, rows - offset, 0)
    tap_grads.append(jnp.sum(grad, axis=0, keepdims=True))
    return back, tap_grads


def causal_of(seg_col, seg_row, rows):
    down = lax.broadcasted_iota(jnp.int32, (rows, rows), 0)
    across = lax.broadcasted_iota(jnp.int32, (rows, rows), 1)
    wide = jnp.broadcast_to(seg_col[:, :1], (rows, rows))
    return (wide == seg_row[0:1]) & (across <= down)


def wide_steps(step_cols, pick_ref, head_ref, rows):
    raw = mm_exact(step_cols, pick_ref[...]) + head_ref[1:2]
    step = jnp.maximum(raw, 0.0) + jnp.log1p(jnp.exp(-jnp.abs(raw)))
    rate = head_ref[0:1] * step
    down = lax.broadcasted_iota(jnp.int32, (rows, rows), 0)
    across = lax.broadcasted_iota(jnp.int32, (rows, rows), 1)
    lower = jnp.where(across <= down, 1.0, 0.0)
    return raw, step, rate, mm_exact(lower, rate)


def decay_of(level, h, causal, rows):
    part = level[:, h * HEAD : (h + 1) * HEAD]
    across = jnp.transpose(part)[0:1]
    diff = jnp.broadcast_to(part[:, :1], (rows, rows)) - across
    return jnp.where(causal, jnp.exp(jnp.where(causal, diff, 0.0)), 0.0)


def rope(v, cosine, sine):
    return v * cosine + pltpu.roll(v, HEAD // 2, 1) * sine


def mixer_forward(heads, mix_ref, row_ref, seg_ref, seg_row_ref, taps_ref, staps_ref, pick_ref,
                  head_ref, cos_ref, sin_ref, gated_ref, square_ref, attended_ref):
    rows = mix_ref.shape[0]
    chans = heads * HEAD
    seg_col, seg_row = seg_ref[...], seg_row_ref[0]
    causal = causal_of(seg_col, seg_row, rows)
    masks = tap_masks(seg_col, rows)
    gate = mix_ref[:, :chans]
    pre = filter_rows(mix_ref[:, chans : 2 * chans], taps_ref[...], masks)
    filtered = pre * sigmoid(pre)
    spre = filter_rows(row_ref[:, : 2 * NS], staps_ref[...], masks)
    sact = (spre * sigmoid(spre)).astype(BF)
    affinity = mm_rt(sact[:, NS:], sact[:, :NS])
    _, step, _, level = wide_steps(row_ref[:, 2 * NS + 2 * HEAD :], pick_ref, head_ref, rows)
    inner = (filtered * step).astype(BF)
    gate_act = gate * sigmoid(gate)
    squares = jnp.zeros((rows, 1), F32)
    for h in range(heads):
        at = slice(h * HEAD, (h + 1) * HEAD)
        mixing = (affinity * decay_of(level, h, causal, rows)).astype(BF)
        scanned = mm(mixing, inner[:, at])
        gated = (scanned + head_ref[2:3, at] * filtered[:, at]) * gate_act[:, at]
        gated_ref[:, at] = gated
        squares = squares + jnp.sum(gated * gated, axis=1, keepdims=True)
    square_ref[0] = jnp.transpose(jnp.broadcast_to(squares, (rows, HEAD)))[:8]
    cosine, sine = cos_ref[...], sin_ref[...]
    query = rope(mix_ref[:, 2 * chans :], cosine, sine).astype(BF)
    keys = rope(row_ref[:, 2 * NS : 2 * NS + HEAD], cosine, sine).astype(BF)
    values = row_ref[:, 2 * NS + HEAD : 2 * NS + 2 * HEAD].astype(BF)
    scores = jnp.where(causal, mm_rt(query, keys) * (HEAD ** -0.5), -1e30)
    raised = jnp.exp(scores - jnp.max(scores, axis=1, keepdims=True))
    shares = (raised / jnp.sum(raised, axis=1, keepdims=True)).astype(BF)
    attended_ref[...] = mm(shares, values).astype(BF)


def mixer_backward(heads, total_chans, mix_ref, row_ref, seg_ref, seg_row_ref, taps_ref, staps_ref,
                   pick_ref, head_ref, cos_ref, sin_ref, slot_ref, grad_ref, gated_ref, scale_ref,
                   gain_ref, sum_ref, mix_low_ref, row_low_ref, small_ref, staps_out_ref):
    rows = mix_ref.shape[0]
    chans = heads * HEAD
    seg_col, seg_row = seg_ref[...], seg_row_ref[0]
    causal = causal_of(seg_col, seg_row, rows)
    masks = tap_masks(seg_col, rows)
    gate = mix_ref[:, :chans]
    filter_input = mix_ref[:, chans : 2 * chans]
    taps, staps = taps_ref[...], staps_ref[...]
    pre = filter_rows(filter_input, taps, masks)
    sig = sigmoid(pre)
    filtered = pre * sig
    state_raw = row_ref[:, : 2 * NS]
    spre = filter_rows(state_raw, staps, masks)
    ssig = sigmoid(spre)
    sact = (spre * ssig).astype(BF)
    affinity = mm_rt(sact[:, NS:], sact[:, :NS])
    raw, step, rate, level = wide_steps(row_ref[:, 2 * NS + 2 * HEAD :], pick_ref, head_ref, rows)
    inner = (filtered * step).astype(BF)
    gsig = sigmoid(gate)
    gate_act = gate * gsig
    norm_grad = grad_ref[:, :chans]
    scale = jnp.transpose(scale_ref[0])[:, :1]
    normal = gated_ref[...] * scale
    mean = jnp.transpose(sum_ref[0])[:, :1] * (1.0 / total_chans)
    gated_grad = scale * (norm_grad * gain_ref[0:1] - normal * mean)
    mix_state_grad = gated_grad * gate_act
    scanned_low = mix_state_grad.astype(BF)
    skip = head_ref[2:3]
    state_mix, inner_grads, level_grads, step_sums = [], [], [], []
    affinity_grad = jnp.zeros((rows, rows), F32)
    for h in range(heads):
        at = slice(h * HEAD, (h + 1) * HEAD)
        decay = decay_of(level, h, causal, rows)
        mixing_full = affinity * decay
        mixing = mixing_full.astype(BF)
        state_mix.append(mm(mixing, inner[:, at]) + skip[:, at] * filtered[:, at])
        mixing_grad = mm_rt(scanned_low[:, at], inner[:, at])
        inner_grad = mm_lt(mixing, scanned_low[:, at])
        flow = mixing_grad * mixing_full
        change = jnp.sum(flow - jnp.transpose(flow), axis=1, keepdims=True)
        level_grads.append(jnp.broadcast_to(change, (rows, HEAD)))
        affinity_grad = affinity_grad + mixing_grad * decay
        inner_grads.append(inner_grad)
        reach = jnp.sum(inner_grad * filtered[:, at], axis=1, keepdims=True)
        step_sums.append(jnp.broadcast_to(reach, (rows, HEAD)))
    state_mix = jnp.concatenate(state_mix, axis=1)
    inner_grad = jnp.concatenate(inner_grads, axis=1)
    mix_low_ref[:, :chans] = (
        gated_grad * state_mix * (gsig * (1.0 + gate * (1.0 - gsig)))
    ).astype(BF)
    down = lax.broadcasted_iota(jnp.int32, (rows, rows), 0)
    across = lax.broadcasted_iota(jnp.int32, (rows, rows), 1)
    upper = jnp.where(across >= down, 1.0, 0.0)
    rate_grad = mm_exact(upper, jnp.concatenate(level_grads, axis=1))
    step_grad = rate_grad * head_ref[0:1] + jnp.concatenate(step_sums, axis=1)
    step_pre_grad = step_grad * sigmoid(raw)
    filtered_grad = skip * mix_state_grad + inner_grad * step
    input_grad, tap_grads = filter_rows_back(
        filter_input, taps, masks, filtered_grad * (sig * (1.0 + pre * (1.0 - sig)))
    )
    mix_low_ref[:, chans : 2 * chans] = input_grad.astype(BF)
    extra = [
        jnp.sum(norm_grad * normal, axis=0, keepdims=True),
        jnp.sum(mix_state_grad * filtered, axis=0, keepdims=True),
        jnp.sum(rate_grad * rate, axis=0, keepdims=True),
        jnp.sum(step_pre_grad, axis=0, keepdims=True),
    ]
    small_ref[0] = jnp.zeros(small_ref.shape[1:], F32)
    for i, v in enumerate(tap_grads + extra):
        small_ref[0, i : i + 1] = v
    low = affinity_grad.astype(BF)
    read_grad = mm(low, sact[:, :NS])
    write_grad = mm_lt(low, sact[:, NS:])
    act_grad = jnp.concatenate([write_grad, read_grad], axis=1)
    state_grad, stap_grads = filter_rows_back(
        state_raw, staps, masks, act_grad * (ssig * (1.0 + spre * (1.0 - ssig)))
    )
    row_low_ref[:, : 2 * NS] = state_grad.astype(BF)
    staps_out_ref[0] = jnp.zeros(staps_out_ref.shape[1:], F32)
    for i, v in enumerate(stap_grads):
        staps_out_ref[0, i : i + 1] = v
    cosine, sine = cos_ref[...], sin_ref[...]
    query = rope(mix_ref[:, 2 * chans :], cosine, sine).astype(BF)
    keys = rope(row_ref[:, 2 * NS : 2 * NS + HEAD], cosine, sine).astype(BF)
    values = row_ref[:, 2 * NS + HEAD : 2 * NS + 2 * HEAD].astype(BF)
    root = HEAD ** -0.5
    scores = jnp.where(causal, mm_rt(query, keys) * root, -1e30)
    raised = jnp.exp(scores - jnp.max(scores, axis=1, keepdims=True))
    shares = raised / jnp.sum(raised, axis=1, keepdims=True)
    attend_grad = grad_ref[:, chans:].astype(BF)
    values_grad = mm_lt(shares.astype(BF), attend_grad)
    shares_grad = mm_rt(attend_grad, values)
    scores_low = (
        shares * (shares_grad - jnp.sum(shares_grad * shares, axis=1, keepdims=True))
    ).astype(BF)
    query_grad = mm(scores_low, keys) * root
    keys_grad = mm_lt(scores_low, query) * root
    mix_low_ref[:, 2 * chans :] = rope(query_grad, cosine, -sine).astype(BF)
    at = 2 * NS
    row_low_ref[:, at : at + HEAD] = rope(keys_grad, cosine, -sine).astype(BF)
    row_low_ref[:, at + HEAD : at + 2 * HEAD] = values_grad.astype(BF)
    row_low_ref[:, at + 2 * HEAD :] = mm(step_pre_grad.astype(BF), slot_ref[...]).astype(BF)


def over_groups(kernel, groups, rows, args, whole, outs):
    def spec(shape):
        if len(shape) == 3:
            return pl.BlockSpec((1,) + shape[1:], lambda g: (g, 0, 0))
        return pl.BlockSpec((rows, shape[1]), lambda g: (g, 0))

    def fixed(shape):
        return pl.BlockSpec(shape, lambda g: (0, 0))

    specs = [
        fixed(v.shape) if w else spec(v.shape) for v, w in zip(args, whole)
    ]
    return pl.pallas_call(
        kernel,
        grid=(groups,),
        in_specs=specs,
        out_specs=[spec(o.shape) for o in outs],
        out_shape=outs,
        compiler_params=grant(24),
    )(*args)


def place_pair(ti_ref, own_ref, t_ref, x_ref, xt_ref, out_ref):
    rows = own_ref.shape[0]
    at = ti_ref[0]
    for i, ref in ((at, own_ref), (1 - at, t_ref), (2 + at, x_ref), (3 - at, xt_ref)):
        out_ref[pl.ds(pl.multiple_of(i * rows, rows), rows)] = ref[...]


def place_rows(at_ref, own_ref, x_ref, c_ref, xc_ref, out_ref, small_ref):
    z, me = at_ref[0], at_ref[1]
    depth, rows = out_ref.shape[0], out_ref.shape[2]
    for k in range(depth):
        to = lax.rem(z + k, depth)
        for offset, src in ((0, own_ref), (2, x_ref), (1, c_ref), (3, xc_ref)):
            out_ref[to, me ^ offset] = src[k, :rows]
            small_ref[to, me ^ offset] = src[k, rows:]


def times(rows, w):
    return tuple(dot(r, w) for r in rows)


def grads(left, right):
    near, far = (contract("tc,tk->ck", a, b) for a, b in zip(left, right))
    return (near + far).astype(BF)


def split_kernel(ti_ref, total_ref, got_ref, mine_ref, t_ref, x_ref, xt_ref):
    rows = mine_ref.shape[0]
    at = ti_ref[0]

    def part(i):
        where = pl.ds(pl.multiple_of(i * rows, rows), rows)
        return total_ref[where] + got_ref[where].astype(F32)

    mine_ref[...] = part(at)
    t_ref[...] = part(1 - at).astype(BF)
    x_ref[...] = part(2 + at).astype(BF)
    xt_ref[...] = part(3 - at).astype(BF)


def split_rows(keep, send, ti):
    got = swap_c(send.astype(BF))
    count, width = keep.shape
    rows, tile = count // 4, 512
    part = pl.BlockSpec((rows, tile), lambda j: (0, j))
    full = pl.BlockSpec((count, tile), lambda j: (0, j))
    return pl.pallas_call(
        split_kernel,
        grid=(width // tile,),
        in_specs=[SMEM, full, full],
        out_specs=[part] * 4,
        out_shape=[jax.ShapeDtypeStruct((rows, width), F32)]
        + [jax.ShapeDtypeStruct((rows, width), BF)] * 3,
        compiler_params=grant(8),
    )(ti.reshape(1), keep, got)


def join_rows(mine, to_t, to_x, to_xt, earlier=()):
    got = (swap_t(to_t), swap_x(to_x), swap_xt(to_xt))
    if earlier:
        mine = after(mine, *earlier)
    return mine + got[0].astype(F32) + got[1].astype(F32) + got[2].astype(F32)


def split_back(terms, ti):
    keep, send = (sum(contract("tk,ck->tc", a[i], w) for a, w in terms) for i in (0, 1))
    return split_rows(keep, send, ti)


def times_back(terms, ti):
    return join_rows(*split_back(terms, ti))


def turned(block):
    return jnp.transpose(block.astype(F32)).astype(BF)


def prepare_kernel(plan, xi_ref, *refs):
    sources, keep_ref, send_ref = refs[:-2], refs[-2], refs[-1]
    first = xi_ref[0] == 0
    for c in range(2):
        at = 0
        for ref, is_turned in zip(sources, plan):
            if is_turned:
                n = ref.shape[0] // 4
                low, high = (turned(ref[(x * 2 + c) * n : (x * 2 + c + 1) * n]) for x in range(2))
            else:
                n = ref.shape[1] // 4
                low, high = (ref[:, (x * 2 + c) * n : (x * 2 + c + 1) * n] for x in range(2))
            keep_ref[c, :, at : at + n] = jnp.where(first, low, high)
            send_ref[c, :, at : at + n] = jnp.where(first, high, low)
            at += n


def middle_kernel(ci_ref, keep_ref, got_ref, keep_out, send_out):
    c = ci_ref[0]
    for i, ref in enumerate((keep_ref, got_ref)):
        keep_out[i] = ref[c]
        send_out[i] = ref[1 - c]


def end_kernel(at_ref, keep_ref, got_ref, out_ref):
    x, c = at_ref[0], at_ref[1]
    for i, ref in enumerate((keep_ref, got_ref)):
        out_ref[x, c ^ i] = ref[0]
        out_ref[1 - x, c ^ i] = ref[1]


def simple(kernel, args, outs, scalars=1, grant_of=8):
    single = not isinstance(outs, list)
    return pl.pallas_call(
        kernel,
        in_specs=[SMEM] * scalars + [VMEM] * (len(args) - scalars),
        out_specs=VMEM if single else [VMEM] * len(outs),
        out_shape=outs,
        compiler_params=grant(grant_of),
    )(*args)


def middle(keep, send, xi, ci):
    shape = jax.ShapeDtypeStruct(keep.shape, BF)
    keep, send = simple(middle_kernel, (ci.reshape(1), keep, swap_x(send)), [shape, shape])
    return keep, swap_c(send)


def prepare(sources, plan, xi):
    rows = [s.shape[1] if t else s.shape[0] for s, t in zip(sources, plan)][0]
    wide = sum((s.shape[0] if t else s.shape[1]) // 4 for s, t in zip(sources, plan))
    shape = jax.ShapeDtypeStruct((2, rows, wide), BF)
    return simple(
        functools.partial(prepare_kernel, plan), (xi.reshape(1), *sources), [shape, shape]
    )


def deal_out(keep, send, xi, ci):
    keep, got = middle(keep, send, xi, ci)
    out = jax.ShapeDtypeStruct((2,) + keep.shape, BF)
    return simple(end_kernel, (jnp.stack([xi, ci]), keep, got), out).reshape(
        -1, keep.shape[-1]
    )


def start_kernel(xi_ref, *refs):
    keep_ref, send_ref = refs[-2:]
    x, at = xi_ref[0], 0
    for ref in refs[:-2]:
        n = ref.shape[-1]
        keep_ref[:, :, at : at + n] = ref[x]
        send_ref[:, :, at : at + n] = ref[1 - x]
        at += n


def finish_kernel(plan, at_ref, keep_ref, got_ref, *outs):
    x, c = at_ref[0], at_ref[1]
    for q in range(4):
        own = c == q % 2
        offset = x ^ (q // 2)
        at = 0
        for ref, kind in zip(outs, plan):
            n = (ref.shape[0] if kind == "turned" else ref.shape[-1]) // 4
            for i in range(2 if kind == "two" else 1):
                block = jnp.where(
                    own, keep_ref[offset, :, at : at + n], got_ref[offset, :, at : at + n]
                ).astype(F32)
                if kind == "turned":
                    ref[q * n : (q + 1) * n] = jnp.transpose(block)
                elif kind == "two":
                    ref[:, i, q * n : (q + 1) * n] = block
                else:
                    ref[:, q * n : (q + 1) * n] = block
                at += n


def deal_start(summed, xi):
    shard = summed[0].shape[0] // 4
    blocks = [v.reshape(2, 2, shard, -1) for v in summed]
    shape = jax.ShapeDtypeStruct((2, shard, sum(v.shape[-1] for v in blocks)), BF)
    return simple(start_kernel, (xi.reshape(1), *blocks), [shape, shape])


def deal_middle(keep, send, ci):
    shape = jax.ShapeDtypeStruct(keep.shape, BF)
    return simple(middle_kernel, (ci.reshape(1), keep, swap_x(send)), [shape, shape])


def deal_finish(keep, send, plan, widths, xi, ci):
    shard = keep.shape[1]
    shapes = {"turned": lambda n: (4 * n, shard), "two": lambda n: (shard, 2, 4 * n)}
    outs = [
        jax.ShapeDtypeStruct(shapes.get(k, lambda n: (shard, 4 * n))(n), F32)
        for n, k in zip(widths, plan)
    ]
    return simple(
        functools.partial(finish_kernel, plan),
        (jnp.stack([xi, ci]), keep, swap_c(send)),
        outs,
    )


def row_first_kernel(ci_ref, part_ref, keep_ref, send_ref):
    c = ci_ref[0]
    for k in range(part_ref.shape[0]):
        for x in range(2):
            keep_ref[x, k] = part_ref[k, x, c]
            send_ref[x, k] = part_ref[k, x, 1 - c]


def row_second_kernel(xi_ref, keep_ref, got_ref, keep_out, send_out):
    x = xi_ref[0]
    keep_out[...] = keep_ref[x].astype(F32) + got_ref[x].astype(F32)
    send_out[...] = (keep_ref[1 - x].astype(F32) + got_ref[1 - x].astype(F32)).astype(BF)


def on_device(
    depth,
    tokens,
    segments,
    cotangent,
    first_gain,
    mixer_in,
    state_weight,
    step_weight,
    filter_taps,
    state_taps,
    decay_log,
    step_bias,
    skip_gain,
    gate_gain,
    mixer_out,
    query_weight,
    key_value_matrix,
    attend_out,
    second_gain,
    gate_up,
    down_weight,
):
    zi, xi = lax.axis_index("z"), lax.axis_index("x")
    ci, ti = lax.axis_index("c"), lax.axis_index("t")
    me = xi * 2 + ci
    rows, width = tokens.shape
    group = segments.shape[0]
    shard = mixer_in.shape[0]
    block = 4 * shard
    heads_in = decay_log.shape[0]
    heads = heads_in // 4
    chans = heads * HEAD
    total_chans = 2 * heads_in * HEAD
    ffn = gate_up.shape[2] // 4
    count = 4 * group
    scale = HEAD ** (-0.5)

    pieces = [first_gain, second_gain, filter_taps, state_taps, gate_gain, segments]
    sizes = [p.size for p in pieces]
    step_pad = jnp.pad(step_weight, ((0, 0), (0, 128 - heads_in)))
    row_pack = jnp.concatenate(
        [state_weight, key_value_matrix.reshape(shard, -1), step_pad], axis=1
    )
    row_wide = row_pack.shape[1]
    vec = jnp.concatenate([p.astype(BF).reshape(-1) for p in pieces])
    vec = jnp.pad(vec, (0, 16 * row_wide - vec.size)).reshape(16, row_wide)
    row_own = jnp.concatenate([row_pack, vec])
    row_got = z_gather_first(row_own, depth)

    first_plan = (True, True, False, False, False)
    first_keep, first_send = prepare(
        (mixer_out, attend_out, mixer_in[:, 0], mixer_in[:, 1], query_weight), first_plan, xi
    )
    first_keep = after(first_keep, *row_got)
    first_mine = deal_out(first_keep, first_send, xi, ci)
    wide = chans + HEAD

    row_z = z_gather_rel(row_own, row_got, zi, depth)
    first_w = z_gather(first_mine)
    row_x = swap_x(row_z)
    row_full, small = simple(
        place_rows,
        (jnp.stack([zi, me]), row_z, row_x, swap_c(row_z), swap_c(row_x)),
        [
            jax.ShapeDtypeStruct((depth, 4, shard, row_wide), BF),
            jax.ShapeDtypeStruct((depth, 4, 16, row_wide), BF),
        ],
        grant_of=16,
    )
    row_full = row_full.reshape(width, row_wide)
    kv_at = 2 * NS
    state_full = row_full[:, :kv_at]
    small = small.reshape(depth, 4, -1)
    offsets = [sum(sizes[:i]) for i in range(6)]
    cut = [small[:, :, at : at + size] for at, size in zip(offsets, sizes)]
    seg_all = lax.dynamic_index_in_dim(cut[5], zi, 0, keepdims=False).astype(F32)
    segs = jnp.stack(
        [lax.dynamic_index_in_dim(seg_all, me ^ k, 0, keepdims=False) for k in (0, 2, 1, 3)]
    )
    first_full = cut[0].reshape(-1).astype(F32)
    second_full = cut[1].reshape(-1).astype(F32)
    eighth = filter_taps.shape[2]
    taps_all = jnp.transpose(
        cut[2].reshape(depth, 4, CONV + 1, heads_in, eighth), (2, 3, 0, 1, 4)
    ).reshape(CONV + 1, 4, chans)
    taps = lax.dynamic_index_in_dim(taps_all, me, 1, keepdims=False).astype(F32)
    staps = (
        jnp.transpose(cut[3].reshape(depth, 4, CONV + 1, -1), (2, 0, 1, 3))
        .reshape(CONV + 1, 2 * NS)
        .astype(F32)
    )
    gate_all = jnp.transpose(
        cut[4].reshape(depth, 4, heads_in, eighth), (2, 0, 1, 3)
    ).reshape(4, chans)
    gate_gain_mine = lax.dynamic_index_in_dim(gate_all, me, 0, keepdims=False).astype(F32)

    order = jnp.arange(group)
    live_all = (segs >= 0).astype(F32)
    same = (segs[:, :, None] == segs[:, None, :]) & (order[None, None, :] <= order[None, :, None])
    position = jnp.sum(same.astype(F32), axis=2) - 1.0
    half = HEAD // 2
    frequency = ROPE_BASE ** (-2.0 * jnp.arange(half).astype(F32) / HEAD)
    angle = position.reshape(count, 1) * frequency[None, :]
    cosine, sine = jnp.cos(angle), jnp.sin(angle)
    cosine = jnp.concatenate([cosine, cosine], axis=1)
    sine = jnp.concatenate([-sine, sine], axis=1)
    live_mine = lax.dynamic_slice_in_dim(
        (segments >= 0).astype(F32), ti * rows, rows
    )[:, None]
    seg_cols = jnp.broadcast_to(segs.reshape(count, 1), (count, HEAD))
    seg_rows = jnp.broadcast_to(segs[:, None, :], (4, 8, group))

    def halves(v):
        n = v.shape[0] // 2
        return v[:n], v[n:]

    my_log = lax.dynamic_slice_in_dim(decay_log, me * heads, heads)
    my_bias = lax.dynamic_slice_in_dim(step_bias, me * heads, heads)
    my_skip = lax.dynamic_slice_in_dim(skip_gain, me * heads, heads)
    head_rows = jnp.pad(
        jnp.repeat(jnp.stack([-jnp.exp(my_log), my_bias, my_skip]), HEAD, axis=1), ((0, 5), (0, 0))
    )
    lane_head = me * heads + jnp.arange(chans) // HEAD
    picker = (jnp.arange(128)[:, None] == lane_head[None, :]).astype(F32)
    first_lane = (jnp.arange(chans) % HEAD == 0)[:, None]
    slots = ((jnp.arange(128)[None, :] == lane_head[:, None]) & first_lane).astype(BF)
    taps_pad = jnp.pad(taps, ((0, 3), (0, 0)))
    staps_pad = jnp.pad(staps, ((0, 3), (0, 0)))
    gain_pad = jnp.pad(gate_gain_mine[None], ((0, 7), (0, 0)))

    resid = tokens.astype(F32)
    normed_input, scale_one = norm_rows(resid, first_full)
    normed_low = normed_input.astype(BF)
    normed = act_gather(normed_low, ti)
    then_plan = (False, False, True)
    then_keep, then_send = prepare(
        (gate_up[:, 0], gate_up[:, 1], down_weight), then_plan, xi
    )
    then_send = after(then_send, normed[0], row_x)
    then_mine = deal_out(then_keep, then_send, xi, ci)
    then_w = z_gather(then_mine)
    grad_out = cotangent.astype(F32)
    feed_low = after((live_mine * grad_out).astype(BF), then_mine)
    row_out = times(normed, row_full)
    first_w = after(first_w, row_out)
    out_w, mix_w = first_w[:, :wide], first_w[:, wide:]
    mix_out = times(normed, mix_w)
    feed_grad = act_gather(feed_low, ti, *mix_out)

    per_half = list(
        zip(mix_out, row_out, halves(seg_cols), halves(seg_rows), halves(cosine), halves(sine))
    )
    near_far, whole = [], (False,) * 4 + (True,) * 4 + (False,) * 2
    for m, r, sc, sr, co, si in per_half:
        near_far.append((m, r, sc, sr, taps_pad, staps_pad, picker, head_rows, co, si))
    ahead = [
        over_groups(
            functools.partial(mixer_forward, heads),
            2,
            group,
            common,
            whole,
            [
                jax.ShapeDtypeStruct((count // 2, chans), F32),
                jax.ShapeDtypeStruct((2, 8, group), F32),
                jax.ShapeDtypeStruct((count // 2, HEAD), BF),
            ],
        )
        for common in near_far
    ]
    squares = jnp.concatenate([ahead[0][1], ahead[1][1]])
    gate_scale = halves(lax.rsqrt(sum_group(squares) / total_chans + EPS))
    gate_normal = [
        a[0] * g[:, 0].reshape(count // 2, 1) for a, g in zip(ahead, gate_scale)
    ]

    out_w = after(out_w, feed_grad)
    branch = [
        jnp.concatenate([(n * gate_gain_mine).astype(BF), a[2]], axis=1)
        for n, a in zip(gate_normal, ahead)
    ]
    hidden = resid + live_mine * times_back([(branch, out_w)], ti)
    second, scale_two = norm_rows(hidden, second_full)

    second_all = act_gather(second.astype(BF), ti)
    gu_w, down_w = then_w[:, : 2 * ffn], then_w[:, 2 * ffn :]
    gate_up_out = times(second_all, gu_w)
    activation = [(jax.nn.silu(v[:, :ffn]) * v[:, ffn:]).astype(BF) for v in gate_up_out]
    down_term = grads(feed_grad, activation)
    down_w = after(down_w, down_term)
    gu_low = []
    for v, feed_half in zip(gate_up_out, feed_grad):
        gate_part, up_part = v[:, :ffn], v[:, ffn:]
        act_grad = dot(feed_half, down_w)
        gu_low.append(
            jnp.concatenate(
                [
                    act_grad * up_part * silu_slope(gate_part),
                    act_grad * jax.nn.silu(gate_part),
                ],
                axis=1,
            ).astype(BF)
        )
    down_sum = z_scatter(down_term)
    gu_sum = z_scatter(grads(second_all, gu_low))
    second_split = split_back([(gu_low, gu_w)], ti)
    second_grad = join_rows(*second_split)
    feed_split = split_back([(after(activation, second_split), down_w)], ti)
    hidden_part, second_gain_grad = norm_rows_back(hidden, second_full, scale_two, second_grad)
    hidden_grad = grad_out + hidden_part
    mix_low_rows = after((live_mine * hidden_grad).astype(BF), feed_split, down_sum)
    mix_grad = act_gather(mix_low_rows, ti)
    branch_grad = times(mix_grad, out_w)
    out_term = grads(mix_grad, branch)
    out_sum = z_scatter(out_term)

    inner_sum = jnp.concatenate(
        [
            jnp.sum(b[:, :chans] * gate_gain_mine * n, axis=-1).reshape(2, 1, group)
            for b, n in zip(branch_grad, gate_normal)
        ]
    )
    inner_sum = sum_group(jnp.broadcast_to(inner_sum, (4, 8, group)))
    inner_sum = after(inner_sum, out_term)
    feed_split = after(feed_split, inner_sum)
    output = (hidden + live_mine * join_rows(*feed_split)).astype(BF)
    inner_sum = halves(inner_sum)
    inner_sum = (inner_sum[0], after(inner_sum[1], gu_sum))
    back = [
        over_groups(
            functools.partial(mixer_backward, heads, total_chans),
            2,
            group,
            common + (slots, branch_grad[i], ahead[i][0], gate_scale[i], gain_pad, inner_sum[i]),
            whole + (True, False, False, False, True, False),
            [
                jax.ShapeDtypeStruct((count // 2, 2 * chans + HEAD), BF),
                jax.ShapeDtypeStruct((count // 2, row_wide), BF),
                jax.ShapeDtypeStruct((2, 16, chans), F32),
                jax.ShapeDtypeStruct((2, 8, 2 * NS), F32),
            ],
        )
        for i, common in enumerate(near_far)
    ]
    mix_low, row_low, small_rows, small_state = zip(*back)
    then_parts = deal_start(after((down_sum, gu_sum), output), xi)
    mix_term = grads(after(normed, then_parts), mix_low)
    then_parts = deal_middle(*then_parts, ci)
    mix_sum = z_scatter(mix_term)

    small_rows = jnp.concatenate(small_rows)
    small_state = jnp.concatenate(small_state)
    state_taps_grad = jnp.sum(small_state, axis=0)[: CONV + 1]
    summed_split = split_back(
        [(after(mix_low, mix_term, then_parts), mix_w), (row_low, row_full)], ti
    )
    row_part = grads(normed, after(row_low, summed_split)).reshape(depth, 2, 2, shard, row_wide)
    shape = jax.ShapeDtypeStruct((2, depth, shard, row_wide), BF)
    keep, send = simple(row_first_kernel, (ci.reshape(1), row_part), [shape, shape], grant_of=16)
    keep, send = simple(
        row_second_kernel,
        (xi.reshape(1), keep, swap_c(send)),
        [jax.ShapeDtypeStruct(shape.shape[1:], F32), jax.ShapeDtypeStruct(shape.shape[1:], BF)],
        grant_of=16,
    )
    row_x = swap_x(send)
    down_weight_grad, gate_up_grad = deal_finish(
        *then_parts, ("turned", "two"), (ffn, ffn), xi, ci
    )
    ready = (send, down_weight_grad, gate_up_grad)
    normed_grad = join_rows(*summed_split, earlier=ready)
    row_sum_xc = after(keep, normed_grad) + row_x.astype(F32)
    row_sum_xc = row_sum_xc.astype(BF)
    row_sum = z_scatter(row_sum_xc.reshape(depth * shard, row_wide))
    out_keep, out_send = deal_start((after(out_sum, normed_grad),), xi)
    out_parts = deal_middle(out_keep, after(out_send, row_sum_xc), ci)
    mixer_out_grad, attend_out_grad = deal_finish(
        *out_parts, ("turned",) * 2, (chans, HEAD), xi, ci
    )
    resid_part, first_gain_grad = norm_rows_back(resid, first_full, scale_one, normed_grad)
    tokens_grad = hidden_grad + resid_part

    mix_parts = deal_middle(*deal_start((mix_sum,), xi), ci)
    mixer_in_grad, query_weight_grad = deal_finish(
        *mix_parts, ("two", ""), (chans, HEAD), xi, ci
    )
    row_sum = after(row_sum, mixer_in_grad)
    state_sum = row_sum[:, :kv_at]
    state_weight_grad = state_sum.astype(F32) + swap_t(state_sum).astype(F32)
    row_sum = row_sum.astype(F32)
    keys_values_grad = row_sum[:, kv_at : kv_at + 2 * HEAD].reshape(shard, 2, HEAD)
    step_weight_grad = row_sum[:, kv_at + 2 * HEAD : kv_at + 2 * HEAD + heads_in]

    dp_at = zi * 4 + me
    head_sum = (small_rows[0] + small_rows[1] + small_rows[2] + small_rows[3])[:9]
    slots_of = jnp.arange(8)[:, None, None] == ti * 4 + me
    head_part = jnp.where(slots_of, head_sum[None], 0.0)
    parts = [second_gain_grad, state_taps_grad.reshape(-1), first_gain_grad]
    packed = jnp.concatenate(
        [head_part.reshape(-1, 128), jnp.concatenate(parts).reshape(-1, 128)]
    )
    packed = sum_all(packed, depth, row_sum_xc)
    head_all = lax.dynamic_slice_in_dim(
        packed[: head_part.size // 128], ti * (head_part.size // 256), head_part.size // 256
    )
    packed = packed[head_part.size // 128 :].reshape(-1)
    second_mine = lax.dynamic_slice_in_dim(packed, dp_at * shard, shard)
    first_mine = lax.dynamic_slice_in_dim(
        packed[packed.size - width :], dp_at * shard, shard
    )
    state_shard = state_taps.shape[1]
    state_taps_mine = lax.dynamic_slice_in_dim(
        packed[width : packed.size - width].reshape(CONV + 1, 2 * NS),
        dp_at * state_shard,
        state_shard,
        1,
    )
    by_head = jnp.transpose(
        head_all.reshape(4, 9, heads, HEAD), (1, 0, 2, 3)
    ).reshape(9, heads_in, HEAD)
    taps_out = lax.dynamic_slice_in_dim(by_head[: CONV + 1], dp_at * eighth, eighth, 2)
    gate_out = lax.dynamic_slice_in_dim(by_head[5], dp_at * eighth, eighth, 1)
    return (
        output,
        tokens_grad,
        first_mine,
        mixer_in_grad,
        state_weight_grad,
        step_weight_grad,
        taps_out,
        state_taps_mine,
        by_head[7, :, 0],
        by_head[8, :, 0],
        jnp.sum(by_head[6], axis=1),
        gate_out,
        mixer_out_grad,
        query_weight_grad,
        keys_values_grad,
        attend_out_grad,
        second_mine,
        gate_up_grad,
        down_weight_grad,
    )


def solution(mesh):
    dp, tensor = mesh.shape["dp"], mesh.shape["tensor"]
    depth = dp // 4
    split = Mesh(mesh.devices.reshape(depth, 2, 2, tensor), ("z", "x", "c", "t"))
    D = ("z", "x", "c")
    T = "t"
    R = ("z", "x", "c", "t")
    weights = (
        P(D),
        P(D, None, T),
        P(D, None),
        P(D, T),
        P(None, T, D),
        P(None, D),
        P(T),
        P(T),
        P(T),
        P(T, D),
        P(T, D),
        P(D, T),
        P(D, None, T),
        P(T, D),
        P(D),
        P(D, None, T),
        P(T, D),
    )

    def run(*args):
        return on_device(depth, *args)

    return jax.shard_map(
        run,
        mesh=split,
        in_specs=(P(R, None), P(D), P(R, None)) + weights,
        out_specs=(P(R, None), P(R, None)) + weights,
        check_vma=False,
    )
```
